32 devices in a mesh: ctx: 4 (over x, core), fsdp: 8 (over z, y).
Axes of the slice: x: 2, y: 2, z: 4, core: 2. Of those that a mesh axis runs over, the one named last changes fastest.
Arguments:
- block_input: bfloat16 [24, 4096, 512], P('fsdp', 'ctx'), may hold values from -6 to 6
- cotangent: bfloat16 [24, 4096, 512], P('fsdp', 'ctx'), may hold values from -6 to 6
- qkv_weight: bfloat16 [512, 1536], P('fsdp'), may hold values from -0.25 to 0.25
- out_weight: bfloat16 [512, 512], P('fsdp'), may hold values from -2 to 2
- up_weight: bfloat16 [512, 2048], P('fsdp'), may hold values from -0.25 to 0.25
- down_weight: bfloat16 [2048, 512], P('fsdp'), may hold values from -0.125 to 0.125
- norm_gains: bfloat16 [2, 512], P(None, 'fsdp'), may hold values from 0.099609375 to 1.8984375
- norm_shifts: bfloat16 [2, 512], P(None, 'fsdp'), may hold values from -0.59765625 to 0.59765625
Outputs:
- block_out: bfloat16 [24, 4096, 512], P('fsdp', 'ctx')
- grad_input: bfloat16 [24, 4096, 512], P('fsdp', 'ctx')
- grad_qkv: float32 [512, 1536], P('fsdp')
- grad_out: float32 [512, 512], P('fsdp')
- grad_up: float32 [512, 2048], P('fsdp')
- grad_down: float32 [2048, 512], P('fsdp')
- grad_gains: float32 [2, 512], P(None, 'fsdp')
- grad_shift_first: float32 [512], P('fsdp')
- grad_shift_second: float32 [512], P('fsdp')
The draws below stay inside these ranges and needn't reach their ends.
All inputs are finite; a program needn't handle non-finite values.
Results may differ from the reference program's by a relative error of at most 0.019.
Values may be sent and summed in bfloat16 or wider, within the bound.
A program may use at most 256 MiB of HBM per device.

```python
import jax
import jax.numpy as jnp
from jax import lax

D = 512
HEADS = 8
HDIM = 64
FF = 2048
SPAN = 128
CONT = 1024
SEQS = 24
LENGTH = 4096
PROMPT = 2048


def levels(stream_key, shape, pieces, smallest, largest):
    def one(dim, blocks):
        steps = jax.random.uniform(jax.random.fold_in(jax.random.fold_in(stream_key, 6), dim), (blocks,), jnp.float32, smallest / len(pieces), largest / len(pieces))
        return jnp.repeat(jnp.exp(steps), shape[dim] // blocks).reshape((-1,) + (1,) * (len(shape) - dim - 1))

    factor_of = one(*pieces[0])
    for cut in pieces[1:]:
        factor_of = factor_of * one(*cut)
    return factor_of


def noise(key, dims, width, limit, split=(), kind=jnp.bfloat16):
    level = levels(key, dims, split, -0.22, 0.18) if split else 1.0
    array = jax.random.normal(key, dims, jnp.float32) * width * level
    return jnp.minimum(jnp.maximum(array, -limit), limit).astype(kind)


def setup_inputs(seed: int = 0) -> dict:
    key_of = jax.random.split(jax.random.key(seed), 9)
    block_input = noise(key_of[0], (SEQS, LENGTH, D), 1.0, 6.0, ((0, 8), (1, 4)))
    cotangent = noise(key_of[1], (SEQS, LENGTH, D), 1.0, 6.0, ((0, 8), (1, 4)))
    qkv_weight = noise(key_of[2], (D, 3 * D), D ** -0.5, 0.25, ((0, 8),))
    out_weight = noise(key_of[3], (D, D), (D // 64) ** -0.5, 2.0, ((0, 8),))
    up_weight = noise(key_of[4], (D, FF), D ** -0.5, 0.25, ((0, 8),))
    down_weight = noise(key_of[5], (FF, D), FF ** -0.5, 0.125, ((0, 8),))
    norm_gains = jnp.clip(1.0 + 0.18 * jax.random.normal(key_of[6], (2, D), jnp.float32), 0.099609375, 1.8984375).astype(jnp.bfloat16)
    norm_shifts = noise(key_of[7], (2, D), 0.1, 0.59765625, ((1, 8),))
    return dict(block_input=block_input, cotangent=cotangent, qkv_weight=qkv_weight, out_weight=out_weight, up_weight=up_weight, down_weight=down_weight, norm_gains=norm_gains, norm_shifts=norm_shifts)


EPS = 1e-05
NEG = -1e+30
HIGHEST_PRECISION = lax.Precision.HIGHEST

@jax.custom_vjp
def low(v):
    return lax.optimization_barrier(v.astype(jnp.bfloat16)).astype(jnp.float32)

@jax.custom_vjp
def low_back(v):
    return v

def low_keep(v):
    return (low(v), None)

def low_pass(kept, grad):
    return (grad,)

def back_keep(v):
    return (v, None)

def back_low(kept, grad):
    return (low(grad),)
low.defvjp(low_keep, low_pass)
low_back.defvjp(back_keep, back_low)

def layer_norm(values, gain, shift):
    center = values - lax.optimization_barrier(jnp.mean(values, axis=-1, keepdims=True))
    spread = lax.optimization_barrier(jnp.mean(center * center, axis=-1, keepdims=True))
    return center * lax.rsqrt(spread + EPS) * gain + shift

def product(left, right):
    return jnp.dot(left, right, precision=HIGHEST_PRECISION)

def segment_of(span_ids, prompt_spans):
    later = (span_ids - prompt_spans) // (CONT // SPAN) + 1
    return jnp.where(span_ids < prompt_spans, 0, later)

def forward(inputs, qkv_weight, out_weight, up_weight, down_weight, norm_gains, norm_shifts):
    length = inputs.shape[0]
    spans = length // SPAN
    normed = layer_norm(inputs, norm_gains[0], norm_shifts[0])
    mixed = low_back(product(low(normed), qkv_weight))
    rounded = low(mixed)
    queries = rounded[:, :D].reshape(spans, SPAN, HEADS, HDIM)
    key_rows = rounded[:, D:2 * D].reshape(spans, SPAN, HEADS, HDIM)
    values = rounded[:, 2 * D:].reshape(spans, SPAN, HEADS, HDIM)
    summary = low(lax.optimization_barrier(jnp.sum(mixed[:, D:].reshape(spans, SPAN, 2 * D), axis=1)) * SPAN ** (-0.5))
    far_keys = summary[:, :D].reshape(spans, HEADS, HDIM)
    far_values = summary[:, D:].reshape(spans, HEADS, HDIM)
    near = jnp.einsum('aqhd,akhd->ahqk', queries, key_rows, precision=HIGHEST_PRECISION) * 0.125
    far = jnp.einsum('aqhd,shd->ahqs', queries, far_keys, precision=HIGHEST_PRECISION) * 0.125
    scores = low_back(jnp.concatenate([near, far], axis=-1))
    position = jnp.arange(SPAN).astype(jnp.int32)
    span_order = jnp.arange(spans).astype(jnp.int32)
    segment = segment_of(span_order, PROMPT // SPAN)
    causal = position[None, :] <= position[:, None]
    visible = (segment[None, :] == 0) | (segment[None, :] == segment[:, None])
    earlier = (span_order[None, :] < span_order[:, None]) & visible
    allowed = jnp.concatenate([jnp.broadcast_to(causal[None, None], (spans, 1, SPAN, SPAN)), jnp.broadcast_to(earlier[:, None, None, :], (spans, 1, SPAN, spans))], axis=-1)
    scores = jnp.where(allowed, scores, NEG)
    weights = low(jax.nn.softmax(scores, axis=-1))
    attended = jnp.einsum('ahqk,akhd->aqhd', weights[..., :SPAN], values, precision=HIGHEST_PRECISION)
    attended = attended + jnp.einsum('ahqs,shd->aqhd', weights[..., SPAN:], far_values, precision=HIGHEST_PRECISION)
    attended = low_back(attended.reshape(length, D))
    branch = low_back(product(low(attended), out_weight))
    middle = inputs + branch
    normed_two = layer_norm(middle, norm_gains[1], norm_shifts[1])
    hidden = low_back(product(low(normed_two), up_weight))
    return middle + product(low(jax.nn.gelu(hidden, approximate=False)), down_weight)

def reference(block_input, cotangent, qkv_weight, out_weight, up_weight, down_weight, norm_gains, norm_shifts):
    params = tuple((param.astype(jnp.float32) for param in (qkv_weight, out_weight, up_weight, down_weight, norm_gains, norm_shifts)))

    def one_sequence(totals, pair):
        inputs, grad_output = pair
        result, pull = jax.vjp(forward, inputs.astype(jnp.float32), *params)
        grads = pull(grad_output.astype(jnp.float32))
        totals = tuple((total + addend for total, addend in zip(totals, grads[1:])))
        return (totals, (result.astype(jnp.bfloat16), grads[0].astype(jnp.bfloat16)))
    start = tuple((jnp.zeros(param.shape, jnp.float32) for param in params))
    totals, (block_out, grad_input) = lax.scan(one_sequence, start, (block_input, cotangent))
    return (block_out, grad_input, totals[0], totals[1], totals[2], totals[3], totals[4], totals[5][0], totals[5][1])
```

```python
import functools

import jax
import jax.numpy as jnp
from jax import lax
from jax.experimental import pallas as pl
from jax.experimental.pallas import tpu as pltpu
from jax.sharding import PartitionSpec as P

D = 512
HEADS = 8
FF = 2048
SPAN = 128
CONT = 1024
PAIRS = HEADS // 2

EPS = 1e-05
NEG = -1e30
F32 = jnp.float32
BF16 = jnp.bfloat16
VMEM_LIMIT = 60 * 1024 * 1024


def nn(a, b):
    return lax.dot_general(a, b, (((1,), (0,)), ((), ())), preferred_element_type=F32)


def nt(a, b):
    return lax.dot_general(a, b, (((1,), (1,)), ((), ())), preferred_element_type=F32)


def unit_of(values):
    center = values - jnp.mean(values, axis=-1, keepdims=True)
    rstd = lax.rsqrt(jnp.mean(center * center, axis=-1, keepdims=True) + EPS)
    return center * rstd, rstd


def norm_back(grad, unit, rstd, gain):
    scaled = grad * gain
    return rstd * (
        scaled
        - jnp.mean(scaled, axis=-1, keepdims=True)
        - unit * jnp.mean(scaled * unit, axis=-1, keepdims=True)
    )


def fold8(values):
    rows = values.shape[0]
    return jnp.sum(values.reshape(rows // 8, 8, values.shape[1]), axis=0)


def gelu_pair(x):
    e = jnp.exp(x * x * -0.5)
    t = 1.0 / (1.0 + (0.3275911 * 0.7071067811865476) * jnp.abs(x))
    poly = 1.061405429 * 0.5
    poly = poly * t + (-1.453152027 * 0.5)
    poly = poly * t + (1.421413741 * 0.5)
    poly = poly * t + (-0.284496736 * 0.5)
    poly = poly * t + (0.254829592 * 0.5)
    half = poly * t * e
    cdf = jnp.where(x < 0.0, half, 1.0 - half)
    return x * cdf, cdf + x * (e * 0.3989422804014327)


def qkv_kernel(x_ref, w_ref, gain_ref, shift_ref, mixed_ref, summary_ref):
    gain = gain_ref[0:1, :]
    shift = shift_ref[0:1, :]
    tile = 256

    def step(i, carry):
        rows = pl.ds(pl.multiple_of(i * tile, tile), tile)
        unit, _ = unit_of(x_ref[0, rows, :].astype(F32))
        low = (unit * gain + shift).astype(BF16)
        mixed_ref[0, rows, 0:D] = (nn(low, w_ref[:, 0:D]).astype(BF16).astype(F32) * 0.125).astype(BF16)
        for c in range(2):
            cols = slice(D + c * D, 2 * D + c * D)
            part = nn(low, w_ref[:, cols])
            mixed_ref[0, rows, cols] = part.astype(BF16)
            for s in range(tile // SPAN):
                total = jnp.sum(part[s * SPAN : (s + 1) * SPAN, :], axis=0, keepdims=True)
                summary_ref[0, pl.ds(i * (tile // SPAN) + s, 1), c * D : (c + 1) * D] = total * SPAN ** (-0.5)
        return carry

    lax.fori_loop(0, x_ref.shape[1] // tile, step, 0)


def qkv_call(x, w, gains, shifts):
    batches, tokens, _ = x.shape
    spans = tokens // SPAN
    return pl.pallas_call(
        qkv_kernel,
        grid=(batches,),
        in_specs=[
            pl.BlockSpec((1, tokens, D), lambda b: (b, 0, 0)),
            pl.BlockSpec((D, 3 * D), lambda b: (0, 0), pipeline_mode=pl.Buffered(1)),
            pl.BlockSpec((2, D), lambda b: (0, 0), pipeline_mode=pl.Buffered(1)),
            pl.BlockSpec((2, D), lambda b: (0, 0), pipeline_mode=pl.Buffered(1)),
        ],
        out_specs=[
            pl.BlockSpec((1, tokens, 3 * D), lambda b: (b, 0, 0)),
            pl.BlockSpec((1, spans, 2 * D), lambda b: (b, 0, 0)),
        ],
        out_shape=[
            jax.ShapeDtypeStruct((batches, tokens, 3 * D), BF16),
            jax.ShapeDtypeStruct((batches, spans, 2 * D), F32),
        ],
        compiler_params=pltpu.CompilerParams(vmem_limit_bytes=VMEM_LIMIT),
        name="qkv",
    )(x, w, gains, shifts)


def main_kernel(
    x_ref, g_ref, mixed_ref, far_ref, wo_ref, wu_ref, wd_ref, gain_ref, shift_ref,
    out_ref, gmid_ref, dmixed_ref, dfar_ref, go_ref, gu_ref, gd_ref, ggain_ref, gshift_ref,
    att_ref, attt_ref, pn_ref, pf_ref, n2_ref, n2t_ref, gt_ref, act_ref, gh_ref, gb_ref, da_ref, fart_ref,
):
    tokens = x_ref.shape[1]
    spans = tokens // SPAN
    count = far_ref.shape[1]
    prompt = count // 2
    first = lax.axis_index("ctx") * spans

    @pl.when(pl.program_id(0) == 0)
    def _():
        go_ref[...] = jnp.zeros_like(go_ref)
        gu_ref[...] = jnp.zeros_like(gu_ref)
        gd_ref[...] = jnp.zeros_like(gd_ref)
        ggain_ref[...] = jnp.zeros_like(ggain_ref)
        gshift_ref[...] = jnp.zeros_like(gshift_ref)

    dfar_ref[...] = jnp.zeros_like(dfar_ref)
    fart_ref[...] = far_ref[0].astype(F32).T.astype(BF16)

    def halves(pair):
        low = lax.broadcasted_iota(jnp.int32, pair.shape, 1) < 64
        zero = jnp.zeros_like(pair)
        return jnp.concatenate([jnp.where(low, pair, zero), jnp.where(low, zero, pair)], axis=0)

    def corner(both):
        return jnp.concatenate([both[0:64, 0:SPAN], both[64:128, SPAN : 2 * SPAN]], axis=0)

    def attend(j, carry):
        rows = pl.ds(pl.multiple_of(j * SPAN, SPAN), SPAN)
        key_id = lax.broadcasted_iota(jnp.int32, (SPAN, 2 * SPAN), 0)
        query_id = lax.broadcasted_iota(jnp.int32, (SPAN, 2 * SPAN), 1) & (SPAN - 1)
        causal = key_id <= query_id
        far_id = lax.broadcasted_iota(jnp.int32, (count, 2 * SPAN), 0)
        mine = first + j
        segment = (mine - prompt) >> 3
        seen = (far_id < mine) & ((far_id < prompt) | (((far_id - prompt) >> 3) == segment))
        for p in range(PAIRS):
            lanes = slice(p * SPAN, (p + 1) * SPAN)
            qs = halves(mixed_ref[0, rows, lanes])
            k = mixed_ref[0, rows, D + p * SPAN : D + (p + 1) * SPAN]
            v = mixed_ref[0, rows, 2 * D + p * SPAN : 2 * D + (p + 1) * SPAN]
            near = jnp.where(causal, nt(k, qs), NEG)
            far = jnp.where(seen, nt(far_ref[0, :, lanes], qs), NEG)
            peak = jnp.maximum(jnp.max(near, axis=0, keepdims=True), jnp.max(far, axis=0, keepdims=True))
            near = jnp.exp(near - peak)
            far = jnp.exp(far - peak)
            inv = 1.0 / (jnp.sum(near, axis=0, keepdims=True) + jnp.sum(far, axis=0, keepdims=True))
            near = (near * inv).astype(BF16)
            far = (far * inv).astype(BF16)
            pn_ref[j, p] = near
            pf_ref[j, p] = far
            vt = v.astype(F32).T.astype(BF16)
            both = nn(vt, near) + nn(fart_ref[D + p * SPAN : D + (p + 1) * SPAN, :], far)
            att = corner(both)
            attt_ref[lanes, rows] = att.astype(BF16)
            att_ref[rows, lanes] = att.T.astype(BF16)
        return carry

    lax.fori_loop(0, spans, attend, 0)

    tile = 256
    gain = gain_ref[1:2, :]
    shift = shift_ref[1:2, :]

    def mlp(i, carry):
        rows = pl.ds(pl.multiple_of(i * tile, tile), tile)
        middle = x_ref[0, rows, :].astype(F32) + nn(att_ref[rows, :], wo_ref[...])
        unit, rstd = unit_of(middle)
        low = unit * gain + shift
        n2t_ref[:, rows] = low.T.astype(BF16)
        low = low.astype(BF16)
        g = g_ref[0, rows, :]
        gt_ref[:, rows] = g.astype(F32).T.astype(BF16)
        for c in range(4):
            cols = slice(c * 512, (c + 1) * 512)
            act, slope = gelu_pair(nn(low, wu_ref[:, cols]))
            act_ref[rows, cols] = act.astype(BF16)
            gh_ref[rows, cols] = (nt(g, wd_ref[cols, :]) * slope).astype(BF16)
        out_ref[0, rows, :] = (middle + nn(act_ref[rows, :], wd_ref[...])).astype(BF16)
        grad = nt(gh_ref[rows, :], wu_ref[...])
        ggain_ref[...] += fold8(grad * unit)
        gshift_ref[...] += fold8(grad)
        grad = g.astype(F32) + norm_back(grad, unit, rstd, gain)
        low = grad.astype(BF16)
        gmid_ref[0, rows, :] = low
        gb_ref[rows, :] = low
        da_ref[rows, :] = nt(low, wo_ref[...]).astype(BF16)
        return carry

    lax.fori_loop(0, tokens // tile, mlp, 0)

    go_ref[...] += nn(attt_ref[...], gb_ref[...])

    def wgrad(c, carry):
        cols = pl.ds(pl.multiple_of(c * 512, 512), 512)
        gu_ref[:, cols] += nn(n2t_ref[...], gh_ref[:, cols])
        gd_ref[:, cols] += nn(gt_ref[...], act_ref[:, cols])
        return carry

    lax.fori_loop(0, 4, wgrad, 0)

    def attend_back(j, carry):
        rows = pl.ds(pl.multiple_of(j * SPAN, SPAN), SPAN)
        for p in range(PAIRS):
            lanes = slice(p * SPAN, (p + 1) * SPAN)
            klanes = slice(D + p * SPAN, D + (p + 1) * SPAN)
            vlanes = slice(2 * D + p * SPAN, 2 * D + (p + 1) * SPAN)
            qs = halves(mixed_ref[0, rows, lanes])
            k = mixed_ref[0, rows, klanes]
            v = mixed_ref[0, rows, vlanes]
            das = halves(da_ref[rows, lanes])
            near_low = pn_ref[j, p]
            far_low = pf_ref[j, p]
            near = near_low.astype(F32)
            far = far_low.astype(F32)
            slope_near = nt(v, das)
            slope_far = nt(far_ref[0, :, klanes], das)
            inner = jnp.sum(near * slope_near, axis=0, keepdims=True) + jnp.sum(far * slope_far, axis=0, keepdims=True)
            near = (near * (slope_near - inner)).astype(BF16)
            far = (far * (slope_far - inner)).astype(BF16)
            dmixed_ref[0, rows, vlanes] = nn(near_low, das).astype(BF16)
            dmixed_ref[0, rows, klanes] = nn(near, qs).astype(BF16)
            dfar_ref[0, :, klanes] += nn(far_low, das)
            dfar_ref[0, :, lanes] += nn(far, qs)
            kt = k.astype(F32).T.astype(BF16)
            both = nn(kt, near) + nn(fart_ref[lanes, :], far)
            dmixed_ref[0, rows, lanes] = (corner(both).T * 0.125).astype(BF16)
        return carry

    lax.fori_loop(0, spans, attend_back, 0)


def main_call(x, g, mixed, far, wo, wu, wd, gains, shifts):
    batches, tokens, _ = x.shape
    spans = tokens // SPAN
    count = far.shape[1]
    one = pl.Buffered(1)
    seq = lambda width: pl.BlockSpec((1, tokens, width), lambda b: (b, 0, 0))
    seq1 = lambda width: pl.BlockSpec((1, tokens, width), lambda b: (b, 0, 0), pipeline_mode=one)
    whole = lambda *shape: pl.BlockSpec(shape, lambda b: (0,) * len(shape), pipeline_mode=one)
    return pl.pallas_call(
        main_kernel,
        grid=(batches,),
        in_specs=[
            seq(D), seq(D), seq(3 * D),
            pl.BlockSpec((1, count, 2 * D), lambda b: (b, 0, 0)),
            whole(D, D), whole(D, FF), whole(FF, D), whole(2, D), whole(2, D),
        ],
        out_specs=[
            seq(D), seq(D), seq1(3 * D),
            pl.BlockSpec((1, count, 2 * D), lambda b: (b, 0, 0)),
            whole(D, D), whole(D, FF), whole(D, FF), whole(8, D), whole(8, D),
        ],
        out_shape=[
            jax.ShapeDtypeStruct((batches, tokens, D), BF16),
            jax.ShapeDtypeStruct((batches, tokens, D), BF16),
            jax.ShapeDtypeStruct((batches, tokens, 3 * D), BF16),
            jax.ShapeDtypeStruct((batches, count, 2 * D), F32),
            jax.ShapeDtypeStruct((D, D), F32),
            jax.ShapeDtypeStruct((D, FF), F32),
            jax.ShapeDtypeStruct((D, FF), F32),
            jax.ShapeDtypeStruct((8, D), F32),
            jax.ShapeDtypeStruct((8, D), F32),
        ],
        scratch_shapes=[
            pltpu.VMEM((tokens, D), BF16),
            pltpu.VMEM((D, tokens), BF16),
            pltpu.VMEM((spans, PAIRS, SPAN, 2 * SPAN), BF16),
            pltpu.VMEM((spans, PAIRS, count, 2 * SPAN), BF16),
            pltpu.VMEM((8, D), BF16),
            pltpu.VMEM((D, tokens), BF16),
            pltpu.VMEM((D, tokens), BF16),
            pltpu.VMEM((tokens, FF), BF16),
            pltpu.VMEM((tokens, FF), BF16),
            pltpu.VMEM((tokens, D), BF16),
            pltpu.VMEM((tokens, D), BF16),
            pltpu.VMEM((2 * D, count), BF16),
        ],
        compiler_params=pltpu.CompilerParams(vmem_limit_bytes=VMEM_LIMIT),
        name="main",
    )(x, g, mixed, far, wo, wu, wd, gains, shifts)


def last_kernel(
    x_ref, dmixed_ref, gsum_ref, gmid_ref, w_ref, gain_ref, shift_ref,
    gin_ref, gw_ref, ggain_ref, gshift_ref,
    gm_ref, nt_ref,
):
    tokens = x_ref.shape[1]
    gain = gain_ref[0:1, :]
    shift = shift_ref[0:1, :]

    @pl.when(pl.program_id(0) == 0)
    def _():
        gw_ref[...] = jnp.zeros_like(gw_ref)
        ggain_ref[...] = jnp.zeros_like(ggain_ref)
        gshift_ref[...] = jnp.zeros_like(gshift_ref)

    tile = 256

    def step(i, carry):
        rows = pl.ds(pl.multiple_of(i * tile, tile), tile)
        unit, rstd = unit_of(x_ref[0, rows, :].astype(F32))
        nt_ref[:, rows] = (unit * gain + shift).T.astype(BF16)
        gm_ref[rows, 0:D] = dmixed_ref[0, rows, 0:D]
        for s in range(tile // SPAN):
            srows = pl.ds(pl.multiple_of(i * tile + s * SPAN, SPAN), SPAN)
            extra = gsum_ref[0, pl.ds(i * (tile // SPAN) + s, 1), :] * SPAN ** (-0.5)
            gm_ref[srows, D:] = (dmixed_ref[0, srows, D:].astype(F32) + extra).astype(BF16)
        grad = nt(gm_ref[rows, :], w_ref[...])
        ggain_ref[...] += fold8(grad * unit)
        gshift_ref[...] += fold8(grad)
        gin_ref[0, rows, :] = (gmid_ref[0, rows, :].astype(F32) + norm_back(grad, unit, rstd, gain)).astype(BF16)
        return carry

    lax.fori_loop(0, tokens // tile, step, 0)

    def wgrad(c, carry):
        cols = pl.ds(pl.multiple_of(c * 512, 512), 512)
        gw_ref[:, cols] += nn(nt_ref[...], gm_ref[:, cols])
        return carry

    lax.fori_loop(0, 3, wgrad, 0)


def last_call(x, dmixed, gsum, gmid, w, gains, shifts):
    batches, tokens, _ = x.shape
    spans = tokens // SPAN
    one = pl.Buffered(1)
    seq = lambda width: pl.BlockSpec((1, tokens, width), lambda b: (b, 0, 0))
    whole = lambda *shape: pl.BlockSpec(shape, lambda b: (0,) * len(shape), pipeline_mode=one)
    return pl.pallas_call(
        last_kernel,
        grid=(batches,),
        in_specs=[
            seq(D), seq(3 * D), pl.BlockSpec((1, spans, 2 * D), lambda b: (b, 0, 0)), seq(D),
            whole(D, 3 * D), whole(2, D), whole(2, D),
        ],
        out_specs=[seq(D), whole(D, 3 * D), whole(8, D), whole(8, D)],
        out_shape=[
            jax.ShapeDtypeStruct((batches, tokens, D), BF16),
            jax.ShapeDtypeStruct((D, 3 * D), F32),
            jax.ShapeDtypeStruct((8, D), F32),
            jax.ShapeDtypeStruct((8, D), F32),
        ],
        scratch_shapes=[pltpu.VMEM((tokens, 3 * D), BF16), pltpu.VMEM((D, tokens), BF16)],
        compiler_params=pltpu.CompilerParams(vmem_limit_bytes=VMEM_LIMIT),
        name="last",
    )(x, dmixed, gsum, gmid, w, gains, shifts)


def scatter(grad, dim=0):
    low = lax.psum_scatter(grad.astype(BF16), "fsdp", scatter_dimension=dim, tiled=True)
    return lax.psum(low, "ctx").astype(F32)


def local(x, g, qkv_weight, out_weight, up_weight, down_weight, norm_gains, norm_shifts):
    gather = lambda shard, axis: lax.all_gather(shard, "fsdp", axis=axis, tiled=True)
    wq, wo, wu, wd = (gather(w, 0) for w in (qkv_weight, out_weight, up_weight, down_weight))
    gains = gather(norm_gains, 1).astype(F32)
    shifts = gather(norm_shifts, 1).astype(F32)
    mixed, summary = qkv_call(x, wq, gains, shifts)
    far = lax.all_gather(summary.astype(BF16), "ctx", axis=1, tiled=True)
    out, gmid, dmixed, dfar, go, gu, gdt, ggain2, gshift2 = main_call(x, g, mixed, far, wo, wu, wd, gains, shifts)
    gsum = lax.psum_scatter(dfar.astype(BF16), "ctx", scatter_dimension=1, tiled=True).astype(F32)
    gin, gw, ggain1, gshift1 = last_call(x, dmixed, gsum, gmid, wq, gains, shifts)
    small = jnp.stack([jnp.sum(v, axis=0) for v in (ggain1, ggain2, gshift1, gshift2)])
    small = lax.psum(small, ("fsdp", "ctx"))
    width = norm_gains.shape[1]
    small = lax.dynamic_slice_in_dim(small, lax.axis_index("fsdp") * width, width, axis=1)
    return (
        out, gin, scatter(gw), scatter(go), scatter(gu), scatter(gdt, 1).T,
        small[0:2], small[2], small[3],
    )


def solution(mesh):
    weight, norm, token = P("fsdp", None), P(None, "fsdp"), P("fsdp", "ctx", None)
    return jax.shard_map(
        local,
        mesh=mesh,
        in_specs=(token, token, weight, weight, weight, weight, norm, norm),
        out_specs=(token, token, weight, weight, weight, weight, norm, P("fsdp"), P("fsdp")),
        check_vma=False,
    )
```

```python
import functools

import jax
import jax.numpy as jnp
from jax import lax
from jax.experimental import pallas as pl
from jax.experimental.pallas import tpu as pltpu
from jax.sharding import PartitionSpec as P

D = 512
HEADS = 8
FF = 2048
SPAN = 128
CONT = 1024
PAIRS = HEADS // 2

EPS = 1e-05
NEG = -1e30
F32 = jnp.float32
BF16 = jnp.bfloat16
VMEM_LIMIT = 60 * 1024 * 1024


def nn(a, b):
    return lax.dot_general(a, b, (((1,), (0,)), ((), ())), preferred_element_type=F32)


def nt(a, b):
    return lax.dot_general(a, b, (((1,), (1,)), ((), ())), preferred_element_type=F32)


def unit_of(values):
    center = values - jnp.mean(values, axis=-1, keepdims=True)
    rstd = lax.rsqrt(jnp.mean(center * center, axis=-1, keepdims=True) + EPS)
    return center * rstd, rstd


def norm_back(grad, unit, rstd, gain):
    scaled = grad * gain
    return rstd * (
        scaled
        - jnp.mean(scaled, axis=-1, keepdims=True)
        - unit * jnp.mean(scaled * unit, axis=-1, keepdims=True)
    )


def fold8(values):
    rows = values.shape[0]
    return jnp.sum(values.reshape(rows // 8, 8, values.shape[1]), axis=0)


def gelu_pair(x):
    e = jnp.exp(x * x * -0.5)
    t = 1.0 / (1.0 + (0.3275911 * 0.7071067811865476) * jnp.abs(x))
    poly = 1.061405429 * 0.5
    poly = poly * t + (-1.453152027 * 0.5)
    poly = poly * t + (1.421413741 * 0.5)
    poly = poly * t + (-0.284496736 * 0.5)
    poly = poly * t + (0.254829592 * 0.5)
    half = poly * t * e
    cdf = jnp.where(x < 0.0, half, 1.0 - half)
    return x * cdf, cdf + x * (e * 0.3989422804014327)


def qkv_kernel(x_ref, w_ref, gain_ref, shift_ref, mixed_ref, summary_ref):
    gain = gain_ref[0:1, :]
    shift = shift_ref[0:1, :]
    tile = 256

    def step(i, carry):
        rows = pl.ds(pl.multiple_of(i * tile, tile), tile)
        unit, _ = unit_of(x_ref[0, rows, :].astype(F32))
        low = (unit * gain + shift).astype(BF16)
        mixed_ref[0, rows, 0:D] = (nn(low, w_ref[:, 0:D]).astype(BF16).astype(F32) * 0.125).astype(BF16)
        for c in range(2):
            cols = slice(D + c * D, 2 * D + c * D)
            part = nn(low, w_ref[:, cols])
            mixed_ref[0, rows, cols] = part.astype(BF16)
            for s in range(tile // SPAN):
                total = jnp.sum(part[s * SPAN : (s + 1) * SPAN, :], axis=0, keepdims=True)
                summary_ref[0, pl.ds(i * (tile // SPAN) + s, 1), c * D : (c + 1) * D] = total * SPAN ** (-0.5)
        return carry

    lax.fori_loop(0, x_ref.shape[1] // tile, step, 0)


def qkv_call(x, w, gains, shifts):
    batches, tokens, _ = x.shape
    spans = tokens // SPAN
    return pl.pallas_call(
        qkv_kernel,
        grid=(batches,),
        in_specs=[
            pl.BlockSpec((1, tokens, D), lambda b: (b, 0, 0)),
            pl.BlockSpec((D, 3 * D), lambda b: (0, 0), pipeline_mode=pl.Buffered(1)),
            pl.BlockSpec((2, D), lambda b: (0, 0), pipeline_mode=pl.Buffered(1)),
            pl.BlockSpec((2, D), lambda b: (0, 0), pipeline_mode=pl.Buffered(1)),
        ],
        out_specs=[
            pl.BlockSpec((1, tokens, 3 * D), lambda b: (b, 0, 0)),
            pl.BlockSpec((1, spans, 2 * D), lambda b: (b, 0, 0)),
        ],
        out_shape=[
            jax.ShapeDtypeStruct((batches, tokens, 3 * D), BF16),
            jax.ShapeDtypeStruct((batches, spans, 2 * D), F32),
        ],
        compiler_params=pltpu.CompilerParams(vmem_limit_bytes=VMEM_LIMIT),
        name="qkv",
    )(x, w, gains, shifts)


def main_kernel(
    x_ref, g_ref, mixed_ref, far_ref, wo_ref, wu_ref, wd_ref, gain_ref, shift_ref,
    out_ref, gmid_ref, dmixed_ref, dfar_ref, go_ref, gu_ref, gd_ref, ggain_ref, gshift_ref,
    att_ref, attt_ref, pn_ref, pf_ref, n2_ref, n2t_ref, gt_ref, act_ref, gh_ref, gb_ref, da_ref, fart_ref,
):
    tokens = x_ref.shape[1]
    spans = tokens // SPAN
    count = far_ref.shape[1]
    prompt = count // 2
    first = lax.axis_index("ctx") * spans

    @pl.when(pl.program_id(0) == 0)
    def _():
        go_ref[...] = jnp.zeros_like(go_ref)
        gu_ref[...] = jnp.zeros_like(gu_ref)
        gd_ref[...] = jnp.zeros_like(gd_ref)
        ggain_ref[...] = jnp.zeros_like(ggain_ref)
        gshift_ref[...] = jnp.zeros_like(gshift_ref)

    dfar_ref[...] = jnp.zeros_like(dfar_ref)
    fart_ref[...] = far_ref[0].astype(F32).T.astype(BF16)

    def halves(pair):
        low = lax.broadcasted_iota(jnp.int32, pair.shape, 1) < 64
        zero = jnp.zeros_like(pair)
        return jnp.concatenate([jnp.where(low, pair, zero), jnp.where(low, zero, pair)], axis=0)

    def corner(both):
        return jnp.concatenate([both[0:64, 0:SPAN], both[64:128, SPAN : 2 * SPAN]], axis=0)

    def attend(j, carry):
        rows = pl.ds(pl.multiple_of(j * SPAN, SPAN), SPAN)
        key_id = lax.broadcasted_iota(jnp.int32, (SPAN, 2 * SPAN), 0)
        query_id = lax.broadcasted_iota(jnp.int32, (SPAN, 2 * SPAN), 1) & (SPAN - 1)
        causal = key_id <= query_id
        far_id = lax.broadcasted_iota(jnp.int32, (count, 2 * SPAN), 0)
        mine = first + j
        segment = (mine - prompt) >> 3
        seen = (far_id < mine) & ((far_id < prompt) | (((far_id - prompt) >> 3) == segment))
        for p in range(PAIRS):
            lanes = slice(p * SPAN, (p + 1) * SPAN)
            qs = halves(mixed_ref[0, rows, lanes])
            k = mixed_ref[0, rows, D + p * SPAN : D + (p + 1) * SPAN]
            v = mixed_ref[0, rows, 2 * D + p * SPAN : 2 * D + (p + 1) * SPAN]
            near = jnp.where(causal, nt(k, qs), NEG)
            far = jnp.where(seen, nt(far_ref[0, :, lanes], qs), NEG)
            peak = jnp.maximum(jnp.max(near, axis=0, keepdims=True), jnp.max(far, axis=0, keepdims=True))
            near = jnp.exp(near - peak)
            far = jnp.exp(far - peak)
            inv = 1.0 / (jnp.sum(near, axis=0, keepdims=True) + jnp.sum(far, axis=0, keepdims=True))
            near = (near * inv).astype(BF16)
            far = (far * inv).astype(BF16)
            pn_ref[j, p] = near
            pf_ref[j, p] = far
            vt = v.astype(F32).T.astype(BF16)
            both = nn(vt, near) + nn(fart_ref[D + p * SPAN : D + (p + 1) * SPAN, :], far)
            att = corner(both)
            attt_ref[lanes, rows] = att.astype(BF16)
            att_ref[rows, lanes] = att.T.astype(BF16)
        return carry

    lax.fori_loop(0, spans, attend, 0)

    tile = 256
    gain = gain_ref[1:2, :]
    shift = shift_ref[1:2, :]

    def mlp(i, carry):
        rows = pl.ds(pl.multiple_of(i * tile, tile), tile)
        middle = x_ref[0, rows, :].astype(F32) + nn(att_ref[rows, :], wo_ref[...])
        unit, rstd = unit_of(middle)
        low = unit * gain + shift
        n2t_ref[:, rows] = low.T.astype(BF16)
        low = low.astype(BF16)
        g = g_ref[0, rows, :]
        gt_ref[:, rows] = g.astype(F32).T.astype(BF16)
        for c in range(4):
            cols = slice(c * 512, (c + 1) * 512)
            act, slope = gelu_pair(nn(low, wu_ref[:, cols]))
            act_ref[rows, cols] = act.astype(BF16)
            gh_ref[rows, cols] = (nt(g, wd_ref[cols, :]) * slope).astype(BF16)
        out_ref[0, rows, :] = (middle + nn(act_ref[rows, :], wd_ref[...])).astype(BF16)
        grad = nt(gh_ref[rows, :], wu_ref[...])
        ggain_ref[...] += fold8(grad * unit)
        gshift_ref[...] += fold8(grad)
        grad = g.astype(F32) + norm_back(grad, unit, rstd, gain)
        low = grad.astype(BF16)
        gmid_ref[0, rows, :] = low
        gb_ref[rows, :] = low
        da_ref[rows, :] = nt(low, wo_ref[...]).astype(BF16)
        return carry

    lax.fori_loop(0, tokens // tile, mlp, 0)

    go_ref[...] += nn(attt_ref[...], gb_ref[...])

    def wgrad(c, carry):
        cols = pl.ds(pl.multiple_of(c * 512, 512), 512)
        gu_ref[:, cols] += nn(n2t_ref[...], gh_ref[:, cols])
        gd_ref[:, cols] += nn(gt_ref[...], act_ref[:, cols])
        return carry

    lax.fori_loop(0, 4, wgrad, 0)

    def attend_back(j, carry):
        rows = pl.ds(pl.multiple_of(j * SPAN, SPAN), SPAN)
        for p in range(PAIRS):
            lanes = slice(p * SPAN, (p + 1) * SPAN)
            klanes = slice(D + p * SPAN, D + (p + 1) * SPAN)
            vlanes = slice(2 * D + p * SPAN, 2 * D + (p + 1) * SPAN)
            qs = halves(mixed_ref[0, rows, lanes])
            k = mixed_ref[0, rows, klanes]
            v = mixed_ref[0, rows, vlanes]
            das = halves(da_ref[rows, lanes])
            near_low = pn_ref[j, p]
            far_low = pf_ref[j, p]
            near = near_low.astype(F32)
            far = far_low.astype(F32)
            slope_near = nt(v, das)
            slope_far = nt(far_ref[0, :, klanes], das)
            inner = jnp.sum(near * slope_near, axis=0, keepdims=True) + jnp.sum(far * slope_far, axis=0, keepdims=True)
            near = (near * (slope_near - inner)).astype(BF16)
            far = (far * (slope_far - inner)).astype(BF16)
            dmixed_ref[0, rows, vlanes] = nn(near_low, das).astype(BF16)
            dmixed_ref[0, rows, klanes] = nn(near, qs).astype(BF16)
            dfar_ref[0, :, klanes] += nn(far_low, das)
            dfar_ref[0, :, lanes] += nn(far, qs)
            kt = k.astype(F32).T.astype(BF16)
            both = nn(kt, near) + nn(fart_ref[lanes, :], far)
            dmixed_ref[0, rows, lanes] = (corner(both).T * 0.125).astype(BF16)
        return carry

    lax.fori_loop(0, spans, attend_back, 0)


def main_call(x, g, mixed, far, wo, wu, wd, gains, shifts):
    batches, tokens, _ = x.shape
    spans = tokens // SPAN
    count = far.shape[1]
    one = pl.Buffered(1)
    seq = lambda width: pl.BlockSpec((1, tokens, width), lambda b: (b, 0, 0))
    seq1 = lambda width: pl.BlockSpec((1, tokens, width), lambda b: (b, 0, 0), pipeline_mode=one)
    whole = lambda *shape: pl.BlockSpec(shape, lambda b: (0,) * len(shape), pipeline_mode=one)
    return pl.pallas_call(
        main_kernel,
        grid=(batches,),
        in_specs=[
            seq(D), seq(D), seq(3 * D),
            pl.BlockSpec((1, count, 2 * D), lambda b: (b, 0, 0)),
            whole(D, D), whole(D, FF), whole(FF, D), whole(2, D), whole(2, D),
        ],
        out_specs=[
            seq(D), seq(D), seq1(3 * D),
            pl.BlockSpec((1, count, 2 * D), lambda b: (b, 0, 0)),
            whole(D, D), whole(D, FF), whole(D, FF), whole(8, D), whole(8, D),
        ],
        out_shape=[
            jax.ShapeDtypeStruct((batches, tokens, D), BF16),
            jax.ShapeDtypeStruct((batches, tokens, D), BF16),
            jax.ShapeDtypeStruct((batches, tokens, 3 * D), BF16),
            jax.ShapeDtypeStruct((batches, count, 2 * D), F32),
            jax.ShapeDtypeStruct((D, D), F32),
            jax.ShapeDtypeStruct((D, FF), F32),
            jax.ShapeDtypeStruct((D, FF), F32),
            jax.ShapeDtypeStruct((8, D), F32),
            jax.ShapeDtypeStruct((8, D), F32),
        ],
        scratch_shapes=[
            pltpu.VMEM((tokens, D), BF16),
            pltpu.VMEM((D, tokens), BF16),
            pltpu.VMEM((spans, PAIRS, SPAN, 2 * SPAN), BF16),
            pltpu.VMEM((spans, PAIRS, count, 2 * SPAN), BF16),
            pltpu.VMEM((8, D), BF16),
            pltpu.VMEM((D, tokens), BF16),
            pltpu.VMEM((D, tokens), BF16),
            pltpu.VMEM((tokens, FF), BF16),
            pltpu.VMEM((tokens, FF), BF16),
            pltpu.VMEM((tokens, D), BF16),
            pltpu.VMEM((tokens, D), BF16),
            pltpu.VMEM((2 * D, count), BF16),
        ],
        compiler_params=pltpu.CompilerParams(vmem_limit_bytes=VMEM_LIMIT),
        name="main",
    )(x, g, mixed, far, wo, wu, wd, gains, shifts)


def last_kernel(
    x_ref, dmixed_ref, gsum_ref, gmid_ref, w_ref, gain_ref, shift_ref,
    gin_ref, gw_ref, ggain_ref, gshift_ref,
    gm_ref, nt_ref,
):
    tokens = x_ref.shape[1]
    gain = gain_ref[0:1, :]
    shift = shift_ref[0:1, :]

    @pl.when(pl.program_id(0) == 0)
    def _():
        gw_ref[...] = jnp.zeros_like(gw_ref)
        ggain_ref[...] = jnp.zeros_like(ggain_ref)
        gshift_ref[...] = jnp.zeros_like(gshift_ref)

    tile = 256

    def step(i, carry):
        rows = pl.ds(pl.multiple_of(i * tile, tile), tile)
        unit, rstd = unit_of(x_ref[0, rows, :].astype(F32))
        nt_ref[:, rows] = (unit * gain + shift).T.astype(BF16)
        gm_ref[rows, 0:D] = dmixed_ref[0, rows, 0:D]
        for s in range(tile // SPAN):
            srows = pl.ds(pl.multiple_of(i * tile + s * SPAN, SPAN), SPAN)
            extra = gsum_ref[0, pl.ds(i * (tile // SPAN) + s, 1), :] * SPAN ** (-0.5)
            gm_ref[srows, D:] = (dmixed_ref[0, srows, D:].astype(F32) + extra).astype(BF16)
        grad = nt(gm_ref[rows, :], w_ref[...])
        ggain_ref[...] += fold8(grad * unit)
        gshift_ref[...] += fold8(grad)
        gin_ref[0, rows, :] = (gmid_ref[0, rows, :].astype(F32) + norm_back(grad, unit, rstd, gain)).astype(BF16)
        return carry

    lax.fori_loop(0, tokens // tile, step, 0)

    def wgrad(c, carry):
        cols = pl.ds(pl.multiple_of(c * 512, 512), 512)
        gw_ref[:, cols] += nn(nt_ref[...], gm_ref[:, cols])
        return carry

    lax.fori_loop(0, 3, wgrad, 0)


def last_call(x, dmixed, gsum, gmid, w, gains, shifts):
    batches, tokens, _ = x.shape
    spans = tokens // SPAN
    one = pl.Buffered(1)
    seq = lambda width: pl.BlockSpec((1, tokens, width), lambda b: (b, 0, 0))
    whole = lambda *shape: pl.BlockSpec(shape, lambda b: (0,) * len(shape), pipeline_mode=one)
    return pl.pallas_call(
        last_kernel,
        grid=(batches,),
        in_specs=[
            seq(D), seq(3 * D), pl.BlockSpec((1, spans, 2 * D), lambda b: (b, 0, 0)), seq(D),
            whole(D, 3 * D), whole(2, D), whole(2, D),
        ],
        out_specs=[seq(D), whole(D, 3 * D), whole(8, D), whole(8, D)],
        out_shape=[
            jax.ShapeDtypeStruct((batches, tokens, D), BF16),
            jax.ShapeDtypeStruct((D, 3 * D), F32),
            jax.ShapeDtypeStruct((8, D), F32),
            jax.ShapeDtypeStruct((8, D), F32),
        ],
        scratch_shapes=[pltpu.VMEM((tokens, 3 * D), BF16), pltpu.VMEM((D, tokens), BF16)],
        compiler_params=pltpu.CompilerParams(vmem_limit_bytes=VMEM_LIMIT),
        name="last",
    )(x, dmixed, gsum, gmid, w, gains, shifts)


MESH = pl.DeviceIdType.MESH


class Place:
    def __init__(self, mesh_shape):
        self.n, self.m = mesh_shape["ctx"], mesh_shape["fsdp"]
        self.inner = 2
        self.line = self.m // 2
        self.c, self.f = lax.axis_index("ctx"), lax.axis_index("fsdp")
        self.core = self.c % 2
        self.z, self.y = self.f // 2, self.f % 2

    def mate(self):
        return {"ctx": self.c + 1 - 2 * self.core, "fsdp": self.f}

    def across(self):
        return {"ctx": self.c, "fsdp": self.z * 2 + 1 - self.y}

    def along(self, step):
        return {"ctx": self.c, "fsdp": self.f + 2 * step}

    def greet(self, barrier, mate=True, grid=True, ctx=False):
        signal = lambda where: pl.semaphore_signal(barrier, inc=1, device_id=where, device_id_type=MESH)
        count = 0
        if ctx:
            for k in range(1, self.n):
                signal({"ctx": (self.c + k) % self.n, "fsdp": self.f})
            count = self.n - 1
        elif mate:
            signal(self.mate())
            count = 1
        if grid:
            signal(self.across())
            up = self.z < self.line - 1
            down = self.z > 0

            @pl.when(up)
            def _():
                signal(self.along(1))

            @pl.when(down)
            def _():
                signal(self.along(-1))

            count = count + 1 + up.astype(jnp.int32) + down.astype(jnp.int32)
        pl.semaphore_wait(barrier, count)


def remote(src, dst, send, recv, where):
    return pltpu.make_async_remote_copy(
        src_ref=src, dst_ref=dst, send_sem=send, recv_sem=recv, device_id=where, device_id_type=MESH
    )


class Gather:
    def __init__(self, place, shard, full, sems, channel):
        self.p, self.shard, self.full = place, shard, full
        self.send, self.recv, self.local = sems
        self.ch = channel

    def piece(self, j, y, core):
        return self.full.at[j * 2 + y, core]

    def line_copy(self, kind, j, source=None):
        p = self.p
        here = self.piece(j, p.y, p.core)
        return remote(
            here if source is None else source, here, self.send.at[self.ch, kind, j], self.recv.at[self.ch, kind, j],
            p.along(1 if kind == 0 else -1),
        )

    def across_copy(self, j, y, source=None):
        p = self.p
        here = self.piece(j, y, p.core)
        return remote(
            here if source is None else source, here, self.send.at[self.ch, 2, j], self.recv.at[self.ch, 2, j], p.across()
        )

    def mate_copy(self, j, y, core):
        p = self.p
        here = self.piece(j, y, core)
        slot = 3 + (y != p.y).astype(jnp.int32)
        return remote(here, here, self.send.at[self.ch, slot, j], self.recv.at[self.ch, slot, j], p.mate())

    def own(self):
        return pltpu.make_async_copy(self.shard, self.full.at[self.p.f], self.local.at[self.ch])

    def step(self, k):
        p, line = self.p, self.p.line
        z, y, core = p.z, p.y, p.core
        if k == 0:
            self.own().start()
            source = self.shard.at[core]

            @pl.when(z < line - 1)
            def _():
                self.line_copy(0, z, source).start()

            @pl.when(z > 0)
            def _():
                self.line_copy(1, z, source).start()

            self.across_copy(z, y, source).start()
            return
        if k < line:

            @pl.when(z >= k)
            def _():
                j = z - k
                self.line_copy(0, j).wait_recv()

                @pl.when(z < line - 1)
                def _():
                    self.line_copy(0, j).start()

                self.across_copy(j, y).start()
                self.mate_copy(j, y, core).start()

            @pl.when(z + k < line)
            def _():
                j = z + k
                self.line_copy(1, j).wait_recv()

                @pl.when(z > 0)
                def _():
                    self.line_copy(1, j).start()

                self.across_copy(j, y).start()
                self.mate_copy(j, y, core).start()

        far = k - 1
        other = 1 - y

        def landed(j):
            self.across_copy(j, other).wait_recv()
            self.mate_copy(j, other, core).start()

        if far == 0:
            landed(z)
        elif far < line:

            @pl.when(z >= far)
            def _():
                landed(z - far)

            @pl.when(z + far < line)
            def _():
                landed(z + far)

    def steps(self):
        return self.p.line + 1

    def finish(self):
        p, line = self.p, self.p.line
        z, y = p.z, p.y
        mate_core = 1 - p.core
        self.own().wait()
        for j in range(line):

            @pl.when(j != z)
            def _():
                self.mate_copy(j, y, mate_core).wait_recv()
                self.mate_copy(j, y, p.core).wait_send()

            self.mate_copy(j, 1 - y, mate_core).wait_recv()
            self.mate_copy(j, 1 - y, p.core).wait_send()
            self.across_copy(j, y).wait_send()

            @pl.when((j <= z) & (z < line - 1))
            def _():
                self.line_copy(0, j).wait_send()

            @pl.when((j >= z) & (z > 0))
            def _():
                self.line_copy(1, j).wait_send()


def gather_sems(place_line, channels):
    return [
        pltpu.SemaphoreType.DMA((channels, 5, place_line)),
        pltpu.SemaphoreType.DMA((channels, 5, place_line)),
        pltpu.SemaphoreType.DMA((channels,)),
    ]


def gather_kernel(shape, *refs):
    count = (len(refs) - 3) // 2
    shards, fulls, sems = refs[:count], refs[count : 2 * count], refs[2 * count :]
    place = Place(shape)
    place.greet(pltpu.get_barrier_semaphore())
    parts = [Gather(place, s, f, sems, i) for i, (s, f) in enumerate(zip(shards, fulls))]
    for part in parts:
        part.step(0)
    for k in range(1, parts[0].steps()):
        for part in parts:
            part.step(k)
    for part in parts:
        part.finish()


def gather_call(shape, shards):
    m = shape["fsdp"]
    any_spec = pl.BlockSpec(memory_space=pl.ANY)
    return pl.pallas_call(
        functools.partial(gather_kernel, shape),
        in_specs=[any_spec] * len(shards),
        out_specs=[any_spec] * len(shards),
        out_shape=[jax.ShapeDtypeStruct((m,) + s.shape, s.dtype) for s in shards],
        scratch_shapes=gather_sems(m // 2, len(shards)),
        compiler_params=pltpu.CompilerParams(collective_id=0, has_side_effects=True),
        name="gather",
    )(*shards)


def share_kernel(shape, own_ref, all_ref, send, recv, local):
    place = Place(shape)
    place.greet(pltpu.get_barrier_semaphore(), grid=False, ctx=True)
    mine = pltpu.make_async_copy(own_ref, all_ref.at[place.c], local)
    mine.start()
    copies = []
    for k in range(1, place.n):
        copies.append(
            remote(own_ref, all_ref.at[place.c], send.at[k], recv.at[k], {"ctx": (place.c + k) % place.n, "fsdp": place.f})
        )
        copies[-1].start()
    for copy in copies:
        copy.wait()
    mine.wait()


def share_call(shape, own):
    n = shape["ctx"]
    any_spec = pl.BlockSpec(memory_space=pl.ANY)
    return pl.pallas_call(
        functools.partial(share_kernel, shape),
        in_specs=[any_spec],
        out_specs=any_spec,
        out_shape=jax.ShapeDtypeStruct((n,) + own.shape, own.dtype),
        scratch_shapes=[pltpu.SemaphoreType.DMA((n,)), pltpu.SemaphoreType.DMA((n,)), pltpu.SemaphoreType.DMA],
        compiler_params=pltpu.CompilerParams(collective_id=1, has_side_effects=True),
        name="share",
    )(own)


def swap_kernel(shape, term_ref, out_ref, held, send, recv):
    place = Place(shape)
    place.greet(pltpu.get_barrier_semaphore(), grid=False, ctx=True)
    copies = []
    for k in range(1, place.n):
        to = (place.c + k) % place.n
        copies.append(remote(term_ref.at[to], held.at[k], send.at[k], recv.at[k], {"ctx": to, "fsdp": place.f}))
        copies[-1].start()
    total = term_ref[place.c].astype(F32)
    for k, copy in enumerate(copies):
        copy.wait()
        total = total + held[k + 1].astype(F32)
    out_ref[...] = total


def swap_call(shape, term):
    n = shape["ctx"]
    vmem = pl.BlockSpec(memory_space=pltpu.VMEM)
    return pl.pallas_call(
        functools.partial(swap_kernel, shape),
        in_specs=[vmem],
        out_specs=vmem,
        out_shape=jax.ShapeDtypeStruct(term.shape[1:], F32),
        scratch_shapes=[pltpu.VMEM(term.shape, BF16), pltpu.SemaphoreType.DMA((n,)), pltpu.SemaphoreType.DMA((n,))],
        compiler_params=pltpu.CompilerParams(collective_id=2, has_side_effects=True, vmem_limit_bytes=VMEM_LIMIT),
        name="swap",
    )(term)


class Reduce:
    def __init__(self, place, term, out, bufs, sems, channel):
        self.p, self.term, self.out = place, term, out
        self.one, self.two, self.up, self.down, self.parts = bufs
        self.send, self.recv = sems
        self.ch = channel

    def copy(self, src, dst, slot, where):
        return remote(src, dst, self.send.at[self.ch, slot], self.recv.at[self.ch, slot], where)

    def mate_copy(self):
        p = self.p
        return self.copy(self.term.at[:, :, 1 - p.core], self.one, 0, p.mate())

    def across_copy(self):
        p = self.p
        return self.copy(self.one.at[:, 1 - p.y], self.two, 1, p.across())

    def up_copy(self, j):
        return self.copy(self.two.at[j], self.up.at[j], 2 + j, self.p.along(1))

    def down_copy(self, j):
        return self.copy(self.two.at[j], self.down.at[j], 2 + self.p.line + j, self.p.along(-1))

    def ctx_copy(self, k):
        p = self.p
        where = {"ctx": (p.c + k) % p.n, "fsdp": p.f}
        return self.copy(self.parts.at[p.c], self.parts.at[p.c], 2 + 2 * p.line + k, where)

    def step0(self):
        self.mate_copy().start()

    def step1(self):
        p = self.p
        self.mate_copy().wait_recv()

        def add(i, carry):
            for y in range(2):
                self.one[i, y] = (self.one[i, y].astype(F32) + self.term[i, y, p.core].astype(F32)).astype(BF16)
            return carry

        lax.fori_loop(0, p.line, add, 0)
        self.across_copy().start()

    def step2(self):
        p = self.p
        self.across_copy().wait_recv()

        def add(i, carry):
            self.two[i] = (self.two[i].astype(F32) + self.one[i, p.y].astype(F32)).astype(BF16)
            return carry

        lax.fori_loop(0, p.line, add, 0)

    def line_step(self, d):
        p = self.p
        for sign, move, buf in ((1, self.up_copy, self.up), (-1, self.down_copy, self.down)):
            j = p.z + sign * d
            valid = (j < p.line) if sign > 0 else (j >= 0)
            inside = (p.z > 0) if sign > 0 else (p.z < p.line - 1)

            @pl.when(valid)
            def _():
                @pl.when(inside)
                def _():
                    move(j).wait_recv()
                    self.two[j] = (self.two[j].astype(F32) + buf[j].astype(F32)).astype(BF16)

                move(j).start()

    def step3(self):
        p = self.p
        for d in range(p.line - 1, 0, -1):
            self.line_step(d)
        z = p.z

        @pl.when(z > 0)
        def _():
            self.up_copy(z).wait_recv()
            self.two[z] = (self.two[z].astype(F32) + self.up[z].astype(F32)).astype(BF16)

        @pl.when(z < p.line - 1)
        def _():
            self.down_copy(z).wait_recv()
            self.two[z] = (self.two[z].astype(F32) + self.down[z].astype(F32)).astype(BF16)

        self.parts[p.c] = self.two[z]
        for k in range(1, p.n):
            self.ctx_copy(k).start()

    def step4(self):
        p = self.p
        for k in range(1, p.n):
            self.ctx_copy(k).wait_recv()
        for half in range(2):
            total = self.parts[half].astype(F32)
            for c in range(half + 2, p.n, 2):
                total = total + self.parts[c].astype(F32)
            self.out[half] = total
        self.mate_copy().wait_send()
        self.across_copy().wait_send()
        for j in range(p.line):

            @pl.when(j > p.z)
            def _():
                self.up_copy(j).wait_send()

            @pl.when(j < p.z)
            def _():
                self.down_copy(j).wait_send()

        for k in range(1, p.n):
            self.ctx_copy(k).wait_send()


def reduce_scratch(shape, h, w):
    line, n = shape["fsdp"] // 2, shape["ctx"]
    return [
        pltpu.VMEM((line, 2, h, w), BF16),
        pltpu.VMEM((line, h, w), BF16),
        pltpu.VMEM((line, h, w), BF16),
        pltpu.VMEM((line, h, w), BF16),
        pltpu.VMEM((n, h, w), BF16),
    ]


def reduce_sems(shape, channels):
    slots = 2 + shape["fsdp"] + shape["ctx"]
    return [pltpu.SemaphoreType.DMA((channels, slots))] * 2


def reduce_kernel(shape, count, *refs):
    terms, outs, bufs, sems = refs[:count], refs[count : 2 * count], refs[2 * count : 7 * count], refs[7 * count :]
    place = Place(shape)
    place.greet(pltpu.get_barrier_semaphore(), ctx=True)
    parts = [Reduce(place, t, o, bufs[5 * i : 5 * i + 5], sems, i) for i, (t, o) in enumerate(zip(terms, outs))]
    for name in ("step0", "step1", "step2", "step3", "step4"):
        for part in parts:
            getattr(part, name)()


def reduce_call(shape, terms):
    line = shape["fsdp"] // 2
    terms = [t.reshape(line, 2, 2, t.shape[0] // (4 * line), t.shape[1]) for t in terms]
    vmem = pl.BlockSpec(memory_space=pltpu.VMEM)
    scratch = []
    for t in terms:
        scratch += reduce_scratch(shape, *t.shape[3:])
    outs = pl.pallas_call(
        functools.partial(reduce_kernel, shape, len(terms)),
        in_specs=[vmem] * len(terms),
        out_specs=[vmem] * len(terms),
        out_shape=[jax.ShapeDtypeStruct(t.shape[2:], F32) for t in terms],
        scratch_shapes=scratch + reduce_sems(shape, len(terms)),
        compiler_params=pltpu.CompilerParams(collective_id=3, has_side_effects=True, vmem_limit_bytes=VMEM_LIMIT),
        name="reduce",
    )(*terms)
    return [o.reshape(-1, o.shape[-1]) for o in outs]


def local(shape, x, g, qkv_weight, out_weight, up_weight, down_weight, norm_gains, norm_shifts):
    n, m = shape["ctx"], shape["fsdp"]
    width = norm_gains.shape[1]
    norms = jnp.concatenate([norm_gains, norm_shifts], axis=0).astype(F32)
    norms = jnp.pad(norms, ((0, 4), (0, 128 - width)))
    halved = lambda shard: shard.reshape(2, shard.shape[0] // 2, shard.shape[1])
    shards = [halved(v) for v in (qkv_weight, jnp.concatenate([norms, norms], axis=0), out_weight, up_weight, down_weight)]
    wq, norms, wo, wu, wd = gather_call(shape, shards)
    wq, wo, wu, wd = (w.reshape(-1, w.shape[-1]) for w in (wq, wo, wu, wd))
    norms = norms[:, 0, 0:4, 0:width].transpose(1, 0, 2).reshape(4, D)
    gains, shifts = norms[0:2], norms[2:4]
    mixed, summary = qkv_call(x, wq, gains, shifts)
    far = share_call(shape, summary.astype(BF16))
    batches, spans = summary.shape[0:2]
    far = far.transpose(1, 0, 2, 3).reshape(batches, n * spans, 2 * D)
    out, gmid, dmixed, dfar, go, gu, gdt, ggain2, gshift2 = main_call(x, g, mixed, far, wo, wu, wd, gains, shifts)
    dfar = dfar.astype(BF16).reshape(batches, n, spans, 2 * D).transpose(1, 0, 2, 3)
    gsum = swap_call(shape, dfar)
    gin, gw, ggain1, gshift1 = last_call(x, dmixed, gsum, gmid, wq, gains, shifts)
    small = jnp.stack([jnp.sum(v, axis=0) for v in (ggain1, ggain2, gshift1, gshift2)])
    small = small.reshape(4, m, width).transpose(1, 0, 2)
    small = jnp.pad(small, ((0, 0), (0, 12), (0, 128 - width))).reshape(m * 16, 128)
    gw, go, gu, gd, small = reduce_call(shape, [gw.astype(BF16), go.astype(BF16), gu.astype(BF16), gdt.astype(BF16).T, small.astype(BF16)])
    small = small[0:4, 0:width]
    return out, gin, gw, go, gu, gd, small[0:2], small[2], small[3]


def solution(mesh):
    weight, norm, token = P("fsdp", None), P(None, "fsdp"), P("fsdp", "ctx", None)
    return jax.shard_map(
        functools.partial(local, dict(mesh.shape)),
        mesh=mesh,
        in_specs=(token, token, weight, weight, weight, weight, norm, norm),
        out_specs=(token, token, weight, weight, weight, weight, norm, P("fsdp"), P("fsdp")),
        check_vma=False,
    )
```

```python
import functools

import jax
import jax.numpy as jnp
from jax import lax
from jax.experimental import pallas as pl
from jax.experimental.pallas import tpu as pltpu
from jax.sharding import PartitionSpec as P

D = 512
HEADS = 8
FF = 2048
SPAN = 128
CONT = 1024
PAIRS = HEADS // 2

EPS = 1e-05
NEG = -1e30
F32 = jnp.float32
BF16 = jnp.bfloat16
VMEM_LIMIT = 60 * 1024 * 1024


def nn(a, b):
    return lax.dot_general(a, b, (((1,), (0,)), ((), ())), preferred_element_type=F32)


def nt(a, b):
    return lax.dot_general(a, b, (((1,), (1,)), ((), ())), preferred_element_type=F32)


def unit_of(values):
    center = values - jnp.mean(values, axis=-1, keepdims=True)
    rstd = lax.rsqrt(jnp.mean(center * center, axis=-1, keepdims=True) + EPS)
    return center * rstd, rstd


def norm_back(grad, unit, rstd, gain):
    scaled = grad * gain
    return rstd * (
        scaled
        - jnp.mean(scaled, axis=-1, keepdims=True)
        - unit * jnp.mean(scaled * unit, axis=-1, keepdims=True)
    )


def fold8(values):
    rows = values.shape[0]
    return jnp.sum(values.reshape(rows // 8, 8, values.shape[1]), axis=0)


def gelu_pair(x):
    e = jnp.exp(x * x * -0.5)
    t = 1.0 / (1.0 + (0.3275911 * 0.7071067811865476) * jnp.abs(x))
    poly = 1.061405429 * 0.5
    poly = poly * t + (-1.453152027 * 0.5)
    poly = poly * t + (1.421413741 * 0.5)
    poly = poly * t + (-0.284496736 * 0.5)
    poly = poly * t + (0.254829592 * 0.5)
    half = poly * t * e
    cdf = jnp.where(x < 0.0, half, 1.0 - half)
    return x * cdf, cdf + x * (e * 0.3989422804014327)


MESH = pl.DeviceIdType.MESH


class Place:
    def __init__(self, mesh_shape):
        self.n, self.m = mesh_shape["ctx"], mesh_shape["fsdp"]
        self.inner = 2
        self.line = self.m // 2
        self.c, self.f = lax.axis_index("ctx"), lax.axis_index("fsdp")
        self.core = self.c % 2
        self.z, self.y = self.f // 2, self.f % 2

    def mate(self):
        return {"ctx": self.c + 1 - 2 * self.core, "fsdp": self.f}

    def across(self):
        return {"ctx": self.c, "fsdp": self.z * 2 + 1 - self.y}

    def along(self, step):
        return {"ctx": self.c, "fsdp": self.f + 2 * step}

    def greet(self, barrier, mate=True, grid=True, ctx=False):
        signal = lambda where: pl.semaphore_signal(barrier, inc=1, device_id=where, device_id_type=MESH)
        count = 0
        if ctx:
            for k in range(1, self.n):
                signal({"ctx": (self.c + k) % self.n, "fsdp": self.f})
            count = self.n - 1
        elif mate:
            signal(self.mate())
            count = 1
        if grid:
            signal(self.across())
            up = self.z < self.line - 1
            down = self.z > 0

            @pl.when(up)
            def _():
                signal(self.along(1))

            @pl.when(down)
            def _():
                signal(self.along(-1))

            count = count + 1 + up.astype(jnp.int32) + down.astype(jnp.int32)
        pl.semaphore_wait(barrier, count)


def remote(src, dst, send, recv, where):
    return pltpu.make_async_remote_copy(
        src_ref=src, dst_ref=dst, send_sem=send, recv_sem=recv, device_id=where, device_id_type=MESH
    )


class Gather:
    def __init__(self, place, shard, full, sems, channel):
        self.p, self.shard, self.full = place, shard, full
        self.send, self.recv, self.local = sems
        self.ch = channel

    def piece(self, j, y, core):
        return self.full.at[j * 2 + y, core]

    def line_copy(self, kind, j, source=None):
        p = self.p
        here = self.piece(j, p.y, p.core)
        return remote(
            here if source is None else source, here, self.send.at[self.ch, kind, j], self.recv.at[self.ch, kind, j],
            p.along(1 if kind == 0 else -1),
        )

    def across_copy(self, j, y, source=None):
        p = self.p
        here = self.piece(j, y, p.core)
        return remote(
            here if source is None else source, here, self.send.at[self.ch, 2, j], self.recv.at[self.ch, 2, j], p.across()
        )

    def mate_copy(self, j, y, core):
        p = self.p
        here = self.piece(j, y, core)
        slot = 3 + (y != p.y).astype(jnp.int32)
        return remote(here, here, self.send.at[self.ch, slot, j], self.recv.at[self.ch, slot, j], p.mate())

    def own(self):
        return pltpu.make_async_copy(self.shard, self.full.at[self.p.f], self.local.at[self.ch])

    def step(self, k):
        p, line = self.p, self.p.line
        z, y, core = p.z, p.y, p.core
        if k == 0:
            self.own().start()
            source = self.shard.at[core]

            @pl.when(z < line - 1)
            def _():
                self.line_copy(0, z, source).start()

            @pl.when(z > 0)
            def _():
                self.line_copy(1, z, source).start()

            self.across_copy(z, y, source).start()
            return
        if k < line:

            @pl.when(z >= k)
            def _():
                j = z - k
                self.line_copy(0, j).wait_recv()

                @pl.when(z < line - 1)
                def _():
                    self.line_copy(0, j).start()

                self.across_copy(j, y).start()
                self.mate_copy(j, y, core).start()

            @pl.when(z + k < line)
            def _():
                j = z + k
                self.line_copy(1, j).wait_recv()

                @pl.when(z > 0)
                def _():
                    self.line_copy(1, j).start()

                self.across_copy(j, y).start()
                self.mate_copy(j, y, core).start()

        far = k - 1
        other = 1 - y

        def landed(j):
            self.across_copy(j, other).wait_recv()
            self.mate_copy(j, other, core).start()

        if far == 0:
            landed(z)
        elif far < line:

            @pl.when(z >= far)
            def _():
                landed(z - far)

            @pl.when(z + far < line)
            def _():
                landed(z + far)

    def steps(self):
        return self.p.line + 1

    def finish(self):
        p, line = self.p, self.p.line
        z, y = p.z, p.y
        mate_core = 1 - p.core
        self.own().wait()
        for j in range(line):

            @pl.when(j != z)
            def _():
                self.mate_copy(j, y, mate_core).wait_recv()
                self.mate_copy(j, y, p.core).wait_send()

            self.mate_copy(j, 1 - y, mate_core).wait_recv()
            self.mate_copy(j, 1 - y, p.core).wait_send()
            self.across_copy(j, y).wait_send()

            @pl.when((j <= z) & (z < line - 1))
            def _():
                self.line_copy(0, j).wait_send()

            @pl.when((j >= z) & (z > 0))
            def _():
                self.line_copy(1, j).wait_send()


def gather_sems(place_line, channels):
    return [
        pltpu.SemaphoreType.DMA((channels, 5, place_line)),
        pltpu.SemaphoreType.DMA((channels, 5, place_line)),
        pltpu.SemaphoreType.DMA((channels,)),
    ]


class Reduce:
    def __init__(self, place, term, mine, out, bufs, sems, channel, line_first):
        self.p, self.term, self.mine, self.out = place, term, mine, out
        self.one, self.two, self.up, self.down, self.parts = bufs
        self.send, self.recv = sems
        self.ch, self.line_first = channel, line_first

    def copy(self, src, dst, slot, where):
        return remote(src, dst, self.send.at[self.ch, slot], self.recv.at[self.ch, slot], where)

    def mate_copy(self):
        p = self.p
        return self.copy(self.term.at[:, :, 1 - p.core], self.one, 0, p.mate())

    def mine_copy(self):
        return pltpu.make_async_copy(self.term.at[:, :, self.p.core], self.mine, self.send.at[self.ch, 2])

    def across_copy(self):
        p = self.p
        if self.line_first:
            return self.copy(self.one.at[p.z, 1 - p.y], self.two, 1, p.across())
        return self.copy(self.one.at[:, 1 - p.y], self.two, 1, p.across())

    def running(self):
        return self.one if self.line_first else self.two

    def up_copy(self, j):
        return self.copy(self.running().at[j], self.up.at[j], 4 + j, self.p.along(1))

    def down_copy(self, j):
        return self.copy(self.running().at[j], self.down.at[j], 4 + self.p.line + j, self.p.along(-1))

    def ctx_copy(self, k):
        p = self.p
        where = {"ctx": (p.c + 2 * k) % p.n, "fsdp": p.f}
        mine = self.parts.at[p.c // 2]
        return self.copy(mine, mine, 4 + 2 * p.line + k, where)

    def last_copy(self):
        p = self.p
        return self.copy(self.out.at[p.core], self.out.at[p.core], 3, p.mate())

    def step0(self):
        self.mate_copy().start()
        self.mine_copy().start()

    def step1(self):
        p = self.p
        self.mine_copy().wait()
        self.mate_copy().wait_recv()

        def add(i, carry):
            for y in range(2):
                self.one[i, y] = (self.one[i, y].astype(F32) + self.mine[i, y].astype(F32)).astype(BF16)
            return carry

        lax.fori_loop(0, p.line, add, 0)
        if self.line_first:
            self.line_start()
        else:
            self.across_copy().start()

    def line_start(self):
        p = self.p

        @pl.when(p.z == 0)
        def _():
            for j in range(p.line - 1, 0, -1):
                self.up_copy(j).start()

        @pl.when(p.z == p.line - 1)
        def _():
            for j in range(0, p.line - 1):
                self.down_copy(j).start()

    def line_step(self, d):
        p = self.p
        running = self.running()
        for sign, move, buf in ((1, self.up_copy, self.up), (-1, self.down_copy, self.down)):
            j = p.z + sign * d
            valid = (j < p.line) & (p.z > 0) if sign > 0 else (j >= 0) & (p.z < p.line - 1)

            @pl.when(valid)
            def _():
                move(j).wait_recv()
                running[j] = (running[j].astype(F32) + buf[j].astype(F32)).astype(BF16)
                if d > 0:
                    move(j).start()

    def step2(self):
        p = self.p
        if self.line_first:
            for d in range(p.line - 1, 0, -1):
                self.line_step(d)
            return
        self.across_copy().wait_recv()

        def add(i, carry):
            self.two[i] = (self.two[i].astype(F32) + self.one[i, p.y].astype(F32)).astype(BF16)
            return carry

        lax.fori_loop(0, p.line, add, 0)
        self.line_start()

    def step3(self):
        p = self.p
        if self.line_first:
            self.line_step(0)
            self.across_copy().start()
            return
        for d in range(p.line - 1, 0, -1):
            self.line_step(d)

    def step4(self):
        p = self.p
        if self.line_first:
            self.across_copy().wait_recv()
            self.parts[p.c // 2] = (self.two[...].astype(F32) + self.one[p.z, p.y].astype(F32)).astype(BF16)
        else:
            self.line_step(0)
            self.parts[p.c // 2] = self.two[p.z]
        for k in range(1, p.n // 2):
            self.ctx_copy(k).start()

    def step5(self):
        p = self.p
        for k in range(1, p.n // 2):
            self.ctx_copy(k).wait_recv()
        total = self.parts[0].astype(F32)
        for c in range(1, p.n // 2):
            total = total + self.parts[c].astype(F32)
        self.out[p.core] = total.astype(BF16)
        self.last_copy().start()

    def finish(self):
        p = self.p
        self.last_copy_in().wait_recv()
        self.last_copy().wait_send()
        self.mate_copy().wait_send()
        self.across_copy().wait_send()
        for j in range(p.line):

            @pl.when(j > p.z)
            def _():
                self.up_copy(j).wait_send()

            @pl.when(j < p.z)
            def _():
                self.down_copy(j).wait_send()

        for k in range(1, p.n // 2):
            self.ctx_copy(k).wait_send()

    def last_copy_in(self):
        p = self.p
        return self.copy(self.out.at[1 - p.core], self.out.at[1 - p.core], 3, p.mate())


def reduce_scratch(shape, h, w, line_first):
    line, n = shape["fsdp"] // 2, shape["ctx"]
    run = (line, 2, h, w) if line_first else (line, h, w)
    return [
        pltpu.VMEM((line, 2, h, w), BF16),
        pltpu.VMEM((line, 2, h, w), BF16),
        pltpu.VMEM((h, w) if line_first else (line, h, w), BF16),
        pltpu.VMEM(run, BF16),
        pltpu.VMEM(run, BF16),
        pltpu.VMEM((n // 2, h, w), BF16),
    ]


def reduce_sems(shape, channels):
    slots = 4 + shape["fsdp"] + shape["ctx"] // 2
    return [pltpu.SemaphoreType.DMA((channels, slots))] * 2


def halves(pair):
    low = lax.broadcasted_iota(jnp.int32, pair.shape, 1) < 64
    zero = jnp.zeros_like(pair)
    return jnp.concatenate([jnp.where(low, pair, zero), jnp.where(low, zero, pair)], axis=0)


def corner(both):
    return jnp.concatenate([both[0:64, 0:SPAN], both[64:128, SPAN : 2 * SPAN]], axis=0)


def turn(value):
    return value.astype(F32).T.astype(BF16)


def slots(items, places):
    count = -(-len(items) // places)
    return [items[i * count : (i + 1) * count] for i in range(places)]


def front_kernel(shape, *refs):
    shards, x_hbm = refs[0:5], refs[5]
    wq_out, wo_out, wu_out, wd_out, norms_ref, mixed_out, pn_out, pf_out, att_out, attt_out, far_ref = refs[6:17]
    (x_ref, wq_ref, raw_ref, mixed_ref, pn_ref, pf_ref, att_ref, attt_ref, own_ref, all_ref, fart_ref,
     gsend, grecv, glocal, ssend, srecv, io_sem) = refs[17:]
    batches, tokens, _ = x_ref.shape
    spans = tokens // SPAN
    count = far_ref.shape[1]
    prompt = count // 2
    m = shape["fsdp"]
    width = D // m
    place = Place(shape)
    first = place.c * spans

    load = [pltpu.make_async_copy(x_hbm.at[b], x_ref.at[b], io_sem.at[0, b]) for b in range(batches)]
    for copy in load:
        copy.start()
    place.greet(pltpu.get_barrier_semaphore(), ctx=True)
    sems = (gsend, grecv, glocal)
    fulls = (wq_ref, raw_ref, wo_out, wu_out, wd_out)
    parts = [Gather(place, s, f, sems, i) for i, (s, f) in enumerate(zip(shards, fulls))]
    soon, later = parts[0:2], parts[2:]
    steps = parts[0].steps()
    for k in range(steps):
        for part in soon:
            part.step(k)
    for part in soon:
        part.finish()
    for part in later:
        part.step(0)
    plan = slots([(k, part) for k in range(1, steps) for part in later], 2 * batches)

    def advance(slot):
        for k, part in plan[slot]:
            part.step(k)

    for f in range(m):
        norms_ref[0:4, f * width : (f + 1) * width] = raw_ref[f, 0, 0:4, 0:width]
    weight_out = pltpu.make_async_copy(wq_ref, wq_out, io_sem.at[1, 0])
    weight_out.start()
    gain = norms_ref[0:1, :]
    shift = norms_ref[2:3, :]
    tile = 256

    def share(b, k):
        to = (place.c + k) % place.n
        return remote(
            own_ref.at[b], all_ref.at[b, place.c], ssend.at[b, k], srecv.at[b, k], {"ctx": to, "fsdp": place.f}
        )

    def mixed_copy(b):
        return pltpu.make_async_copy(mixed_ref.at[b], mixed_out.at[b], io_sem.at[2, b])

    for b in range(batches):
        load[b].wait()

        def project(i, carry, b=b):
            rows = pl.ds(pl.multiple_of(i * tile, tile), tile)
            unit, _ = unit_of(x_ref[b, rows, :].astype(F32))
            low = (unit * gain + shift).astype(BF16)
            weight = lambda c: wq_ref[:, :, :, c * D : (c + 1) * D].reshape(D, D)
            mixed_ref[b, rows, 0:D] = (nn(low, weight(0)).astype(BF16).astype(F32) * 0.125).astype(BF16)
            for c in range(1, 3):
                part = nn(low, weight(c))
                mixed_ref[b, rows, c * D : (c + 1) * D] = part.astype(BF16)
                for s in range(tile // SPAN):
                    total = jnp.sum(part[s * SPAN : (s + 1) * SPAN, :], axis=0, keepdims=True) * SPAN ** (-0.5)
                    own_ref[b, pl.ds(i * (tile // SPAN) + s, 1), (c - 1) * D : c * D] = total.astype(BF16).astype(F32)
            return carry

        lax.fori_loop(0, tokens // tile, project, 0)
        for k in range(1, place.n):
            share(b, k).start()
        all_ref[b, place.c] = own_ref[b]
        mixed_copy(b).start()
        advance(b)

    out_copies = lambda b: [
        pltpu.make_async_copy(src.at[b], dst.at[b], io_sem.at[3 + i, b])
        for i, (src, dst) in enumerate(((pn_ref, pn_out), (pf_ref, pf_out), (att_ref, att_out), (attt_ref, attt_out)))
    ]

    for b in range(batches):
        for k in range(1, place.n):
            share(b, k).wait()
        far_ref[b] = all_ref[b].reshape(count, 2 * D).astype(BF16)
        fart_ref[...] = all_ref[b].reshape(count, 2 * D).T.astype(BF16)

        def attend(j, carry, b=b):
            rows = pl.ds(pl.multiple_of(j * SPAN, SPAN), SPAN)
            key_id = lax.broadcasted_iota(jnp.int32, (SPAN, 2 * SPAN), 0)
            query_id = lax.broadcasted_iota(jnp.int32, (SPAN, 2 * SPAN), 1) & (SPAN - 1)
            causal = key_id <= query_id
            far_id = lax.broadcasted_iota(jnp.int32, (count, 2 * SPAN), 0)
            mine = first + j
            segment = (mine - prompt) >> 3
            seen = (far_id < mine) & ((far_id < prompt) | (((far_id - prompt) >> 3) == segment))
            for p in range(PAIRS):
                lanes = slice(p * SPAN, (p + 1) * SPAN)
                qs = halves(mixed_ref[b, rows, lanes])
                k = mixed_ref[b, rows, D + p * SPAN : D + (p + 1) * SPAN]
                v = mixed_ref[b, rows, 2 * D + p * SPAN : 2 * D + (p + 1) * SPAN]
                near = jnp.where(causal, nt(k, qs), NEG)
                far = jnp.where(seen, nt(far_ref[b, :, lanes], qs), NEG)
                peak = jnp.maximum(jnp.max(near, axis=0, keepdims=True), jnp.max(far, axis=0, keepdims=True))
                near = jnp.exp(near - peak)
                far = jnp.exp(far - peak)
                inv = 1.0 / (jnp.sum(near, axis=0, keepdims=True) + jnp.sum(far, axis=0, keepdims=True))
                near = (near * inv).astype(BF16)
                far = (far * inv).astype(BF16)
                pn_ref[b, j, p] = near
                pf_ref[b, j, p] = far
                both = nn(turn(v), near) + nn(fart_ref[D + p * SPAN : D + (p + 1) * SPAN, :], far)
                att = corner(both)
                attt_ref[b, lanes, rows] = att.astype(BF16)
                att_ref[b, rows, lanes] = att.T.astype(BF16)
            return carry

        lax.fori_loop(0, spans, attend, 0)
        for copy in out_copies(b):
            copy.start()
        advance(batches + b)

    for part in later:
        part.finish()
    weight_out.wait()
    for b in range(batches):
        mixed_copy(b).wait()
        for copy in out_copies(b):
            copy.wait()


def front_call(shape, shards, x):
    batches, tokens, _ = x.shape
    spans = tokens // SPAN
    n, m = shape["ctx"], shape["fsdp"]
    count = n * spans
    any_spec = pl.BlockSpec(memory_space=pl.ANY)
    vmem = pl.BlockSpec(memory_space=pltpu.VMEM)
    full = [jax.ShapeDtypeStruct((m,) + s.shape, s.dtype) for s in shards]
    big = [
        jax.ShapeDtypeStruct((batches, tokens, 3 * D), BF16),
        jax.ShapeDtypeStruct((batches, spans, PAIRS, SPAN, 2 * SPAN), BF16),
        jax.ShapeDtypeStruct((batches, spans, PAIRS, count, 2 * SPAN), BF16),
        jax.ShapeDtypeStruct((batches, tokens, D), BF16),
        jax.ShapeDtypeStruct((batches, D, tokens), BF16),
    ]
    return pl.pallas_call(
        functools.partial(front_kernel, shape),
        in_specs=[any_spec] * 6,
        out_specs=[any_spec] * 4 + [vmem] + [any_spec] * 5 + [vmem],
        out_shape=[full[0], full[2], full[3], full[4], jax.ShapeDtypeStruct((8, D), F32)]
        + big
        + [jax.ShapeDtypeStruct((batches, count, 2 * D), BF16)],
        scratch_shapes=[
            pltpu.VMEM((batches, tokens, D), BF16),
            pltpu.VMEM(full[0].shape, BF16),
            pltpu.VMEM(full[1].shape, F32),
        ]
        + [pltpu.VMEM(v.shape, v.dtype) for v in big]
        + [
            pltpu.VMEM((batches, spans, 2 * D), F32),
            pltpu.VMEM((batches, n, spans, 2 * D), F32),
            pltpu.VMEM((2 * D, count), BF16),
        ]
        + gather_sems(m // 2, 5)
        + [
            pltpu.SemaphoreType.DMA((batches, n)),
            pltpu.SemaphoreType.DMA((batches, n)),
            pltpu.SemaphoreType.DMA((7, batches)),
        ],
        compiler_params=pltpu.CompilerParams(collective_id=0, has_side_effects=True, vmem_limit_bytes=VMEM_LIMIT),
        name="front",
    )(*shards, x)


def middle_kernel(
    x_ref, g_ref, att_ref, attt_ref, wo_ref, wu_ref, wd_ref, norms_ref,
    out_ref, gmid_ref, da_ref, go_ref, gu_ref, gd_ref, ggain_ref, gshift_ref,
    n2t_ref, gt_ref, act_ref, gh_ref, goa_ref, gua_ref, gda_ref,
):
    tokens = x_ref.shape[1]

    @pl.when(pl.program_id(0) == 0)
    def _():
        goa_ref[...] = jnp.zeros_like(goa_ref)
        gua_ref[...] = jnp.zeros_like(gua_ref)
        gda_ref[...] = jnp.zeros_like(gda_ref)
        ggain_ref[...] = jnp.zeros_like(ggain_ref)
        gshift_ref[...] = jnp.zeros_like(gshift_ref)

    tile = 256
    gain = norms_ref[1:2, :]
    shift = norms_ref[3:4, :]

    def mlp(i, carry):
        rows = pl.ds(pl.multiple_of(i * tile, tile), tile)
        middle = x_ref[0, rows, :].astype(F32) + nn(att_ref[0, rows, :], wo_ref[...])
        unit, rstd = unit_of(middle)
        low = unit * gain + shift
        n2t_ref[:, rows] = low.T.astype(BF16)
        low = low.astype(BF16)
        g = g_ref[0, rows, :]
        gt_ref[:, rows] = turn(g)
        for c in range(4):
            cols = slice(c * 512, (c + 1) * 512)
            act, slope = gelu_pair(nn(low, wu_ref[:, cols]))
            act_ref[rows, cols] = act.astype(BF16)
            gh_ref[rows, cols] = (nt(g, wd_ref[cols, :]) * slope).astype(BF16)
        out_ref[0, rows, :] = (middle + nn(act_ref[rows, :], wd_ref[...])).astype(BF16)
        grad = nt(gh_ref[rows, :], wu_ref[...])
        ggain_ref[...] += fold8(grad * unit)
        gshift_ref[...] += fold8(grad)
        grad = g.astype(F32) + norm_back(grad, unit, rstd, gain)
        low = grad.astype(BF16)
        gmid_ref[0, rows, :] = low
        da_ref[0, rows, :] = nt(low, wo_ref[...]).astype(BF16)
        return carry

    lax.fori_loop(0, tokens // tile, mlp, 0)

    goa_ref[...] += nn(attt_ref[0], gmid_ref[0])

    def wgrad(c, carry):
        cols = pl.ds(pl.multiple_of(c * 512, 512), 512)
        gua_ref[:, cols] += nn(n2t_ref[...], gh_ref[:, cols])
        gda_ref[:, cols] += nn(gt_ref[...], act_ref[:, cols])
        return carry

    lax.fori_loop(0, 4, wgrad, 0)

    @pl.when(pl.program_id(0) == pl.num_programs(0) - 1)
    def _():
        go_ref[...] = goa_ref[...].astype(BF16)

        def close(c, carry):
            cols = pl.ds(pl.multiple_of(c * 512, 512), 512)
            gu_ref[:, cols] = gua_ref[:, cols].astype(BF16)
            gd_ref[cols, :] = gda_ref[:, cols].T.astype(BF16)
            return carry

        lax.fori_loop(0, 4, close, 0)


def middle_call(x, g, att, attt, wo, wu, wd, norms):
    batches, tokens, _ = x.shape
    one = pl.Buffered(1)
    seq = lambda *dims: pl.BlockSpec((1,) + dims, lambda b: (b, 0, 0))
    whole = lambda *shape: pl.BlockSpec(shape, lambda b: (0,) * len(shape), pipeline_mode=one)
    return pl.pallas_call(
        middle_kernel,
        grid=(batches,),
        in_specs=[
            seq(tokens, D), seq(tokens, D), seq(tokens, D), seq(D, tokens),
            whole(D, D), whole(D, FF), whole(FF, D), whole(8, D),
        ],
        out_specs=[
            seq(tokens, D), seq(tokens, D), seq(tokens, D),
            whole(D, D), whole(D, FF), whole(FF, D), whole(8, D), whole(8, D),
        ],
        out_shape=[
            jax.ShapeDtypeStruct((batches, tokens, D), BF16),
            jax.ShapeDtypeStruct((batches, tokens, D), BF16),
            jax.ShapeDtypeStruct((batches, tokens, D), BF16),
            jax.ShapeDtypeStruct((D, D), BF16),
            jax.ShapeDtypeStruct((D, FF), BF16),
            jax.ShapeDtypeStruct((FF, D), BF16),
            jax.ShapeDtypeStruct((8, D), F32),
            jax.ShapeDtypeStruct((8, D), F32),
        ],
        scratch_shapes=[
            pltpu.VMEM((D, tokens), BF16),
            pltpu.VMEM((D, tokens), BF16),
            pltpu.VMEM((tokens, FF), BF16),
            pltpu.VMEM((tokens, FF), BF16),
            pltpu.VMEM((D, D), F32),
            pltpu.VMEM((D, FF), F32),
            pltpu.VMEM((D, FF), F32),
        ],
        compiler_params=pltpu.CompilerParams(vmem_limit_bytes=VMEM_LIMIT),
        name="middle",
    )(x, g, att, attt, wo, wu, wd, norms)


def back_kernel(shape, *refs):
    mixed_hbm, da_hbm, pn_hbm, pf_hbm, x_hbm, gmid_hbm, wq_hbm, gu_hbm, gd_hbm, go_hbm = refs[0:10]
    far_ref, norms_ref, gain2_ref, shift2_ref = refs[10:14]
    gin_out, gq_out, gu_out, gd_out, go_out, small_out = refs[14:20]
    (mixed_ref, da_ref, pn_ref, pf_ref, x_ref, gmid_ref, wq_ref, dmixed_ref, nt_ref, gw_ref, gq_ref, small_ref, gin_ref,
     far_t, dfar_ref, held_ref, gsum_ref) = refs[20:37]
    bufs, sems = refs[37:67], refs[67:69]
    xsend, xrecv, io_sem = refs[69:72]
    batches, tokens, _ = x_ref.shape
    spans = tokens // SPAN
    count = far_ref.shape[1]
    m = shape["fsdp"]
    width = D // m
    place = Place(shape)

    ins = lambda b: [
        pltpu.make_async_copy(src.at[b], dst.at[b % 2], io_sem.at[i, b])
        for i, (src, dst) in enumerate(((mixed_hbm, mixed_ref), (da_hbm, da_ref), (pn_hbm, pn_ref), (pf_hbm, pf_ref)))
    ]
    rest = [
        pltpu.make_async_copy(src, dst, io_sem.at[4 + i, 0])
        for i, (src, dst) in enumerate(((x_hbm, x_ref), (gmid_hbm, gmid_ref), (wq_hbm, wq_ref)))
    ]
    for copy in ins(0):
        copy.start()
    place.greet(pltpu.get_barrier_semaphore(), ctx=True)
    big = [
        Reduce(place, t, bufs[6 * i], o, bufs[6 * i + 1 : 6 * i + 6], sems, i, lf)
        for i, (t, o, lf) in enumerate(((gu_hbm, gu_out, False), (gd_hbm, gd_out, True), (go_hbm, go_out, False)))
    ]
    tail = [
        Reduce(place, t, bufs[6 * i], o, bufs[6 * i + 1 : 6 * i + 6], sems, i, lf)
        for i, (t, o, lf) in ((3, (gq_ref, gq_out, False)), (4, (small_ref, small_out, False)))
    ]
    for part in big:
        part.step0()
    for copy in rest:
        copy.start()

    def swap(b, k):
        to = (place.c + k) % place.n
        source = dfar_ref.at[b, pl.ds(pl.multiple_of(to * spans, spans), spans)]
        return remote(source, held_ref.at[b, k], xsend.at[b, k], xrecv.at[b, k], {"ctx": to, "fsdp": place.f})

    for b in range(batches):
        slot = b % 2
        for copy in ins(b):
            copy.wait()
        if b + 1 < batches:
            for copy in ins(b + 1):
                copy.start()
        dfar_ref[b] = jnp.zeros((count, 2 * D), F32)
        far_t[...] = turn(far_ref[b, :, 0:D])

        def attend_back(j, carry, b=b, slot=slot):
            rows = pl.ds(pl.multiple_of(j * SPAN, SPAN), SPAN)
            for p in range(PAIRS):
                lanes = slice(p * SPAN, (p + 1) * SPAN)
                klanes = slice(D + p * SPAN, D + (p + 1) * SPAN)
                vlanes = slice(2 * D + p * SPAN, 2 * D + (p + 1) * SPAN)
                qs = halves(mixed_ref[slot, rows, lanes])
                k = mixed_ref[slot, rows, klanes]
                v = mixed_ref[slot, rows, vlanes]
                das = halves(da_ref[slot, rows, lanes])
                near_low = pn_ref[slot, j, p]
                far_low = pf_ref[slot, j, p]
                near = near_low.astype(F32)
                far = far_low.astype(F32)
                slope_near = nt(v, das)
                slope_far = nt(far_ref[b, :, klanes], das)
                inner = jnp.sum(near * slope_near, axis=0, keepdims=True)
                inner = inner + jnp.sum(far * slope_far, axis=0, keepdims=True)
                near = (near * (slope_near - inner)).astype(BF16)
                far = (far * (slope_far - inner)).astype(BF16)
                dmixed_ref[b, rows, vlanes] = nn(near_low, das).astype(BF16)
                dmixed_ref[b, rows, klanes] = nn(near, qs).astype(BF16)
                dfar_ref[b, :, klanes] += nn(far_low, das)
                dfar_ref[b, :, lanes] += nn(far, qs)
                both = nn(turn(k), near) + nn(far_t[lanes, :], far)
                dmixed_ref[b, rows, lanes] = (corner(both).T * 0.125).astype(BF16)
            return carry

        lax.fori_loop(0, spans, attend_back, 0)
        for k in range(1, place.n):
            swap(b, k).start()
        for part in big:
            getattr(part, ("step1", "step2", "step3")[b] if b < 3 else "idle")()

    for copy in rest:
        copy.wait()
    gain = norms_ref[0:1, :]
    shift = norms_ref[2:3, :]
    tile = 256

    for b in range(batches):
        for k in range(1, place.n):
            swap(b, k).wait()
        total = dfar_ref[b, pl.ds(pl.multiple_of(place.c * spans, spans), spans), :]
        for k in range(1, place.n):
            total = total + held_ref[b, k]
        gsum_ref[...] = total * SPAN ** (-0.5)

        def spread(i, carry, b=b):
            rows = pl.ds(pl.multiple_of(i * tile, tile), tile)
            unit, _ = unit_of(x_ref[b, rows, :].astype(F32))
            nt_ref[:, rows] = (unit * gain + shift).T.astype(BF16)
            for s in range(tile // SPAN):
                srows = pl.ds(pl.multiple_of(i * tile + s * SPAN, SPAN), SPAN)
                extra = gsum_ref[pl.ds(i * (tile // SPAN) + s, 1), :]
                dmixed_ref[b, srows, D:] = (dmixed_ref[b, srows, D:].astype(F32) + extra).astype(BF16)
            return carry

        lax.fori_loop(0, tokens // tile, spread, 0)

        def wgrad(c, carry, b=b):
            cols = pl.ds(pl.multiple_of(c * 512, 512), 512)
            part = nn(nt_ref[...], dmixed_ref[b, :, cols])
            gw_ref[:, cols] = part if b == 0 else gw_ref[:, cols] + part
            return carry

        lax.fori_loop(0, 3, wgrad, 0)
        if b == 0:
            for part in big:
                part.step4()
        if b == 1:
            for part in big:
                part.step5()

    line = m // 2
    half = D // m // 2

    def low(i, carry):
        for y in range(2):
            for s in range(2):
                start = pl.multiple_of(((i * 2 + y) * 2 + s) * half, half)
                gq_ref[i, y, s] = gw_ref[pl.ds(start, half), :].astype(BF16)
        return carry

    lax.fori_loop(0, line, low, 0)
    tail[0].step0()

    gin_copy = lambda b: pltpu.make_async_copy(gin_ref.at[b], gin_out.at[b], io_sem.at[7, b])
    gains_at = jnp.zeros((8, D), F32)
    shifts_at = jnp.zeros((8, D), F32)
    for b in range(batches):

        def data(i, carry, b=b):
            rows = pl.ds(pl.multiple_of(i * tile, tile), tile)
            unit, rstd = unit_of(x_ref[b, rows, :].astype(F32))
            grad = nt(dmixed_ref[b, rows, :], wq_ref[...].reshape(D, 3 * D))
            gin_ref[b, rows, :] = (gmid_ref[b, rows, :].astype(F32) + norm_back(grad, unit, rstd, gain)).astype(BF16)
            return carry[0] + fold8(grad * unit), carry[1] + fold8(grad)

        gains_at, shifts_at = lax.fori_loop(0, tokens // tile, data, (gains_at, shifts_at))
        gin_copy(b).start()
        getattr(tail[0], ("step1", "step2", "step3")[b])()

    sums = [jnp.sum(v, axis=0, keepdims=True) for v in (gains_at, gain2_ref[...], shifts_at, shift2_ref[...])]
    sums = jnp.concatenate(sums + [jnp.zeros((4, D), F32)], axis=0)
    small_ref[...] = jnp.zeros_like(small_ref)
    for f in range(m):
        small_ref[f // 2, f % 2, 0, :, 0:width] = sums[:, f * width : (f + 1) * width].astype(BF16)
    tail[1].step0()
    tail[0].step4()
    for name in ("step1", "step2", "step3", "step4", "step5"):
        getattr(tail[1], name)()
    tail[0].step5()
    for part in big + tail:
        part.finish()
    for b in range(batches):
        gin_copy(b).wait()


def back_call(shape, mixed, da, pn, pf, x, gmid, wq, gu, gd, go, far, norms, gain2, shift2):
    batches, tokens, _ = x.shape
    spans = tokens // SPAN
    n, m = shape["ctx"], shape["fsdp"]
    line = m // 2
    count = n * spans
    any_spec = pl.BlockSpec(memory_space=pl.ANY)
    vmem = pl.BlockSpec(memory_space=pltpu.VMEM)
    halved = lambda rows, w: (line, 2, 2, rows // (2 * m), w)
    terms = [halved(D, FF), halved(FF, D), halved(D, D), halved(D, 3 * D), (line, 2, 2, 8, 128)]
    gu, gd, go = (v.reshape(t) for v, t in zip((gu, gd, go), terms))
    out = lambda t: jax.ShapeDtypeStruct(t[2:], BF16)
    two = lambda *dims: pltpu.VMEM((2,) + dims, BF16)
    scratch = [
        two(tokens, 3 * D), two(tokens, D), two(spans, PAIRS, SPAN, 2 * SPAN), two(spans, PAIRS, count, 2 * SPAN),
        pltpu.VMEM(x.shape, BF16), pltpu.VMEM(x.shape, BF16), pltpu.VMEM(wq.shape, BF16),
        pltpu.VMEM((batches, tokens, 3 * D), BF16), pltpu.VMEM((D, tokens), BF16), pltpu.VMEM((D, 3 * D), F32),
        pltpu.VMEM(terms[3], BF16), pltpu.VMEM(terms[4], BF16), pltpu.VMEM(x.shape, BF16),
        pltpu.VMEM((D, count), BF16), pltpu.VMEM((batches, count, 2 * D), F32),
        pltpu.VMEM((batches, n, spans, 2 * D), F32), pltpu.VMEM((spans, 2 * D), F32),
    ]
    for t, line_first in zip(terms, (False, True, False, False, False)):
        scratch += reduce_scratch(shape, *t[3:], line_first)
    scratch += reduce_sems(shape, 5)
    scratch += [
        pltpu.SemaphoreType.DMA((batches, n)), pltpu.SemaphoreType.DMA((batches, n)), pltpu.SemaphoreType.DMA((8, batches))
    ]
    return pl.pallas_call(
        functools.partial(back_kernel, shape),
        in_specs=[any_spec] * 10 + [vmem] * 4,
        out_specs=[any_spec] + [vmem] * 5,
        out_shape=[
            jax.ShapeDtypeStruct(x.shape, BF16), out(terms[3]), out(terms[0]), out(terms[1]), out(terms[2]), out(terms[4]),
        ],
        scratch_shapes=scratch,
        compiler_params=pltpu.CompilerParams(collective_id=1, has_side_effects=True, vmem_limit_bytes=VMEM_LIMIT),
        name="back",
    )(mixed, da, pn, pf, x, gmid, wq, gu, gd, go, far, norms, gain2, shift2)


def widen_kernel(*refs):
    half = len(refs) // 2
    for src, dst in zip(refs[:half], refs[half:]):
        dst[...] = src[...].astype(F32)


def widen_call(values):
    return pl.pallas_call(
        widen_kernel,
        out_shape=[jax.ShapeDtypeStruct(v.shape, F32) for v in values],
        name="widen",
    )(*values)


def local(shape, x, g, qkv_weight, out_weight, up_weight, down_weight, norm_gains, norm_shifts):
    width = norm_gains.shape[1]
    norms = jnp.concatenate([norm_gains, norm_shifts], axis=0).astype(F32)
    norms = jnp.pad(norms, ((0, 4), (0, 128 - width)))
    halved = lambda shard: shard.reshape(2, shard.shape[0] // 2, shard.shape[1])
    shards = [halved(v) for v in (qkv_weight, jnp.concatenate([norms, norms], axis=0), out_weight, up_weight, down_weight)]
    wq, wo, wu, wd, norms, mixed, pn, pf, att, attt, far = front_call(shape, shards, x)
    wo, wu, wd = (w.reshape(-1, w.shape[-1]) for w in (wo, wu, wd))
    out, gmid, da, go, gu, gd, gain2, shift2 = middle_call(x, g, att, attt, wo, wu, wd, norms)
    gin, gq, gu, gd, go, small = back_call(
        shape, mixed, da, pn, pf, x, gmid, wq, gu, gd, go, far, norms, gain2, shift2
    )
    gq, go, gu, gd, small = widen_call([v.reshape(-1, v.shape[-1]) for v in (gq, go, gu, gd, small)])
    small = small[0:4, 0:width]
    return out, gin, gq, go, gu, gd, small[0:2], small[2], small[3]


def solution(mesh):
    weight, norm, token = P("fsdp", None), P(None, "fsdp"), P("fsdp", "ctx", None)
    return jax.shard_map(
        functools.partial(local, dict(mesh.shape)),
        mesh=mesh,
        in_specs=(token, token, weight, weight, weight, weight, norm, norm),
        out_specs=(token, token, weight, weight, weight, weight, norm, P("fsdp"), P("fsdp")),
        check_vma=False,
    )
```

```python
import functools

import jax
import jax.numpy as jnp
from jax import lax
from jax.experimental import pallas as pl
from jax.experimental.pallas import tpu as pltpu
from jax.sharding import PartitionSpec as P

D = 512
HEADS = 8
FF = 2048
SPAN = 128
CONT = 1024
PAIRS = HEADS // 2
CHUNK = 1024
LEAD = 1
WAIT = 2
EXTRA = 3

EPS = 1e-05
NEG = -1e30
F32 = jnp.float32
BF16 = jnp.bfloat16
VMEM_LIMIT = 60 * 1024 * 1024


def nn(a, b):
    return lax.dot_general(a, b, (((1,), (0,)), ((), ())), preferred_element_type=F32)


def nt(a, b):
    return lax.dot_general(a, b, (((1,), (1,)), ((), ())), preferred_element_type=F32)


def unit_of(values):
    center = values - jnp.mean(values, axis=-1, keepdims=True)
    rstd = lax.rsqrt(jnp.mean(center * center, axis=-1, keepdims=True) + EPS)
    return center * rstd, rstd


def norm_back(grad, unit, rstd, gain):
    scaled = grad * gain
    return rstd * (
        scaled
        - jnp.mean(scaled, axis=-1, keepdims=True)
        - unit * jnp.mean(scaled * unit, axis=-1, keepdims=True)
    )


def fold8(values):
    rows = values.shape[0]
    return jnp.sum(values.reshape(rows // 8, 8, values.shape[1]), axis=0)


def gelu_pair(x):
    cdf = lax.erf(x * 0.7071067811865476) + 1.0
    slope = jnp.exp2(x * x * (-0.5 * 1.4426950408889634)) * (x * 0.7978845608028654)
    return x * cdf, cdf + slope


MESH = pl.DeviceIdType.MESH


class Place:
    def __init__(self, mesh_shape):
        self.n, self.m = mesh_shape["ctx"], mesh_shape["fsdp"]
        self.inner = 2
        self.line = self.m // 2
        self.c, self.f = lax.axis_index("ctx"), lax.axis_index("fsdp")
        self.core = self.c % 2
        self.z, self.y = self.f // 2, self.f % 2

    def mate(self):
        return {"ctx": self.c + 1 - 2 * self.core, "fsdp": self.f}

    def across(self):
        return {"ctx": self.c, "fsdp": self.z * 2 + 1 - self.y}

    def along(self, step):
        return {"ctx": self.c, "fsdp": self.f + 2 * step}

    def greet(self, barrier, rows=False):
        signal = lambda where: pl.semaphore_signal(barrier, inc=1, device_id=where, device_id_type=MESH)
        for k in range(1, self.n):
            signal({"ctx": (self.c + k) % self.n, "fsdp": self.f})
        count = self.n - 1
        if rows:
            for k in range(1, self.m):
                signal({"ctx": self.c, "fsdp": (self.f + k) % self.m})
            count = count + self.m - 1
        else:
            signal(self.across())
            up = self.z < self.line - 1
            down = self.z > 0

            @pl.when(up)
            def _():
                signal(self.along(1))

            @pl.when(down)
            def _():
                signal(self.along(-1))

            count = count + 1 + up.astype(jnp.int32) + down.astype(jnp.int32)
        pl.semaphore_wait(barrier, count)


def remote(src, dst, send, recv, where):
    return pltpu.make_async_remote_copy(
        src_ref=src, dst_ref=dst, send_sem=send, recv_sem=recv, device_id=where, device_id_type=MESH
    )


class Gather:
    def __init__(self, place, shard, full, sems, channel, cols=slice(None)):
        self.p, self.shard, self.full, self.cols = place, shard, full, cols
        self.send, self.recv, self.local = sems
        self.ch = channel

    def piece(self, j, y, core):
        return self.full.at[j * 2 + y, core, :, self.cols]

    def line_copy(self, kind, j, source=None):
        p = self.p
        here = self.piece(j, p.y, p.core)
        return remote(
            here if source is None else source, here, self.send.at[self.ch, kind, j], self.recv.at[self.ch, kind, j],
            p.along(1 if kind == 0 else -1),
        )

    def across_copy(self, j, y, source=None):
        p = self.p
        here = self.piece(j, y, p.core)
        return remote(
            here if source is None else source, here, self.send.at[self.ch, 2, j], self.recv.at[self.ch, 2, j], p.across()
        )

    def mate_copy(self, j, y, core):
        p = self.p
        here = self.piece(j, y, core)
        slot = 3 + (y != p.y).astype(jnp.int32)
        return remote(here, here, self.send.at[self.ch, slot, j], self.recv.at[self.ch, slot, j], p.mate())

    def own(self):
        return pltpu.make_async_copy(
            self.shard.at[:, :, self.cols], self.full.at[self.p.f, :, :, self.cols], self.local.at[self.ch]
        )

    def step(self, k):
        p, line = self.p, self.p.line
        z, y, core = p.z, p.y, p.core
        if k == 0:
            self.own().start()
            source = self.shard.at[core, :, self.cols]

            @pl.when(z < line - 1)
            def _():
                self.line_copy(0, z, source).start()

            @pl.when(z > 0)
            def _():
                self.line_copy(1, z, source).start()

            self.across_copy(z, y, source).start()
            return
        if k < line:

            @pl.when(z >= k)
            def _():
                j = z - k
                self.line_copy(0, j).wait_recv()

                @pl.when(z < line - 1)
                def _():
                    self.line_copy(0, j).start()

                self.across_copy(j, y).start()
                self.mate_copy(j, y, core).start()

            @pl.when(z + k < line)
            def _():
                j = z + k
                self.line_copy(1, j).wait_recv()

                @pl.when(z > 0)
                def _():
                    self.line_copy(1, j).start()

                self.across_copy(j, y).start()
                self.mate_copy(j, y, core).start()

        far = k - 1
        other = 1 - y

        def landed(j):
            self.across_copy(j, other).wait_recv()
            self.mate_copy(j, other, core).start()

        if far == 0:
            landed(z)
        elif far < line:

            @pl.when(z >= far)
            def _():
                landed(z - far)

            @pl.when(z + far < line)
            def _():
                landed(z + far)

    def steps(self):
        return self.p.line + 1

    def finish(self):
        p, line = self.p, self.p.line
        z, y = p.z, p.y
        mate_core = 1 - p.core
        self.own().wait()
        for j in range(line):

            @pl.when(j != z)
            def _():
                self.mate_copy(j, y, mate_core).wait_recv()
                self.mate_copy(j, y, p.core).wait_send()

            self.mate_copy(j, 1 - y, mate_core).wait_recv()
            self.mate_copy(j, 1 - y, p.core).wait_send()
            self.across_copy(j, y).wait_send()

            @pl.when((j <= z) & (z < line - 1))
            def _():
                self.line_copy(0, j).wait_send()

            @pl.when((j >= z) & (z > 0))
            def _():
                self.line_copy(1, j).wait_send()


def gather_sems(place_line, channels):
    return [
        pltpu.SemaphoreType.DMA((channels, 5, place_line)),
        pltpu.SemaphoreType.DMA((channels, 5, place_line)),
        pltpu.SemaphoreType.DMA((channels,)),
    ]


class Reduce:
    def __init__(self, place, term, mine, out, bufs, sems, channel, line_first):
        self.p, self.term, self.mine, self.out = place, term, mine, out
        self.one, self.two, self.up, self.down, self.parts = bufs
        self.send, self.recv = sems
        self.ch, self.line_first = channel, line_first

    def copy(self, src, dst, slot, where):
        return remote(src, dst, self.send.at[self.ch, slot], self.recv.at[self.ch, slot], where)

    def mate_copy(self):
        p = self.p
        return self.copy(self.term.at[:, :, 1 - p.core], self.one, 0, p.mate())

    def mine_copy(self):
        return pltpu.make_async_copy(self.term.at[:, :, self.p.core], self.mine, self.send.at[self.ch, 2])

    def across_copy(self):
        p = self.p
        if self.line_first:
            return self.copy(self.one.at[p.z, 1 - p.y], self.two, 1, p.across())
        return self.copy(self.one.at[:, 1 - p.y], self.two, 1, p.across())

    def running(self):
        return self.one if self.line_first else self.two

    def up_copy(self, j):
        return self.copy(self.running().at[j], self.up.at[j], 4 + j, self.p.along(1))

    def down_copy(self, j):
        return self.copy(self.running().at[j], self.down.at[j], 4 + self.p.line + j, self.p.along(-1))

    def ctx_copy(self, k):
        p = self.p
        where = {"ctx": (p.c + 2 * k) % p.n, "fsdp": p.f}
        mine = self.parts.at[p.c // 2]
        return self.copy(mine, mine, 4 + 2 * p.line + k, where)

    def last_copy(self):
        p = self.p
        return self.copy(self.out.at[p.core], self.out.at[p.core], 3, p.mate())

    def step0(self):
        self.mate_copy().start()
        if self.mine is not None:
            self.mine_copy().start()

    def step1(self):
        p = self.p
        if self.mine is not None:
            self.mine_copy().wait()
        self.mate_copy().wait_recv()

        def add(i, carry):
            for y in range(2):
                own = self.term[i, y, p.core] if self.mine is None else self.mine[i, y]
                self.one[i, y] = (self.one[i, y].astype(F32) + own.astype(F32)).astype(BF16)
            return carry

        lax.fori_loop(0, p.line, add, 0)
        if self.line_first:
            self.line_start()
        else:
            self.across_copy().start()

    def line_start(self):
        p = self.p

        @pl.when(p.z == 0)
        def _():
            for j in range(p.line - 1, 0, -1):
                self.up_copy(j).start()

        @pl.when(p.z == p.line - 1)
        def _():
            for j in range(0, p.line - 1):
                self.down_copy(j).start()

    def line_step(self, d):
        p = self.p
        running = self.running()
        for sign, move, buf in ((1, self.up_copy, self.up), (-1, self.down_copy, self.down)):
            j = p.z + sign * d
            valid = (j < p.line) & (p.z > 0) if sign > 0 else (j >= 0) & (p.z < p.line - 1)

            @pl.when(valid)
            def _():
                move(j).wait_recv()
                running[j] = (running[j].astype(F32) + buf[j].astype(F32)).astype(BF16)
                if d > 0:
                    move(j).start()

    def step2(self):
        p = self.p
        self.across_copy().wait_recv()

        def add(i, carry):
            self.two[i] = (self.two[i].astype(F32) + self.one[i, p.y].astype(F32)).astype(BF16)
            return carry

        lax.fori_loop(0, p.line, add, 0)
        self.line_start()

    def step3(self):
        self.line_step(0)
        self.across_copy().start()

    def step4(self):
        p = self.p
        if self.line_first:
            self.across_copy().wait_recv()
            self.parts[p.c // 2] = (self.two[...].astype(F32) + self.one[p.z, p.y].astype(F32)).astype(BF16)
        else:
            self.line_step(0)
            self.parts[p.c // 2] = self.two[p.z]
        for k in range(1, p.n // 2):
            self.ctx_copy(k).start()

    def actions(self):
        line = [lambda d=d: self.line_step(d) for d in range(self.p.line - 1, 0, -1)]
        if self.line_first:
            return [self.step1] + line + [self.step3, self.step4, self.step5]
        return [self.step1, self.step2] + line + [self.step4, self.step5]

    def step5(self):
        p = self.p
        for k in range(1, p.n // 2):
            self.ctx_copy(k).wait_recv()
        total = self.parts[0].astype(F32)
        for c in range(1, p.n // 2):
            total = total + self.parts[c].astype(F32)
        self.out[p.core] = total.astype(BF16)
        self.last_copy().start()

    def finish(self):
        p = self.p
        self.last_copy_in().wait_recv()
        self.last_copy().wait_send()
        self.mate_copy().wait_send()
        self.across_copy().wait_send()
        for j in range(p.line):

            @pl.when(j > p.z)
            def _():
                self.up_copy(j).wait_send()

            @pl.when(j < p.z)
            def _():
                self.down_copy(j).wait_send()

        for k in range(1, p.n // 2):
            self.ctx_copy(k).wait_send()

    def last_copy_in(self):
        p = self.p
        return self.copy(self.out.at[1 - p.core], self.out.at[1 - p.core], 3, p.mate())


def reduce_scratch(shape, h, w, line_first, stored=True):
    line, n = shape["fsdp"] // 2, shape["ctx"]
    run = (line, 2, h, w) if line_first else (line, h, w)
    return [
        pltpu.VMEM((line, 2, h, w) if stored else (8, 128), BF16),
        pltpu.VMEM((line, 2, h, w), BF16),
        pltpu.VMEM((h, w) if line_first else (line, h, w), BF16),
        pltpu.VMEM(run, BF16),
        pltpu.VMEM(run, BF16),
        pltpu.VMEM((n // 2, h, w), BF16),
    ]


def reduce_sems(shape, channels):
    slots = 4 + shape["fsdp"] + shape["ctx"] // 2
    return [pltpu.SemaphoreType.DMA((channels, slots))] * 2


def halves(pair):
    low = lax.broadcasted_iota(jnp.int32, pair.shape, 1) < 64
    zero = jnp.zeros_like(pair)
    return jnp.concatenate([jnp.where(low, pair, zero), jnp.where(low, zero, pair)], axis=0)


def corner(both):
    return jnp.concatenate([both[0:64, 0:SPAN], both[64:128, SPAN : 2 * SPAN]], axis=0)


def turn(value):
    return value.astype(F32).T.astype(BF16)


class Agenda:
    def __init__(self, actions, places):
        self.plan = {}
        for i, action in enumerate(actions):
            self.plan.setdefault(i * places // len(actions), []).append(action)

    def at(self, place, index=None, count=1):
        if index is None:
            for action in self.plan.get(place, ()):
                action()
            return
        for k in range(count):
            if place + k in self.plan:

                @pl.when(index == k)
                def _(k=k):
                    for action in self.plan[place + k]:
                        action()


def front_kernel(shape, *refs):
    shards, x_hbm = refs[0:5], refs[5]
    wq_out, wo_out, wu_out, wd_out, norms_ref, mixed_out, prob_out, att_out, attt_out, normt_out, unit_out, far_ref, rstd_ref = refs[6:19]
    (x_ref, wq_ref, raw_ref, mixed_ref, prob_ref, att_ref, attt_ref, normt_ref, low_ref, own_ref, all_ref, fart_ref, bias_ref,
     gsend, grecv, glocal, ssend, srecv, nsend, nrecv, io_sem) = refs[19:]
    batches, tokens, _ = x_ref.shape
    spans = tokens // SPAN
    count = far_ref.shape[1]
    prompt = count // 2
    m = shape["fsdp"]
    width = D // m
    place = Place(shape)
    first = place.c * spans

    load = [pltpu.make_async_copy(x_hbm.at[b], x_ref.at[b], io_sem.at[0, b]) for b in range(batches)]
    for copy in load:
        copy.start()
    place.greet(pltpu.get_barrier_semaphore(), rows=True)
    norm_copies = []
    for k in range(1, m):
        where = {"ctx": place.c, "fsdp": (place.f + k) % m}
        norm_copies.append(remote(shards[1], raw_ref.at[place.f], nsend.at[k], nrecv.at[k], where))
        norm_copies[-1].start()
    sems = (gsend, grecv, glocal)
    soon = [Gather(place, shards[0], wq_ref, sems, c, pl.ds(c * D, D)) for c in (1, 2, 0)]
    later = [Gather(place, shards[i], full, sems, 1 + i) for i, full in ((2, wo_out), (3, wu_out), (4, wd_out))]
    steps = soon[0].steps()
    for part in soon:
        part.step(0)
    raw_ref[place.f] = shards[1][...]
    for copy in norm_copies:
        copy.wait()
    for f in range(m):
        norms_ref[0:4, f * width : (f + 1) * width] = raw_ref[f, 0:4, 0:width]
    gain = norms_ref[0:1, :]
    shift = norms_ref[2:3, :]
    key_id = lax.broadcasted_iota(jnp.int32, (SPAN, 2 * SPAN), 0)
    query_id = lax.broadcasted_iota(jnp.int32, (SPAN, 2 * SPAN), 1) & (SPAN - 1)
    for s in range(2):
        bias_ref[s, 0:SPAN, :] = jnp.where(key_id <= query_id, 0.0, NEG)

    norm_outs = lambda b: [
        pltpu.make_async_copy(normt_ref.at[b], normt_out.at[b], io_sem.at[1, b]),
        pltpu.make_async_copy(x_ref.at[b], unit_out.at[b], io_sem.at[7, b]),
    ]
    tile = 512
    tiles = tokens // tile
    step_of = lambda part, k: lambda: part.step(k)
    early = Agenda([lambda: None] * 2 + [lambda: [part.step(1) for part in soon]] + [lambda: None] * 2, batches * tiles)

    for b in range(batches):
        load[b].wait()

        def norm(i, carry, b=b):
            early.at(b * tiles, i, tiles)
            rows = pl.ds(pl.multiple_of(i * tile, tile), tile)
            unit, rstd = unit_of(x_ref[b, rows, :].astype(F32))
            low = (unit * gain + shift).astype(BF16)
            low_ref[b, rows, :] = low
            normt_ref[b, :, rows] = low.T
            x_ref[b, rows, :] = unit.astype(BF16)
            rstd_ref[b, rows, :] = rstd
            return carry

        lax.fori_loop(0, tiles, norm, 0)
        for copy in norm_outs(b):
            copy.start()

    def share(k):
        to = (place.c + k) % place.n
        return remote(own_ref, all_ref.at[place.c], ssend.at[k], srecv.at[k], {"ctx": to, "fsdp": place.f})

    def project(c):
        def body(i, carry):
            for b in range(batches):
                rows = pl.ds(pl.multiple_of(i * tile, tile), tile)
                part = nn(low_ref[b, rows, :], wq_ref[:, :, :, c * D : (c + 1) * D].reshape(D, D))
                if c == 0:
                    mixed_ref[b, rows, 0:D] = part.astype(BF16) * 0.125
                    continue
                mixed_ref[b, rows, c * D : (c + 1) * D] = part.astype(BF16)
                for s in range(tile // SPAN):
                    total = jnp.sum(part[s * SPAN : (s + 1) * SPAN, :], axis=0, keepdims=True) * SPAN ** (-0.5)
                    own_ref[b, pl.ds(i * (tile // SPAN) + s, 1), (c - 1) * D : c * D] = total.astype(BF16).astype(F32)
            return carry

        lax.fori_loop(0, tiles, body, 0)

    for k in range(2, steps):
        for part in soon:
            part.step(k)
    for part in later:
        part.step(0)
    soon[0].finish()
    project(1)
    soon[1].finish()
    project(2)
    for k in range(1, place.n):
        share(k).start()
    all_ref[place.c] = own_ref[...]
    later[0].step(1)
    soon[2].finish()
    project(0)
    later[1].step(1)
    pairs = spans // 2
    rest = Agenda(
        [step_of(later[2], 1)] + [step_of(part, k) for k in range(2, steps) for part in later],
        batches * pairs - LEAD,
    )
    weight_out = pltpu.make_async_copy(wq_ref, wq_out, io_sem.at[6, 0])
    weight_out.start()
    for k in range(1, place.n):
        share(k).wait()

    out_copies = lambda b: [
        pltpu.make_async_copy(src.at[b], dst.at[b], io_sem.at[2 + i, b])
        for i, (src, dst) in enumerate(
            ((mixed_ref, mixed_out), (prob_ref, prob_out), (att_ref, att_out), (attt_ref, attt_out))
        )
    ]

    for b in range(batches):
        out_copies(b)[0].start()
        for c in range(place.n):
            far_ref[b, c * spans : (c + 1) * spans, :] = all_ref[c, b].astype(BF16)
        fart_ref[...] = far_ref[b, :, D:].T

        def attend(i, carry, b=b):
            rest.at(b * pairs, i, pairs)
            for s in range(2):
                far_id = lax.broadcasted_iota(jnp.int32, (count, 2 * SPAN), 0)
                mine = first + i * 2 + s
                segment = (mine - prompt) >> 3
                seen = (far_id < mine) & ((far_id < prompt) | (((far_id - prompt) >> 3) == segment))
                bias_ref[s, SPAN:, :] = jnp.where(seen, 0.0, NEG)
            scores, probs = {}, {}
            items = [(s, p) for p in range(PAIRS) for s in range(2)]
            for t in range(len(items) + 2):
                if t < len(items):
                    s, p = items[t]
                    rows = pl.ds(pl.multiple_of(i * 2 * SPAN + s * SPAN, SPAN), SPAN)
                    lanes = slice(p * SPAN, (p + 1) * SPAN)
                    qs = halves(mixed_ref[b, rows, lanes])
                    keys = jnp.concatenate(
                        [mixed_ref[b, rows, D + p * SPAN : D + (p + 1) * SPAN], far_ref[b, :, lanes]], axis=0
                    )
                    scores[t] = nt(keys, qs)
                if 1 <= t <= len(items):
                    s, p = items[t - 1]
                    score = scores.pop(t - 1) + bias_ref[s]
                    score = jnp.exp(score - jnp.max(score, axis=0, keepdims=True))
                    prob = (score * (1.0 / jnp.sum(score, axis=0, keepdims=True))).astype(BF16)
                    prob_ref[b, i * 2 + s, p] = prob
                    probs[t - 1] = prob
                if t >= 2:
                    s, p = items[t - 2]
                    rows = pl.ds(pl.multiple_of(i * 2 * SPAN + s * SPAN, SPAN), SPAN)
                    lanes = slice(p * SPAN, (p + 1) * SPAN)
                    turned = mixed_ref[b, rows, 2 * D + p * SPAN : 2 * D + (p + 1) * SPAN].T
                    turned = jnp.concatenate([turned, fart_ref[lanes, :]], axis=1)
                    att = corner(nn(turned, probs.pop(t - 2))).astype(BF16)
                    attt_ref[b, lanes, rows] = att
                    att_ref[b, rows, lanes] = att.T
            return carry

        lax.fori_loop(0, pairs, attend, 0)
        for copy in out_copies(b)[1:]:
            copy.start()

    for part in later:
        part.finish()
    weight_out.wait()
    for b in range(batches):
        for copy in norm_outs(b) + out_copies(b):
            copy.wait()


def front_call(shape, shards, x):
    batches, tokens, _ = x.shape
    spans = tokens // SPAN
    n, m = shape["ctx"], shape["fsdp"]
    count = n * spans
    any_spec = pl.BlockSpec(memory_space=pl.ANY)
    vmem = pl.BlockSpec(memory_space=pltpu.VMEM)
    full = [jax.ShapeDtypeStruct((m,) + s.shape, s.dtype) for s in shards]
    big = [
        jax.ShapeDtypeStruct((batches, tokens, 3 * D), BF16),
        jax.ShapeDtypeStruct((batches, spans, PAIRS, SPAN + count, 2 * SPAN), BF16),
        jax.ShapeDtypeStruct((batches, tokens, D), BF16),
        jax.ShapeDtypeStruct((batches, D, tokens), BF16),
        jax.ShapeDtypeStruct((batches, D, tokens), BF16),
    ]
    return pl.pallas_call(
        functools.partial(front_kernel, shape),
        in_specs=[any_spec, vmem] + [any_spec] * 4,
        out_specs=[any_spec] * 4 + [vmem] + [any_spec] * 6 + [vmem] * 2,
        out_shape=[full[0], full[2], full[3], full[4], jax.ShapeDtypeStruct((8, D), F32)]
        + big
        + [
            jax.ShapeDtypeStruct(x.shape, BF16),
            jax.ShapeDtypeStruct((batches, count, 2 * D), BF16),
            jax.ShapeDtypeStruct((batches, tokens, 1), F32),
        ],
        scratch_shapes=[
            pltpu.VMEM((batches, tokens, D), BF16),
            pltpu.VMEM(full[0].shape, BF16),
            pltpu.VMEM(full[1].shape, F32),
        ]
        + [pltpu.VMEM(v.shape, v.dtype) for v in big]
        + [
            pltpu.VMEM((batches, tokens, D), BF16),
            pltpu.VMEM((batches, spans, 2 * D), F32),
            pltpu.VMEM((n, batches, spans, 2 * D), F32),
            pltpu.VMEM((D, count), BF16),
            pltpu.VMEM((2, SPAN + count, 2 * SPAN), F32),
        ]
        + gather_sems(m // 2, 6)
        + [
            pltpu.SemaphoreType.DMA((n,)),
            pltpu.SemaphoreType.DMA((n,)),
            pltpu.SemaphoreType.DMA((m,)),
            pltpu.SemaphoreType.DMA((m,)),
            pltpu.SemaphoreType.DMA((8, batches)),
        ],
        compiler_params=pltpu.CompilerParams(collective_id=0, has_side_effects=True, vmem_limit_bytes=VMEM_LIMIT),
        name="front",
    )(*shards, x)


def middle_kernel(
    x_ref, g_ref, att_ref, attt_ref, wo_ref, wu_ref, wd_ref, norms_ref,
    out_ref, gmid_ref, da_ref, go_ref, gu_ref, gd_ref, ggain_ref, gshift_ref,
    n2t_ref, gt_ref, act_ref, gh_ref, goa_ref, gua_ref, gda_ref, half_ref,
):
    tokens = x_ref.shape[1]

    @pl.when(pl.program_id(0) == 0)
    def _():
        half_ref[...] = wd_ref[...] * 0.5
        goa_ref[...] = jnp.zeros_like(goa_ref)
        gua_ref[...] = jnp.zeros_like(gua_ref)
        gda_ref[...] = jnp.zeros_like(gda_ref)
        ggain_ref[...] = jnp.zeros_like(ggain_ref)
        gshift_ref[...] = jnp.zeros_like(gshift_ref)

    tile = 512
    gain = norms_ref[1:2, :]
    shift = norms_ref[3:4, :]

    def mlp(i, carry):
        rows = pl.ds(pl.multiple_of(i * tile, tile), tile)
        middle = x_ref[0, rows, :].astype(F32) + nn(att_ref[0, rows, :], wo_ref[...])
        unit, rstd = unit_of(middle)
        low = unit * gain + shift
        low = low.astype(BF16)
        n2t_ref[:, rows] = low.T
        g = g_ref[0, rows, :]
        gt_ref[:, rows] = g.T
        for c in range(FF // CHUNK):
            cols = slice(c * CHUNK, (c + 1) * CHUNK)
            act, slope = gelu_pair(nn(low, wu_ref[:, cols]))
            act_ref[rows, cols] = act.astype(BF16)
            gh_ref[rows, cols] = (nt(g, half_ref[cols, :]) * slope).astype(BF16)
        out_ref[0, rows, :] = (middle + nn(act_ref[rows, :], half_ref[...])).astype(BF16)
        grad = nt(gh_ref[rows, :], wu_ref[...])
        ggain_ref[...] += fold8(grad * unit)
        gshift_ref[...] += fold8(grad)
        grad = g.astype(F32) + norm_back(grad, unit, rstd, gain)
        low = grad.astype(BF16)
        gmid_ref[0, rows, :] = low
        da_ref[0, rows, :] = nt(low, wo_ref[...]).astype(BF16)
        return carry

    lax.fori_loop(0, tokens // tile, mlp, 0)

    goa_ref[...] += nn(attt_ref[0], gmid_ref[0])

    def wgrad(c, carry):
        cols = pl.ds(pl.multiple_of(c * 512, 512), 512)
        gua_ref[:, cols] += nn(n2t_ref[...], gh_ref[:, cols])
        gda_ref[:, cols] += nn(gt_ref[...], act_ref[:, cols])
        return carry

    lax.fori_loop(0, 4, wgrad, 0)

    @pl.when(pl.program_id(0) == pl.num_programs(0) - 1)
    def _():
        go_ref[...] = goa_ref[...].astype(BF16)

        def close(c, carry):
            cols = pl.ds(pl.multiple_of(c * 512, 512), 512)
            gu_ref[:, cols] = gua_ref[:, cols].astype(BF16)
            gd_ref[cols, :] = (gda_ref[:, cols] * 0.5).astype(BF16).T
            return carry

        lax.fori_loop(0, 4, close, 0)


def middle_call(x, g, att, attt, wo, wu, wd, norms):
    batches, tokens, _ = x.shape
    one = pl.Buffered(1)
    seq = lambda *dims: pl.BlockSpec((1,) + dims, lambda b: (b, 0, 0))
    whole = lambda *shape: pl.BlockSpec(shape, lambda b: (0,) * len(shape), pipeline_mode=one)
    return pl.pallas_call(
        middle_kernel,
        grid=(batches,),
        in_specs=[
            seq(tokens, D), seq(tokens, D), seq(tokens, D), seq(D, tokens),
            whole(D, D), whole(D, FF), whole(FF, D), whole(8, D),
        ],
        out_specs=[
            seq(tokens, D), seq(tokens, D), seq(tokens, D),
            whole(D, D), whole(D, FF), whole(FF, D), whole(8, D), whole(8, D),
        ],
        out_shape=[
            jax.ShapeDtypeStruct((batches, tokens, D), BF16),
            jax.ShapeDtypeStruct((batches, tokens, D), BF16),
            jax.ShapeDtypeStruct((batches, tokens, D), BF16),
            jax.ShapeDtypeStruct((D, D), BF16),
            jax.ShapeDtypeStruct((D, FF), BF16),
            jax.ShapeDtypeStruct((FF, D), BF16),
            jax.ShapeDtypeStruct((8, D), F32),
            jax.ShapeDtypeStruct((8, D), F32),
        ],
        scratch_shapes=[
            pltpu.VMEM((D, tokens), BF16),
            pltpu.VMEM((D, tokens), BF16),
            pltpu.VMEM((tokens, FF), BF16),
            pltpu.VMEM((tokens, FF), BF16),
            pltpu.VMEM((D, D), F32),
            pltpu.VMEM((D, FF), F32),
            pltpu.VMEM((D, FF), F32),
            pltpu.VMEM((FF, D), BF16),
        ],
        compiler_params=pltpu.CompilerParams(vmem_limit_bytes=VMEM_LIMIT),
        name="middle",
    )(x, g, att, attt, wo, wu, wd, norms)


def back_kernel(shape, *refs):
    mixed_hbm, da_hbm, prob_hbm, unit_hbm, normt_hbm, gmid_hbm, wq_hbm, gu_hbm, gd_hbm, go_hbm = refs[0:10]
    far_ref, rstd_ref, norms_ref, gain2_ref, shift2_ref = refs[10:15]
    gin_out, gq_out, gkv_out, gu_out, gd_out, go_out, small_out = refs[15:22]
    (mixed_ref, da_ref, prob_ref, unit_ref, normt_ref, gmid_ref, wq_ref, dmixed_ref, gw_ref, gq_ref, gkv_ref,
     far_t, dfar_ref, held_ref, gsum_ref, vec_ref, vecs_ref, vsum_ref, pieces_ref) = refs[22:41]
    bufs, sems = refs[41:71], refs[71:73]
    xsend, xrecv, vsend, vrecv, io_sem = refs[73:78]
    batches, tokens, _ = unit_ref.shape
    spans = tokens // SPAN
    count = far_ref.shape[1]
    m = shape["fsdp"]
    width = D // m
    place = Place(shape)

    ins = lambda b: [
        pltpu.make_async_copy(src.at[b], dst.at[b % 2], io_sem.at[i, b])
        for i, (src, dst) in enumerate(((mixed_hbm, mixed_ref), (da_hbm, da_ref), (prob_hbm, prob_ref)))
    ]
    rest = [
        pltpu.make_async_copy(src, dst, io_sem.at[4 + i, 0])
        for i, (src, dst) in enumerate(
            ((normt_hbm, normt_ref), (unit_hbm, unit_ref), (gmid_hbm, gmid_ref), (wq_hbm, wq_ref))
        )
    ]
    for copy in ins(0):
        copy.start()
    place.greet(pltpu.get_barrier_semaphore(), rows=True)
    channel = lambda i, term, out, line_first, stored: Reduce(
        place, term, bufs[6 * i] if stored else None, out, bufs[6 * i + 1 : 6 * i + 6], sems, i, line_first
    )
    gu = channel(0, gu_hbm, gu_out, False, True)
    gd = channel(1, gd_hbm, gd_out, True, True)
    go = channel(2, go_hbm, go_out, False, True)
    gq = channel(3, gq_ref, gq_out, True, False)
    gkv = channel(4, gkv_ref, gkv_out, False, False)
    for part in (gu, gd, go):
        part.step0()
    for copy in rest:
        copy.start()

    def swap(b, k):
        to = (place.c + k) % place.n
        source = dfar_ref.at[b, pl.ds(pl.multiple_of(to * spans, spans), spans)]
        return remote(source, held_ref.at[b, k], xsend.at[b, k], xrecv.at[b, k], {"ctx": to, "fsdp": place.f})

    pairs = spans // 2
    mixed_actions = [action for both in zip(gu.actions(), gd.actions()) for action in both]
    big = Agenda([lambda: None] * WAIT + mixed_actions[:-2] + go.actions(), batches * (pairs + EXTRA))

    def attend_back(b):
        slot = b % 2
        for copy in ins(b):
            copy.wait()
        if b + 1 < batches:
            for copy in ins(b + 1):
                copy.start()
        dfar_ref[b] = jnp.zeros((count, 2 * D), F32)
        far_t[...] = far_ref[b, :, 0:D].T
        base = b * (pairs + EXTRA)

        def body(i, carry):
            big.at(base, i, pairs)
            items = [(s, p) for p in range(PAIRS) for s in range(2)]
            held, grads = {}, {}
            where = lambda t: (
                pl.ds(pl.multiple_of(i * 2 * SPAN + items[t][0] * SPAN, SPAN), SPAN),
                *(slice(c * D + items[t][1] * SPAN, c * D + (items[t][1] + 1) * SPAN) for c in range(3)),
            )
            for t in range(len(items) + 2):
                if t < len(items):
                    rows, lanes, klanes, vlanes = where(t)
                    das = halves(da_ref[slot, rows, lanes])
                    values = jnp.concatenate([mixed_ref[slot, rows, vlanes], far_ref[b, :, klanes]], axis=0)
                    held[t] = (das, nt(values, das))
                if 1 <= t <= len(items):
                    rows, lanes, klanes, vlanes = where(t - 1)
                    das, slope = held.pop(t - 1)
                    low = prob_ref[slot, i * 2 + items[t - 1][0], items[t - 1][1]]
                    prob = low.astype(F32)
                    inner = jnp.sum(prob * slope, axis=0, keepdims=True)
                    grads[t - 1] = (prob * (slope - inner)).astype(BF16)
                    dv = nn(low, das)
                    dmixed_ref[b, rows, vlanes] = dv[0:SPAN].astype(BF16)
                    dfar_ref[b, :, klanes] += dv[SPAN:]
                if t >= 2:
                    rows, lanes, klanes, vlanes = where(t - 2)
                    grad = grads.pop(t - 2)
                    dk = nn(grad, halves(mixed_ref[slot, rows, lanes]))
                    dmixed_ref[b, rows, klanes] = dk[0:SPAN].astype(BF16)
                    dfar_ref[b, :, lanes] += dk[SPAN:]
                    turned = jnp.concatenate([mixed_ref[slot, rows, klanes].T, far_t[lanes, :]], axis=1)
                    dmixed_ref[b, rows, lanes] = (corner(nn(turned, grad)) * 0.125).astype(BF16).T
            return carry

        lax.fori_loop(0, pairs, body, 0)
        for k in range(1, place.n):
            swap(b, k).start()

    def wgrad(b, c):
        cols = slice(c * D, (c + 1) * D)
        part = nn(normt_ref[b], dmixed_ref[b, :, cols])
        gw_ref[:, cols] = part if b == 0 else gw_ref[:, cols] + part

    def spread(b):
        for k in range(1, place.n):
            swap(b, k).wait()
        total = dfar_ref[b, pl.ds(pl.multiple_of(place.c * spans, spans), spans), :]
        for k in range(1, place.n):
            total = total + held_ref[b, k]
        gsum_ref[...] = total * SPAN ** (-0.5)

        def body(s, carry):
            rows = pl.ds(pl.multiple_of(s * SPAN, SPAN), SPAN)
            extra = jnp.broadcast_to(gsum_ref[pl.ds(s, 1), :], (16, 2 * D)).astype(BF16)
            for r in range(SPAN // 16):
                at = pl.ds(pl.multiple_of(s * SPAN + r * 16, 16), 16)
                dmixed_ref[b, at, D:] = dmixed_ref[b, at, D:] + extra
            return carry

        lax.fori_loop(0, spans, body, 0)

    half = D // m // 2

    def low(dst, cols):
        def body(i, carry):
            for y in range(2):
                for s in range(2):
                    start = pl.multiple_of(((i * 2 + y) * 2 + s) * half, half)
                    dst[i, y, s] = gw_ref[pl.ds(start, half), cols].astype(BF16)
            return carry

        lax.fori_loop(0, m // 2, body, 0)

    for b in range(batches):
        attend_back(b)
        if b == 0:
            for copy in rest:
                copy.wait()
        base = b * (pairs + EXTRA) + pairs
        big.at(base)
        wgrad(b, 0)
        if b + 1 == batches:
            low(gq_ref, slice(0, D))
            gq.step0()
        big.at(base + 1)
        if b > 0:
            spread(b - 1)
            for c in (1, 2):
                wgrad(b - 1, c)
        big.at(base + 2)
    last = batches - 1
    spread(last)
    for c in (1, 2):
        wgrad(last, c)
    low(gkv_ref, slice(D, 3 * D))
    gkv.step0()
    for action in mixed_actions[-2:]:
        action()

    gain = norms_ref[0:1, :]
    tile = 512
    tiles = tokens // tile
    late = Agenda([action for both in zip(gkv.actions(), gq.actions()) for action in both], batches * tiles)
    gin_copy = lambda b: pltpu.make_async_copy(gmid_ref.at[b], gin_out.at[b], io_sem.at[3, b])
    gains_at = jnp.zeros((8, D), F32)
    shifts_at = jnp.zeros((8, D), F32)
    for b in range(batches):

        def data(i, carry, b=b):
            late.at(b * tiles, i, tiles)
            spots = [pl.ds(pl.multiple_of(i * tile + r * (tile // 2), tile // 2), tile // 2) for r in range(2)]
            grads = [nt(dmixed_ref[b, rows, :], wq_ref[...].reshape(D, 3 * D)) for rows in spots]
            gains_at, shifts_at = carry
            for rows, grad in zip(spots, grads):
                unit = unit_ref[b, rows, :].astype(F32)
                change = norm_back(grad, unit, rstd_ref[b, rows, :], gain)
                gmid_ref[b, rows, :] = (gmid_ref[b, rows, :].astype(F32) + change).astype(BF16)
                gains_at = gains_at + fold8(grad * unit)
                shifts_at = shifts_at + fold8(grad)
            return gains_at, shifts_at

        gains_at, shifts_at = lax.fori_loop(0, tiles, data, (gains_at, shifts_at))
        gin_copy(b).start()

    sums = [jnp.sum(v, axis=0, keepdims=True) for v in (gains_at, gain2_ref[...], shifts_at, shift2_ref[...])]
    vec_ref[...] = jnp.concatenate(sums + [jnp.zeros((4, D), F32)], axis=0)
    over_ctx = [
        remote(vec_ref, vecs_ref.at[k], vsend.at[0, k], vrecv.at[0, k], {"ctx": (place.c + k) % place.n, "fsdp": place.f})
        for k in range(1, place.n)
    ]
    for copy in over_ctx:
        copy.start()
    vecs_ref[0] = vec_ref[...]
    for copy in over_ctx:
        copy.wait()
    total = jnp.zeros((8, D), F32)
    for c in range(place.n):
        total = total + vecs_ref[(place.c - c + place.n) % place.n]
    vsum_ref[...] = jnp.zeros_like(vsum_ref)
    for f in range(m):
        vsum_ref[f, :, 0:width] = total[:, f * width : (f + 1) * width]
    over_rows = []
    for k in range(1, m):
        to = (place.f + k) % m
        over_rows.append(
            remote(vsum_ref.at[to], pieces_ref.at[place.f], vsend.at[1, k], vrecv.at[1, k], {"ctx": place.c, "fsdp": to})
        )
        over_rows[-1].start()
    pieces_ref[place.f] = vsum_ref[place.f]
    for copy in over_rows:
        copy.wait()
    total = pieces_ref[0]
    for f in range(1, m):
        total = total + pieces_ref[f]
    small_out[...] = total
    for part in (gu, gd, go, gq, gkv):
        part.finish()
    for b in range(batches):
        gin_copy(b).wait()


def back_call(shape, mixed, da, prob, unit, normt, gmid, wq, gu, gd, go, far, rstd, norms, gain2, shift2):
    batches, tokens, _ = unit.shape
    spans = tokens // SPAN
    n, m = shape["ctx"], shape["fsdp"]
    line = m // 2
    count = n * spans
    any_spec = pl.BlockSpec(memory_space=pl.ANY)
    vmem = pl.BlockSpec(memory_space=pltpu.VMEM)
    halved = lambda rows, w: (line, 2, 2, rows // (2 * m), w)
    terms = [halved(D, FF), halved(FF, D), halved(D, D), halved(D, D), halved(D, 2 * D)]
    gu, gd, go = (v.reshape(t) for v, t in zip((gu, gd, go), terms))
    out = lambda t: jax.ShapeDtypeStruct(t[2:], BF16)
    two = lambda *dims: pltpu.VMEM((2,) + dims, BF16)
    scratch = [
        two(tokens, 3 * D), two(tokens, D), two(spans, PAIRS, SPAN + count, 2 * SPAN),
        pltpu.VMEM(unit.shape, BF16), pltpu.VMEM(normt.shape, BF16), pltpu.VMEM(unit.shape, BF16),
        pltpu.VMEM(wq.shape, BF16), pltpu.VMEM((batches, tokens, 3 * D), BF16), pltpu.VMEM((D, 3 * D), F32),
        pltpu.VMEM(terms[3], BF16), pltpu.VMEM(terms[4], BF16),
        pltpu.VMEM((D, count), BF16), pltpu.VMEM((batches, count, 2 * D), F32),
        pltpu.VMEM((batches, n, spans, 2 * D), F32), pltpu.VMEM((spans, 2 * D), F32),
        pltpu.VMEM((8, D), F32), pltpu.VMEM((n, 8, D), F32), pltpu.VMEM((m, 8, 128), F32), pltpu.VMEM((m, 8, 128), F32),
    ]
    for t, line_first, stored in zip(terms, (False, True, False, True, False), (True, True, True, False, False)):
        scratch += reduce_scratch(shape, *t[3:], line_first, stored)
    scratch += reduce_sems(shape, 5)
    most = max(n, m)
    scratch += [
        pltpu.SemaphoreType.DMA((batches, n)), pltpu.SemaphoreType.DMA((batches, n)),
        pltpu.SemaphoreType.DMA((2, most)), pltpu.SemaphoreType.DMA((2, most)), pltpu.SemaphoreType.DMA((8, batches)),
    ]
    return pl.pallas_call(
        functools.partial(back_kernel, shape),
        in_specs=[any_spec] * 10 + [vmem] * 5,
        out_specs=[any_spec] + [vmem] * 6,
        out_shape=[
            jax.ShapeDtypeStruct(unit.shape, BF16), out(terms[3]), out(terms[4]), out(terms[0]), out(terms[1]),
            out(terms[2]), jax.ShapeDtypeStruct((8, 128), F32),
        ],
        scratch_shapes=scratch,
        compiler_params=pltpu.CompilerParams(collective_id=1, has_side_effects=True, vmem_limit_bytes=VMEM_LIMIT),
        name="back",
    )(mixed, da, prob, unit, normt, gmid, wq, gu, gd, go, far, rstd, norms, gain2, shift2)


def widen_kernel(gq_ref, gkv_ref, go_ref, gu_ref, gd_ref, qkv_out, out_out, up_out, down_out):
    qkv_out[:, 0:D] = gq_ref[...].astype(F32)
    qkv_out[:, D:] = gkv_ref[...].astype(F32)
    out_out[...] = go_ref[...].astype(F32)
    up_out[...] = gu_ref[...].astype(F32)
    down_out[...] = gd_ref[...].astype(F32)


def widen_call(gq, gkv, go, gu, gd):
    shapes = ((gq.shape[0], 3 * D), go.shape, gu.shape, gd.shape)
    return pl.pallas_call(
        widen_kernel,
        out_shape=[jax.ShapeDtypeStruct(v, F32) for v in shapes],
        name="widen",
    )(gq, gkv, go, gu, gd)


def local(shape, x, g, qkv_weight, out_weight, up_weight, down_weight, norm_gains, norm_shifts):
    width = norm_gains.shape[1]
    norms = jnp.concatenate([norm_gains, norm_shifts], axis=0).astype(F32)
    norms = jnp.pad(norms, ((0, 4), (0, 128 - width)))
    halved = lambda shard: shard.reshape(2, shard.shape[0] // 2, shard.shape[1])
    shards = [halved(qkv_weight), norms, halved(out_weight), halved(up_weight), halved(down_weight)]
    wq, wo, wu, wd, norms, mixed, prob, att, attt, normt, unit, far, rstd = front_call(shape, shards, x)
    wo, wu, wd = (w.reshape(-1, w.shape[-1]) for w in (wo, wu, wd))
    out, gmid, da, go, gu, gd, gain2, shift2 = middle_call(x, g, att, attt, wo, wu, wd, norms)
    gin, gq, gkv, gu, gd, go, small = back_call(
        shape, mixed, da, prob, unit, normt, gmid, wq, gu, gd, go, far, rstd, norms, gain2, shift2
    )
    gq, go, gu, gd = widen_call(*(v.reshape(-1, v.shape[-1]) for v in (gq, gkv, go, gu, gd)))
    small = small[0:4, 0:width]
    return out, gin, gq, go, gu, gd, small[0:2], small[2], small[3]


def solution(mesh):
    weight, norm, token = P("fsdp", None), P(None, "fsdp"), P("fsdp", "ctx", None)
    return jax.shard_map(
        functools.partial(local, dict(mesh.shape)),
        mesh=mesh,
        in_specs=(token, token, weight, weight, weight, weight, norm, norm),
        out_specs=(token, token, weight, weight, weight, weight, norm, P("fsdp"), P("fsdp")),
        check_vma=False,
    )
```

```python
import functools

import jax
import jax.numpy as jnp
from jax import lax
from jax.experimental import pallas as pl
from jax.experimental.pallas import tpu as pltpu
from jax.sharding import PartitionSpec as P

D = 512
HEADS = 8
FF = 2048
SPAN = 128
CONT = 1024
PAIRS = HEADS // 2
CHUNK = 512
UNIT = 128
LEAD = 1
EXTRA = 3

EPS = 1e-05
NEG = -1e30
F32 = jnp.float32
BF16 = jnp.bfloat16
VMEM_LIMIT = 60 * 1024 * 1024


def nn(a, b):
    return lax.dot_general(a, b, (((1,), (0,)), ((), ())), preferred_element_type=F32)


def nt(a, b):
    return lax.dot_general(a, b, (((1,), (1,)), ((), ())), preferred_element_type=F32)


def unit_of(values):
    center = values - jnp.mean(values, axis=-1, keepdims=True)
    rstd = lax.rsqrt(jnp.mean(center * center, axis=-1, keepdims=True) + EPS)
    return center * rstd, rstd


def norm_back(grad, unit, rstd, gain):
    scaled = grad * gain
    return rstd * (
        scaled
        - jnp.mean(scaled, axis=-1, keepdims=True)
        - unit * jnp.mean(scaled * unit, axis=-1, keepdims=True)
    )


def fold8(values):
    rows = values.shape[0]
    return jnp.sum(values.reshape(rows // 8, 8, values.shape[1]), axis=0)


def gelu_pair(x):
    cdf = lax.erf(x * 0.7071067811865476) + 1.0
    slope = jnp.exp2(x * x * (-0.5 * 1.4426950408889634)) * (x * 0.7978845608028654)
    return x * cdf, cdf + slope


MESH = pl.DeviceIdType.MESH


class Place:
    def __init__(self, mesh_shape):
        self.n, self.m = mesh_shape["ctx"], mesh_shape["fsdp"]
        self.inner = 2
        self.line = self.m // 2
        self.c, self.f = lax.axis_index("ctx"), lax.axis_index("fsdp")
        self.core = self.c % 2
        self.z, self.y = self.f // 2, self.f % 2

    def mate(self):
        return {"ctx": self.c + 1 - 2 * self.core, "fsdp": self.f}

    def across(self):
        return {"ctx": self.c, "fsdp": self.z * 2 + 1 - self.y}

    def along(self, step):
        return {"ctx": self.c, "fsdp": self.f + 2 * step}

    def greet(self, barrier, rows=False):
        signal = lambda where: pl.semaphore_signal(barrier, inc=1, device_id=where, device_id_type=MESH)
        for k in range(1, self.n):
            signal({"ctx": (self.c + k) % self.n, "fsdp": self.f})
        count = self.n - 1
        if rows:
            for k in range(1, self.m):
                signal({"ctx": self.c, "fsdp": (self.f + k) % self.m})
            count = count + self.m - 1
        else:
            signal(self.across())
            up = self.z < self.line - 1
            down = self.z > 0

            @pl.when(up)
            def _():
                signal(self.along(1))

            @pl.when(down)
            def _():
                signal(self.along(-1))

            count = count + 1 + up.astype(jnp.int32) + down.astype(jnp.int32)
        pl.semaphore_wait(barrier, count)


def remote(src, dst, send, recv, where):
    return pltpu.make_async_remote_copy(
        src_ref=src, dst_ref=dst, send_sem=send, recv_sem=recv, device_id=where, device_id_type=MESH
    )


class Gather:
    def __init__(self, place, shard, full, sems, channel, cols=slice(None)):
        self.p, self.shard, self.full, self.cols = place, shard, full, cols
        self.send, self.recv, self.local = sems
        self.ch = channel

    def piece(self, j, y, core):
        return self.full.at[j * 2 + y, core, :, self.cols]

    def line_copy(self, kind, j, source=None):
        p = self.p
        here = self.piece(j, p.y, p.core)
        return remote(
            here if source is None else source, here, self.send.at[self.ch, kind, j], self.recv.at[self.ch, kind, j],
            p.along(1 if kind == 0 else -1),
        )

    def across_copy(self, j, y, source=None):
        p = self.p
        here = self.piece(j, y, p.core)
        return remote(
            here if source is None else source, here, self.send.at[self.ch, 2, j], self.recv.at[self.ch, 2, j], p.across()
        )

    def mate_copy(self, j, y, core):
        p = self.p
        here = self.piece(j, y, core)
        slot = 3 + (y != p.y).astype(jnp.int32)
        return remote(here, here, self.send.at[self.ch, slot, j], self.recv.at[self.ch, slot, j], p.mate())

    def own(self):
        return pltpu.make_async_copy(
            self.shard.at[:, :, self.cols], self.full.at[self.p.f, :, :, self.cols], self.local.at[self.ch]
        )

    def step(self, k):
        p, line = self.p, self.p.line
        z, y, core = p.z, p.y, p.core
        if k == 0:
            self.own().start()
            source = self.shard.at[core, :, self.cols]

            @pl.when(z < line - 1)
            def _():
                self.line_copy(0, z, source).start()

            @pl.when(z > 0)
            def _():
                self.line_copy(1, z, source).start()

            self.across_copy(z, y, source).start()
            return
        if k < line:

            @pl.when(z >= k)
            def _():
                j = z - k
                self.line_copy(0, j).wait_recv()

                @pl.when(z < line - 1)
                def _():
                    self.line_copy(0, j).start()

                self.across_copy(j, y).start()
                self.mate_copy(j, y, core).start()

            @pl.when(z + k < line)
            def _():
                j = z + k
                self.line_copy(1, j).wait_recv()

                @pl.when(z > 0)
                def _():
                    self.line_copy(1, j).start()

                self.across_copy(j, y).start()
                self.mate_copy(j, y, core).start()

        far = k - 1
        other = 1 - y

        def landed(j):
            self.across_copy(j, other).wait_recv()
            self.mate_copy(j, other, core).start()

        if far == 0:
            landed(z)
        elif far < line:

            @pl.when(z >= far)
            def _():
                landed(z - far)

            @pl.when(z + far < line)
            def _():
                landed(z + far)

    def steps(self):
        return self.p.line + 1

    def finish(self):
        p, line = self.p, self.p.line
        z, y = p.z, p.y
        mate_core = 1 - p.core
        self.own().wait()
        for j in range(line):

            @pl.when(j != z)
            def _():
                self.mate_copy(j, y, mate_core).wait_recv()
                self.mate_copy(j, y, p.core).wait_send()

            self.mate_copy(j, 1 - y, mate_core).wait_recv()
            self.mate_copy(j, 1 - y, p.core).wait_send()
            self.across_copy(j, y).wait_send()

            @pl.when((j <= z) & (z < line - 1))
            def _():
                self.line_copy(0, j).wait_send()

            @pl.when((j >= z) & (z > 0))
            def _():
                self.line_copy(1, j).wait_send()


def gather_sems(place_line, channels):
    return [
        pltpu.SemaphoreType.DMA((channels, 5, place_line)),
        pltpu.SemaphoreType.DMA((channels, 5, place_line)),
        pltpu.SemaphoreType.DMA((channels,)),
    ]


class Reduce:
    def __init__(self, place, term, mine, out, bufs, sems, channel, line_first):
        self.p, self.term, self.mine, self.out = place, term, mine, out
        self.one, self.two, self.ins, self.parts = bufs
        self.send, self.recv = sems
        self.ch, self.line_first = channel, line_first

    def copy(self, src, dst, slot, where, back=None):
        back = slot if back is None else back
        return remote(src, dst, self.send.at[self.ch, slot], self.recv.at[self.ch, back], where)

    def mate_copy(self):
        p = self.p
        return self.copy(self.term.at[:, :, 1 - p.core], self.one, 0, p.mate())

    def mine_copy(self):
        return pltpu.make_async_copy(self.term.at[:, :, self.p.core], self.mine, self.send.at[self.ch, 2])

    def across_copy(self):
        p = self.p
        source = self.one.at[p.z, 1 - p.y] if self.line_first else self.one.at[:, 1 - p.y]
        return self.copy(source, self.two, 1, p.across())

    def line_out(self, k):
        p = self.p
        j = (p.z + k) % p.line
        source = self.one if self.line_first else self.two
        return self.copy(source.at[j], self.ins.at[k], 4 + k, {"ctx": p.c, "fsdp": j * 2 + p.y})

    def ctx_copy(self, k):
        p = self.p
        where = {"ctx": (p.c + 2 * k) % p.n, "fsdp": p.f}
        mine = self.parts.at[p.c // 2]
        return self.copy(mine, mine, 4 + p.line + k, where)

    def last_copy(self, core):
        return self.copy(self.out.at[core], self.out.at[core], 3, self.p.mate())

    def step0(self):
        self.mate_copy().start()
        if self.mine is not None:
            self.mine_copy().start()

    def from_mate(self):
        p = self.p
        if self.mine is not None:
            self.mine_copy().wait()
        self.mate_copy().wait_recv()

        def add(i, carry):
            for y in range(2):
                own = self.term[i, y, p.core] if self.mine is None else self.mine[i, y]
                self.one[i, y] = (self.one[i, y].astype(F32) + own.astype(F32)).astype(BF16)
            return carry

        lax.fori_loop(0, p.line, add, 0)

    def line_start(self):
        for k in range(1, self.p.line):
            self.line_out(k).start()

    def line_sum(self):
        p = self.p
        total = (self.one if self.line_first else self.two)[p.z].astype(F32)
        for k in range(1, p.line):
            self.line_out(k).wait_recv()
            total = total + self.ins[k].astype(F32)
        return total.astype(BF16)

    def ctx_start(self, value):
        p = self.p
        self.parts[p.c // 2] = value
        for k in range(1, p.n // 2):
            self.ctx_copy(k).start()

    def step1(self):
        self.from_mate()
        if self.line_first:
            self.line_start()
        else:
            self.across_copy().start()

    def step2(self):
        p = self.p
        if self.line_first:
            self.one[p.z] = self.line_sum()
            self.across_copy().start()
            return
        self.across_copy().wait_recv()

        def add(i, carry):
            self.two[i] = (self.two[i].astype(F32) + self.one[i, p.y].astype(F32)).astype(BF16)
            return carry

        lax.fori_loop(0, p.line, add, 0)
        self.line_start()

    def step3(self):
        p = self.p
        if self.line_first:
            self.across_copy().wait_recv()
            self.ctx_start((self.two[...].astype(F32) + self.one[p.z, p.y].astype(F32)).astype(BF16))
        else:
            self.ctx_start(self.line_sum())

    def step4(self):
        p = self.p
        for k in range(1, p.n // 2):
            self.ctx_copy(k).wait_recv()
        total = self.parts[0].astype(F32)
        for c in range(1, p.n // 2):
            total = total + self.parts[c].astype(F32)
        self.out[p.core] = total.astype(BF16)
        self.last_copy(p.core).start()

    def finish(self):
        p = self.p
        self.last_copy(1 - p.core).wait_recv()
        self.last_copy(p.core).wait_send()
        self.mate_copy().wait_send()
        self.across_copy().wait_send()
        for k in range(1, p.line):
            self.line_out(k).wait_send()
        for k in range(1, p.n // 2):
            self.ctx_copy(k).wait_send()


def reduce_scratch(shape, h, w, line_first, stored=True):
    line, n = shape["fsdp"] // 2, shape["ctx"]
    run = (line, 2, h, w) if line_first else (line, h, w)
    return [
        pltpu.VMEM((line, 2, h, w) if stored else (8, 128), BF16),
        pltpu.VMEM((line, 2, h, w), BF16),
        pltpu.VMEM((h, w) if line_first else (line, h, w), BF16),
        pltpu.VMEM(run, BF16),
        pltpu.VMEM((n // 2, h, w), BF16),
    ]


def reduce_sems(shape, channels):
    slots = 4 + shape["fsdp"] // 2 + shape["ctx"] // 2
    return [pltpu.SemaphoreType.DMA((channels, slots))] * 2


def halves(pair):
    low = lax.broadcasted_iota(jnp.int32, pair.shape, 1) < 64
    zero = jnp.zeros_like(pair)
    return jnp.concatenate([jnp.where(low, pair, zero), jnp.where(low, zero, pair)], axis=0)


def corner(both):
    return jnp.concatenate([both[0:64, 0:SPAN], both[64:128, SPAN : 2 * SPAN]], axis=0)


def turn(value):
    return value.astype(F32).T.astype(BF16)


class Agenda:
    def __init__(self, actions, places=None):
        self.plan = {}
        if places is None:
            for place, action in actions:
                self.plan.setdefault(place, []).append(action)
            return
        for i, action in enumerate(actions):
            self.plan.setdefault(i * places // len(actions), []).append(action)

    def at(self, place, index=None, count=1):
        if index is None:
            for action in self.plan.get(place, ()):
                action()
            return
        for k in range(count):
            if place + k in self.plan:

                @pl.when(index == k)
                def _(k=k):
                    for action in self.plan[place + k]:
                        action()


def front_kernel(shape, *refs):
    shards, x_hbm = refs[0:5], refs[5]
    wq_out, wo_out, wu_out, wd_out, norms_ref, mixed_out, prob_out, att_out, attt_out, normt_out, unit_out, far_ref, rstd_ref = refs[6:19]
    (x_ref, wq_ref, raw_ref, mixed_ref, prob_ref, att_ref, attt_ref, normt_ref, low_ref, own_ref, all_ref, fart_ref, bias_ref,
     gsend, grecv, glocal, ssend, srecv, nsend, nrecv, io_sem) = refs[19:]
    batches, tokens, _ = x_ref.shape
    spans = tokens // SPAN
    count = far_ref.shape[1]
    prompt = count // 2
    m = shape["fsdp"]
    width = D // m
    place = Place(shape)
    first = place.c * spans

    load = [pltpu.make_async_copy(x_hbm.at[b], x_ref.at[b], io_sem.at[0, b]) for b in range(batches)]
    for copy in load:
        copy.start()
    place.greet(pltpu.get_barrier_semaphore(), rows=True)
    norm_copies = []
    for k in range(1, m):
        where = {"ctx": place.c, "fsdp": (place.f + k) % m}
        norm_copies.append(remote(shards[1], raw_ref.at[place.f], nsend.at[k], nrecv.at[k], where))
        norm_copies[-1].start()
    sems = (gsend, grecv, glocal)
    soon = [Gather(place, shards[0], wq_ref, sems, c, pl.ds(c * D, D)) for c in (1, 2, 0)]
    later = [Gather(place, shards[i], full, sems, 1 + i) for i, full in ((2, wo_out), (3, wu_out), (4, wd_out))]
    steps = soon[0].steps()
    for part in soon:
        part.step(0)
    raw_ref[place.f] = shards[1][...]
    for copy in norm_copies:
        copy.wait()
    for f in range(m):
        norms_ref[0:4, f * width : (f + 1) * width] = raw_ref[f, 0:4, 0:width]
    gain = norms_ref[0:1, :]
    shift = norms_ref[2:3, :]
    key_id = lax.broadcasted_iota(jnp.int32, (SPAN, 2 * SPAN), 0)
    query_id = lax.broadcasted_iota(jnp.int32, (SPAN, 2 * SPAN), 1) & (SPAN - 1)
    for s in range(2):
        bias_ref[s, 0:SPAN, :] = jnp.where(key_id <= query_id, 0.0, NEG)

    norm_outs = lambda b: [
        pltpu.make_async_copy(normt_ref.at[b], normt_out.at[b], io_sem.at[1, b]),
        pltpu.make_async_copy(x_ref.at[b], unit_out.at[b], io_sem.at[7, b]),
    ]
    tile = 512
    tiles = tokens // tile
    step_of = lambda part, k: lambda: part.step(k)
    early = Agenda([lambda: None] * 2 + [lambda: [part.step(1) for part in soon]] + [lambda: None] * 2, batches * tiles)

    for b in range(batches):
        load[b].wait()

        def norm(i, carry, b=b):
            early.at(b * tiles, i, tiles)
            rows = pl.ds(pl.multiple_of(i * tile, tile), tile)
            unit, rstd = unit_of(x_ref[b, rows, :].astype(F32))
            low = (unit * gain + shift).astype(BF16)
            low_ref[b, rows, :] = low
            normt_ref[b, :, rows] = low.T
            x_ref[b, rows, :] = unit.astype(BF16)
            rstd_ref[b, rows, :] = rstd
            return carry

        lax.fori_loop(0, tiles, norm, 0)
        for copy in norm_outs(b):
            copy.start()

    def share(k):
        to = (place.c + k) % place.n
        return remote(own_ref, all_ref.at[place.c], ssend.at[k], srecv.at[k], {"ctx": to, "fsdp": place.f})

    def project(c):
        def body(i, carry):
            for b in range(batches):
                rows = pl.ds(pl.multiple_of(i * tile, tile), tile)
                part = nn(low_ref[b, rows, :], wq_ref[:, :, :, c * D : (c + 1) * D].reshape(D, D))
                if c == 0:
                    mixed_ref[b, rows, 0:D] = part.astype(BF16) * 0.125
                    continue
                mixed_ref[b, rows, c * D : (c + 1) * D] = part.astype(BF16)
                for s in range(tile // SPAN):
                    total = jnp.sum(part[s * SPAN : (s + 1) * SPAN, :], axis=0, keepdims=True) * SPAN ** (-0.5)
                    own_ref[b, pl.ds(i * (tile // SPAN) + s, 1), (c - 1) * D : c * D] = total.astype(BF16).astype(F32)
            return carry

        lax.fori_loop(0, tiles, body, 0)

    for k in range(2, steps):
        for part in soon:
            part.step(k)
    for part in later:
        part.step(0)
    soon[0].finish()
    project(1)
    soon[1].finish()
    project(2)
    for k in range(1, place.n):
        share(k).start()
    all_ref[place.c] = own_ref[...]
    later[0].step(1)
    soon[2].finish()
    project(0)
    later[1].step(1)
    pairs = spans // 2
    rest = Agenda(
        [step_of(later[2], 1)] + [step_of(part, k) for k in range(2, steps) for part in later],
        batches * pairs - LEAD,
    )
    weight_out = pltpu.make_async_copy(wq_ref, wq_out, io_sem.at[6, 0])
    weight_out.start()
    for k in range(1, place.n):
        share(k).wait()

    out_copies = lambda b: [
        pltpu.make_async_copy(src.at[b], dst.at[b], io_sem.at[2 + i, b])
        for i, (src, dst) in enumerate(
            ((mixed_ref, mixed_out), (prob_ref, prob_out), (att_ref, att_out), (attt_ref, attt_out))
        )
    ]

    for b in range(batches):
        out_copies(b)[0].start()
        for c in range(place.n):
            far_ref[b, c * spans : (c + 1) * spans, :] = all_ref[c, b].astype(BF16)
        fart_ref[...] = far_ref[b, :, D:].T

        def attend(i, carry, b=b):
            rest.at(b * pairs, i, pairs)
            for s in range(2):
                far_id = lax.broadcasted_iota(jnp.int32, (count, 2 * SPAN), 0)
                mine = first + i * 2 + s
                segment = (mine - prompt) >> 3
                seen = (far_id < mine) & ((far_id < prompt) | (((far_id - prompt) >> 3) == segment))
                bias_ref[s, SPAN:, :] = jnp.where(seen, 0.0, NEG)
            scores, probs = {}, {}
            items = [(s, p) for p in range(PAIRS) for s in range(2)]
            for t in range(len(items) + 2):
                if t < len(items):
                    s, p = items[t]
                    rows = pl.ds(pl.multiple_of(i * 2 * SPAN + s * SPAN, SPAN), SPAN)
                    lanes = slice(p * SPAN, (p + 1) * SPAN)
                    qs = halves(mixed_ref[b, rows, lanes])
                    keys = jnp.concatenate(
                        [mixed_ref[b, rows, D + p * SPAN : D + (p + 1) * SPAN], far_ref[b, :, lanes]], axis=0
                    )
                    scores[t] = nt(keys, qs)
                if 1 <= t <= len(items):
                    s, p = items[t - 1]
                    score = scores.pop(t - 1) + bias_ref[s]
                    score = jnp.exp(score - jnp.max(score, axis=0, keepdims=True))
                    prob = (score * (1.0 / jnp.sum(score, axis=0, keepdims=True))).astype(BF16)
                    prob_ref[b, i * 2 + s, p] = prob
                    probs[t - 1] = prob
                if t >= 2:
                    s, p = items[t - 2]
                    rows = pl.ds(pl.multiple_of(i * 2 * SPAN + s * SPAN, SPAN), SPAN)
                    lanes = slice(p * SPAN, (p + 1) * SPAN)
                    turned = mixed_ref[b, rows, 2 * D + p * SPAN : 2 * D + (p + 1) * SPAN].T
                    turned = jnp.concatenate([turned, fart_ref[lanes, :]], axis=1)
                    att = corner(nn(turned, probs.pop(t - 2))).astype(BF16)
                    attt_ref[b, lanes, rows] = att
                    att_ref[b, rows, lanes] = att.T
            return carry

        lax.fori_loop(0, pairs, attend, 0)
        for copy in out_copies(b)[1:]:
            copy.start()

    for part in later:
        part.finish()
    weight_out.wait()
    for b in range(batches):
        for copy in norm_outs(b) + out_copies(b):
            copy.wait()


def front_call(shape, shards, x):
    batches, tokens, _ = x.shape
    spans = tokens // SPAN
    n, m = shape["ctx"], shape["fsdp"]
    count = n * spans
    any_spec = pl.BlockSpec(memory_space=pl.ANY)
    vmem = pl.BlockSpec(memory_space=pltpu.VMEM)
    full = [jax.ShapeDtypeStruct((m,) + s.shape, s.dtype) for s in shards]
    big = [
        jax.ShapeDtypeStruct((batches, tokens, 3 * D), BF16),
        jax.ShapeDtypeStruct((batches, spans, PAIRS, SPAN + count, 2 * SPAN), BF16),
        jax.ShapeDtypeStruct((batches, tokens, D), BF16),
        jax.ShapeDtypeStruct((batches, D, tokens), BF16),
        jax.ShapeDtypeStruct((batches, D, tokens), BF16),
    ]
    return pl.pallas_call(
        functools.partial(front_kernel, shape),
        in_specs=[any_spec, vmem] + [any_spec] * 4,
        out_specs=[any_spec] * 4 + [vmem] + [any_spec] * 6 + [vmem] * 2,
        out_shape=[full[0], full[2], full[3], full[4], jax.ShapeDtypeStruct((8, D), F32)]
        + big
        + [
            jax.ShapeDtypeStruct(x.shape, BF16),
            jax.ShapeDtypeStruct((batches, count, 2 * D), BF16),
            jax.ShapeDtypeStruct((batches, tokens, 1), F32),
        ],
        scratch_shapes=[
            pltpu.VMEM((batches, tokens, D), BF16),
            pltpu.VMEM(full[0].shape, BF16),
            pltpu.VMEM(full[1].shape, F32),
        ]
        + [pltpu.VMEM(v.shape, v.dtype) for v in big]
        + [
            pltpu.VMEM((batches, tokens, D), BF16),
            pltpu.VMEM((batches, spans, 2 * D), F32),
            pltpu.VMEM((n, batches, spans, 2 * D), F32),
            pltpu.VMEM((D, count), BF16),
            pltpu.VMEM((2, SPAN + count, 2 * SPAN), F32),
        ]
        + gather_sems(m // 2, 6)
        + [
            pltpu.SemaphoreType.DMA((n,)),
            pltpu.SemaphoreType.DMA((n,)),
            pltpu.SemaphoreType.DMA((m,)),
            pltpu.SemaphoreType.DMA((m,)),
            pltpu.SemaphoreType.DMA((8, batches)),
        ],
        compiler_params=pltpu.CompilerParams(collective_id=0, has_side_effects=True, vmem_limit_bytes=VMEM_LIMIT),
        name="front",
    )(*shards, x)


def middle_kernel(shape, *refs):
    x_hbm, g_hbm, att_hbm, attt_hbm, wo_hbm, wu_hbm, wd_hbm, norms_ref = refs[0:8]
    out_hbm, gmid_hbm, da_hbm, go_ref, gu_ref, gd_ref, gu_sum, gd_sum, ggain_ref, gshift_ref = refs[8:18]
    (x_ref, att_ref, attt_ref, g_ref, n2_ref, n2t_ref, gt_ref, unit_ref, rstd_ref, acc_ref, gn2_ref, act_ref, gh_ref,
     wo_ref, wu_ref, wd_ref, goa_ref, gua_ref, gda_ref, gu_term, gd_term) = refs[18:39]
    bufs, sems, io_sem, w_sem = refs[39:47], refs[47:49], refs[49], refs[50]
    batches, tokens, _ = g_ref.shape
    m = shape["fsdp"]
    place = Place(shape)
    per = FF // m // UNIT
    group = UNIT * m
    tile = 512
    tiles = tokens // tile

    ins = lambda b: [
        pltpu.make_async_copy(src.at[b], dst, io_sem.at[i, b])
        for i, (src, dst) in enumerate(
            ((x_hbm, x_ref.at[b % 2]), (att_hbm, att_ref.at[b % 2]), (g_hbm, g_ref.at[b]))
        )
    ]
    turned = lambda b: pltpu.make_async_copy(attt_hbm.at[b], attt_ref.at[b % 2], io_sem.at[3, b])
    wo_copy = pltpu.make_async_copy(wo_hbm, wo_ref, io_sem.at[4, 0])
    weights = []
    for h in range(per):
        for f in range(m):
            src, dst = (f * per + h) * UNIT, h * group + f * UNIT
            weights.append(
                pltpu.make_async_copy(wu_hbm.at[:, pl.ds(src, UNIT)], wu_ref.at[:, pl.ds(dst, UNIT)], w_sem.at[0, h, f])
            )
            weights.append(
                pltpu.make_async_copy(wd_hbm.at[pl.ds(src, UNIT)], wd_ref.at[pl.ds(dst, UNIT)], w_sem.at[1, h, f])
            )
    wo_copy.start()
    for copy in ins(0):
        copy.start()
    for copy in weights:
        copy.start()
    early = per > 1
    if early:
        place.greet(pltpu.get_barrier_semaphore(), rows=True)
        gu = Reduce(place, gu_term, None, gu_sum, bufs[0:4], sems, 0, False)
        gd = Reduce(place, gd_term, None, gd_sum, bufs[4:8], sems, 1, False)
        chain = [(0, gu.step0), (0, gd.step0), (1, gu.step1), (1, gd.step1), (3, gu.step2), (4, gd.step2)]
        chain += [(6, gu.step3), (7, gd.step3), (9, gu.step4), (10, gd.step4)]
    gain = norms_ref[1:2, :]
    shift = norms_ref[3:4, :]

    wo_copy.wait()
    for b in range(batches):
        if b + 1 < batches:
            for copy in ins(b + 1):
                copy.start()
        for copy in ins(b):
            copy.wait()

        def before(i, carry, b=b):
            rows = pl.ds(pl.multiple_of(i * tile, tile), tile)
            middle = x_ref[b % 2, rows, :].astype(F32) + nn(att_ref[b % 2, rows, :], wo_ref[...])
            unit, rstd = unit_of(middle)
            low = (unit * gain + shift).astype(BF16)
            acc_ref[b, rows, :] = middle
            gn2_ref[b, rows, :] = jnp.zeros((tile, D), F32)
            unit_ref[b, rows, :] = unit.astype(BF16)
            rstd_ref[b, rows, :] = rstd
            n2_ref[b, rows, :] = low
            n2t_ref[b, :, rows] = low.T
            gt_ref[b, :, rows] = g_ref[b, rows, :].T
            return carry

        lax.fori_loop(0, tiles, before, 0)
    for copy in weights:
        copy.wait()
    wd_ref[...] = wd_ref[...] * 0.5
    act_ref[1] = jnp.zeros((tokens, CHUNK), BF16)
    gh_ref[1] = jnp.zeros((tokens, CHUNK), BF16)

    def wgrad(i):
        b = lax.rem(i, batches)
        slot = lax.rem(i, 2)
        keep = b > 0
        total = nn(n2t_ref[b], gh_ref[slot])
        gua_ref[...] = jnp.where(keep, gua_ref[...], 0.0) + total
        total = nn(gt_ref[b], act_ref[slot])
        gda_ref[...] = jnp.where(keep, gda_ref[...], 0.0) + total

    half = D // m // 2

    def close(c):
        h, base = c * CHUNK // group, c * CHUNK % group
        ups, downs = (gu_term, gd_term) if early and h == 0 else (gu_ref, gd_ref)

        def body(i, carry):
            for y in range(2):
                for s in range(2):
                    start = pl.multiple_of(((i * 2 + y) * 2 + s) * half, half)
                    ups[i, y, s, :, base : base + CHUNK] = gua_ref[pl.ds(start, half), :].astype(BF16)
            return carry

        lax.fori_loop(0, m // 2, body, 0)
        for k in range(CHUNK // UNIT):
            f = base // UNIT + k
            rows = (gda_ref[:, k * UNIT : (k + 1) * UNIT] * 0.5).astype(BF16).T
            downs[f // 2, f % 2, 0] = rows[0 : UNIT // 2]
            downs[f // 2, f % 2, 1] = rows[UNIT // 2 :]

    chunks = FF // CHUNK
    steps = chunks * batches
    opening = (chunks // per) * batches + 1 if early else steps
    agenda = Agenda(chain) if early else None

    def step(i, carry):
        for c in range(chunks - 1):

            @pl.when(i == (c + 1) * batches + 1)
            def _(c=c):
                close(c)

        if early:
            agenda.at(0, i - opening, steps - opening)
        c = lax.div(i, batches)
        b = lax.rem(i, batches)
        slot = lax.rem(i, 2)
        cols = pl.ds(pl.multiple_of(c * CHUNK, CHUNK), CHUNK)
        for r in range(1):
            rows = slice(0, tokens)
            act, slope = gelu_pair(nn(n2_ref[b, rows, :], wu_ref[:, cols]))
            act = act.astype(BF16)
            act_ref[slot, rows, :] = act
            grad = (nt(g_ref[b, rows, :], wd_ref[cols, :]) * slope).astype(BF16)
            gh_ref[slot, rows, :] = grad
            acc_ref[b, rows, :] += nn(act, wd_ref[cols, :])
            gn2_ref[b, rows, :] += nt(grad, wu_ref[:, cols])
            if r == 0:
                wgrad(i + steps * 2 - 1)
        return carry

    lax.fori_loop(0, steps, step, 0)
    wgrad(steps - 1)
    turned(0).start()
    close(chunks - 1)

    outs = lambda b: [
        pltpu.make_async_copy(src, dst.at[b], io_sem.at[5 + i, b])
        for i, (src, dst) in enumerate(((unit_ref.at[b], out_hbm), (g_ref.at[b], gmid_hbm), (n2_ref.at[b], da_hbm)))
    ]
    ggain_ref[...] = jnp.zeros_like(ggain_ref)
    gshift_ref[...] = jnp.zeros_like(gshift_ref)
    for b in range(batches):
        if b + 1 < batches:
            turned(b + 1).start()

        def after(i, carry, b=b):
            if early:
                agenda.at(steps - opening + b * tiles, i, tiles)
            rows = pl.ds(pl.multiple_of(i * tile, tile), tile)
            unit = unit_ref[b, rows, :].astype(F32)
            grad = gn2_ref[b, rows, :]
            ggain_ref[...] += fold8(grad * unit)
            gshift_ref[...] += fold8(grad)
            grad = g_ref[b, rows, :].astype(F32) + norm_back(grad, unit, rstd_ref[b, rows, :], gain)
            low = grad.astype(BF16)
            unit_ref[b, rows, :] = acc_ref[b, rows, :].astype(BF16)
            g_ref[b, rows, :] = low
            n2_ref[b, rows, :] = nt(low, wo_ref[...]).astype(BF16)
            return carry

        lax.fori_loop(0, tiles, after, 0)
        for copy in outs(b):
            copy.start()
        turned(b).wait()
        total = nn(attt_ref[b % 2], g_ref[b])
        goa_ref[...] = total if b == 0 else goa_ref[...] + total
    go_ref[...] = goa_ref[...].astype(BF16)
    if early:
        gu.finish()
        gd.finish()
    for b in range(batches):
        for copy in outs(b):
            copy.wait()


def middle_call(shape, x, g, att, attt, wo, wu, wd, norms):
    batches, tokens, _ = x.shape
    m = shape["fsdp"]
    line = m // 2
    group = UNIT * m
    any_spec = pl.BlockSpec(memory_space=pl.ANY)
    vmem = pl.BlockSpec(memory_space=pltpu.VMEM)
    up = (line, 2, 2, D // m // 2, group)
    down = (line, 2, 2, UNIT // 2, D)
    low = lambda *dims: jax.ShapeDtypeStruct(dims, BF16)
    seqs = lambda: pltpu.VMEM((batches, tokens, D), BF16)
    turned = lambda count: pltpu.VMEM((count, D, tokens), BF16)
    scratch = [
        pltpu.VMEM((2, tokens, D), BF16), pltpu.VMEM((2, tokens, D), BF16), turned(2), seqs(), seqs(), turned(batches),
        turned(batches), seqs(), pltpu.VMEM((batches, tokens, 1), F32), pltpu.VMEM((batches, tokens, D), F32),
        pltpu.VMEM((batches, tokens, D), F32), pltpu.VMEM((2, tokens, CHUNK), BF16), pltpu.VMEM((2, tokens, CHUNK), BF16),
        pltpu.VMEM((D, D), BF16), pltpu.VMEM((D, FF), BF16), pltpu.VMEM((FF, D), BF16),
        pltpu.VMEM((D, D), F32), pltpu.VMEM((D, CHUNK), F32), pltpu.VMEM((D, CHUNK), F32),
    ]
    early = FF // m // UNIT > 1
    small = (8, 128)
    scratch += [pltpu.VMEM(up if early else small, BF16), pltpu.VMEM(down if early else small, BF16)]
    for t in (up, down):
        if early:
            scratch += reduce_scratch(shape, *t[3:], False, False)[1:]
        else:
            scratch += [pltpu.VMEM(small, BF16)] * 4
    scratch += reduce_sems(shape, 2)
    scratch += [pltpu.SemaphoreType.DMA((8, batches)), pltpu.SemaphoreType.DMA((2, FF // m // UNIT, m))]
    return pl.pallas_call(
        functools.partial(middle_kernel, shape),
        in_specs=[any_spec] * 7 + [vmem],
        out_specs=[any_spec] * 3 + [vmem] * 7,
        out_shape=[
            low(*x.shape), low(*x.shape), low(*x.shape), low(D, D), low(*up), low(*down),
            low(*(up[2:] if early else small)), low(*(down[2:] if early else small)),
            jax.ShapeDtypeStruct((8, D), F32), jax.ShapeDtypeStruct((8, D), F32),
        ],
        scratch_shapes=scratch,
        compiler_params=pltpu.CompilerParams(
            collective_id=2 if early else None, has_side_effects=True, vmem_limit_bytes=VMEM_LIMIT
        ),
        name="middle",
    )(x, g, att, attt, wo, wu, wd, norms)


def back_kernel(shape, *refs):
    mixed_hbm, da_hbm, prob_hbm, unit_hbm, normt_hbm, gmid_hbm, wq_hbm, gu_hbm, gd_hbm, go_hbm = refs[0:10]
    far_ref, rstd_ref, norms_ref, gain2_ref, shift2_ref = refs[10:15]
    gin_out, gq_out, gk_out, gv_out, gu_out, gd_out, go_out, small_out = refs[15:23]
    (mixed_ref, da_ref, prob_ref, unit_ref, normt_ref, gmid_ref, wq_ref, dmixed_ref, gw_ref, gq_ref, gk_ref, gv_ref,
     far_t, dfar_ref, held_ref, gsum_ref, vec_ref, vecs_ref, vsum_ref, pieces_ref) = refs[23:43]
    bufs, sems = refs[43:73], refs[73:75]
    xsend, xrecv, vsend, vrecv, io_sem = refs[75:80]
    batches, tokens, _ = unit_ref.shape
    spans = tokens // SPAN
    count = far_ref.shape[1]
    m = shape["fsdp"]
    width = D // m
    place = Place(shape)

    ins = lambda b: [
        pltpu.make_async_copy(src.at[b], dst.at[b % 2], io_sem.at[i, b])
        for i, (src, dst) in enumerate(((mixed_hbm, mixed_ref), (da_hbm, da_ref), (prob_hbm, prob_ref)))
    ]
    rest = [
        pltpu.make_async_copy(src, dst, io_sem.at[4 + i, 0])
        for i, (src, dst) in enumerate(
            ((normt_hbm, normt_ref), (unit_hbm, unit_ref), (gmid_hbm, gmid_ref), (wq_hbm, wq_ref))
        )
    ]
    for copy in ins(0):
        copy.start()
    place.greet(pltpu.get_barrier_semaphore(), rows=True)
    channel = lambda i, term, out, line_first, stored: Reduce(
        place, term, bufs[5 * i] if stored else None, out, bufs[5 * i + 1 : 5 * i + 5], sems, i, line_first
    )
    gu = channel(0, gu_hbm, gu_out, False, True)
    gd = channel(1, gd_hbm, gd_out, False, True)
    go = channel(2, go_hbm, go_out, False, True)
    gq = channel(3, gq_ref, gq_out, False, False)
    gk = channel(4, gk_ref, gk_out, True, False)
    gv = channel(5, gv_ref, gv_out, False, False)
    for part in (gu, gd, go):
        part.step0()
    for copy in rest:
        copy.start()

    def swap(b, k):
        to = (place.c + k) % place.n
        source = dfar_ref.at[b, pl.ds(pl.multiple_of(to * spans, spans), spans)]
        return remote(source, held_ref.at[b, k], xsend.at[b, k], xrecv.at[b, k], {"ctx": to, "fsdp": place.f})

    pairs = spans // 2
    big = Agenda([(at, getattr(part, step)) for at, part, step in (
        (2, gu, "step1"), (3, gd, "step1"), (4, go, "step1"), (9, gu, "step2"), (15, gd, "step2"), (16, go, "step2"),
        (17, gu, "step3"), (20, gu, "step4"), (20, gq, "step1"), (21, gd, "step3"), (21, go, "step3"), (22, gk, "step1"),
        (22, gv, "step1"), (23, gq, "step2"), (24, gd, "step4"), (24, go, "step4"), (25, gv, "step2"), (26, gq, "step3"),
        (26, gk, "step2"), (27, gv, "step3"), (27, gk, "step3"), (27, gq, "step4"), (28, gv, "step4"), (28, gk, "step4"),
    )])

    def attend_back(b):
        slot = b % 2
        for copy in ins(b):
            copy.wait()
        if b + 1 < batches:
            for copy in ins(b + 1):
                copy.start()
        dfar_ref[b] = jnp.zeros((count, 2 * D), F32)
        far_t[...] = far_ref[b, :, 0:D].T
        base = b * (pairs + EXTRA)

        def body(i, carry):
            big.at(base, i, pairs)
            items = [(s, p) for p in range(PAIRS) for s in range(2)]
            held, grads = {}, {}
            where = lambda t: (
                pl.ds(pl.multiple_of(i * 2 * SPAN + items[t][0] * SPAN, SPAN), SPAN),
                *(slice(c * D + items[t][1] * SPAN, c * D + (items[t][1] + 1) * SPAN) for c in range(3)),
            )
            for t in range(len(items) + 2):
                if t < len(items):
                    rows, lanes, klanes, vlanes = where(t)
                    das = halves(da_ref[slot, rows, lanes])
                    values = jnp.concatenate([mixed_ref[slot, rows, vlanes], far_ref[b, :, klanes]], axis=0)
                    held[t] = (das, nt(values, das))
                if 1 <= t <= len(items):
                    rows, lanes, klanes, vlanes = where(t - 1)
                    das, slope = held.pop(t - 1)
                    low = prob_ref[slot, i * 2 + items[t - 1][0], items[t - 1][1]]
                    prob = low.astype(F32)
                    inner = jnp.sum(prob * slope, axis=0, keepdims=True)
                    grads[t - 1] = (prob * (slope - inner)).astype(BF16)
                    dv = nn(low, das)
                    dmixed_ref[b, rows, vlanes] = dv[0:SPAN].astype(BF16)
                    dfar_ref[b, :, klanes] += dv[SPAN:]
                if t >= 2:
                    rows, lanes, klanes, vlanes = where(t - 2)
                    grad = grads.pop(t - 2)
                    dk = nn(grad, halves(mixed_ref[slot, rows, lanes]))
                    dmixed_ref[b, rows, klanes] = dk[0:SPAN].astype(BF16)
                    dfar_ref[b, :, lanes] += dk[SPAN:]
                    turned = jnp.concatenate([mixed_ref[slot, rows, klanes].T, far_t[lanes, :]], axis=1)
                    dmixed_ref[b, rows, lanes] = (corner(nn(turned, grad)) * 0.125).astype(BF16).T
            return carry

        lax.fori_loop(0, pairs, body, 0)
        for k in range(1, place.n):
            swap(b, k).start()

    def wgrad(b, c):
        cols = slice(c * D, (c + 1) * D)
        part = nn(normt_ref[b], dmixed_ref[b, :, cols])
        gw_ref[:, cols] = part if b == 0 else gw_ref[:, cols] + part

    def spread(b):
        for k in range(1, place.n):
            swap(b, k).wait()
        total = dfar_ref[b, pl.ds(pl.multiple_of(place.c * spans, spans), spans), :]
        for k in range(1, place.n):
            total = total + held_ref[b, k]
        gsum_ref[...] = total * SPAN ** (-0.5)

        def body(s, carry):
            rows = pl.ds(pl.multiple_of(s * SPAN, SPAN), SPAN)
            extra = jnp.broadcast_to(gsum_ref[pl.ds(s, 1), :], (16, 2 * D)).astype(BF16)
            for r in range(SPAN // 16):
                at = pl.ds(pl.multiple_of(s * SPAN + r * 16, 16), 16)
                dmixed_ref[b, at, D:] = dmixed_ref[b, at, D:] + extra
            return carry

        lax.fori_loop(0, spans, body, 0)

    half = D // m // 2

    def low(dst, cols):
        def body(i, carry):
            for y in range(2):
                for s in range(2):
                    start = pl.multiple_of(((i * 2 + y) * 2 + s) * half, half)
                    dst[i, y, s] = gw_ref[pl.ds(start, half), cols].astype(BF16)
            return carry

        lax.fori_loop(0, m // 2, body, 0)

    for b in range(batches):
        attend_back(b)
        if b == 0:
            for copy in rest:
                copy.wait()
        base = b * (pairs + EXTRA) + pairs
        big.at(base)
        wgrad(b, 0)
        if b + 1 == batches:
            low(gq_ref, slice(0, D))
            gq.step0()
        big.at(base + 1)
        if b > 0:
            spread(b - 1)
            for c in (1, 2):
                wgrad(b - 1, c)
        big.at(base + 2)
    last = batches - 1
    spread(last)
    for c in (1, 2):
        wgrad(last, c)
    low(gk_ref, slice(D, 2 * D))
    low(gv_ref, slice(2 * D, 3 * D))
    gk.step0()
    gv.step0()

    gain = norms_ref[0:1, :]
    tile = 512
    tiles = tokens // tile
    late = batches * (pairs + EXTRA)
    gin_copy = lambda b: pltpu.make_async_copy(gmid_ref.at[b], gin_out.at[b], io_sem.at[3, b])
    gains_at = jnp.zeros((8, D), F32)
    shifts_at = jnp.zeros((8, D), F32)
    for b in range(batches):

        def data(i, carry, b=b):
            big.at(late + b * tiles, i, tiles)
            spots = [pl.ds(pl.multiple_of(i * tile + r * (tile // 2), tile // 2), tile // 2) for r in range(2)]
            grads = [nt(dmixed_ref[b, rows, :], wq_ref[...].reshape(D, 3 * D)) for rows in spots]
            gains_at, shifts_at = carry
            for rows, grad in zip(spots, grads):
                unit = unit_ref[b, rows, :].astype(F32)
                change = norm_back(grad, unit, rstd_ref[b, rows, :], gain)
                gmid_ref[b, rows, :] = (gmid_ref[b, rows, :].astype(F32) + change).astype(BF16)
                gains_at = gains_at + fold8(grad * unit)
                shifts_at = shifts_at + fold8(grad)
            return gains_at, shifts_at

        gains_at, shifts_at = lax.fori_loop(0, tiles, data, (gains_at, shifts_at))
        gin_copy(b).start()

    sums = [jnp.sum(v, axis=0, keepdims=True) for v in (gains_at, gain2_ref[...], shifts_at, shift2_ref[...])]
    vec_ref[...] = jnp.concatenate(sums + [jnp.zeros((4, D), F32)], axis=0)
    over_ctx = [
        remote(vec_ref, vecs_ref.at[k], vsend.at[0, k], vrecv.at[0, k], {"ctx": (place.c + k) % place.n, "fsdp": place.f})
        for k in range(1, place.n)
    ]
    for copy in over_ctx:
        copy.start()
    vecs_ref[0] = vec_ref[...]
    big.at(late + batches * tiles)
    for copy in over_ctx:
        copy.wait()
    total = jnp.zeros((8, D), F32)
    for c in range(place.n):
        total = total + vecs_ref[(place.c - c + place.n) % place.n]
    vsum_ref[...] = jnp.zeros_like(vsum_ref)
    for f in range(m):
        vsum_ref[f, :, 0:width] = total[:, f * width : (f + 1) * width]
    over_rows = []
    for k in range(1, m):
        to = (place.f + k) % m
        over_rows.append(
            remote(vsum_ref.at[to], pieces_ref.at[place.f], vsend.at[1, k], vrecv.at[1, k], {"ctx": place.c, "fsdp": to})
        )
        over_rows[-1].start()
    pieces_ref[place.f] = vsum_ref[place.f]
    big.at(late + batches * tiles + 1)
    for copy in over_rows:
        copy.wait()
    total = pieces_ref[0]
    for f in range(1, m):
        total = total + pieces_ref[f]
    small_out[...] = total
    for part in (gu, gd, go, gq, gk, gv):
        part.finish()
    for b in range(batches):
        gin_copy(b).wait()


def back_call(shape, mixed, da, prob, unit, normt, gmid, wq, gu, gd, go, far, rstd, norms, gain2, shift2):
    batches, tokens, _ = unit.shape
    spans = tokens // SPAN
    n, m = shape["ctx"], shape["fsdp"]
    line = m // 2
    count = n * spans
    any_spec = pl.BlockSpec(memory_space=pl.ANY)
    vmem = pl.BlockSpec(memory_space=pltpu.VMEM)
    halved = lambda rows, w: (line, 2, 2, rows // (2 * m), w)
    terms = [gu.shape, gd.shape, halved(D, D), halved(D, D), halved(D, D), halved(D, D)]
    go = go.reshape(terms[2])
    out = lambda t: jax.ShapeDtypeStruct(t[2:], BF16)
    two = lambda *dims: pltpu.VMEM((2,) + dims, BF16)
    scratch = [
        two(tokens, 3 * D), two(tokens, D), two(spans, PAIRS, SPAN + count, 2 * SPAN),
        pltpu.VMEM(unit.shape, BF16), pltpu.VMEM(normt.shape, BF16), pltpu.VMEM(unit.shape, BF16),
        pltpu.VMEM(wq.shape, BF16), pltpu.VMEM((batches, tokens, 3 * D), BF16), pltpu.VMEM((D, 3 * D), F32),
        pltpu.VMEM(terms[3], BF16), pltpu.VMEM(terms[4], BF16), pltpu.VMEM(terms[5], BF16),
        pltpu.VMEM((D, count), BF16), pltpu.VMEM((batches, count, 2 * D), F32),
        pltpu.VMEM((batches, n, spans, 2 * D), F32), pltpu.VMEM((spans, 2 * D), F32),
        pltpu.VMEM((8, D), F32), pltpu.VMEM((n, 8, D), F32), pltpu.VMEM((m, 8, 128), F32), pltpu.VMEM((m, 8, 128), F32),
    ]
    for t, line_first, stored in zip(terms, (False,) * 4 + (True, False), (True,) * 3 + (False,) * 3):
        scratch += reduce_scratch(shape, *t[3:], line_first, stored)
    scratch += reduce_sems(shape, 6)
    most = max(n, m)
    scratch += [
        pltpu.SemaphoreType.DMA((batches, n)), pltpu.SemaphoreType.DMA((batches, n)),
        pltpu.SemaphoreType.DMA((2, most)), pltpu.SemaphoreType.DMA((2, most)), pltpu.SemaphoreType.DMA((8, batches)),
    ]
    return pl.pallas_call(
        functools.partial(back_kernel, shape),
        in_specs=[any_spec] * 10 + [vmem] * 5,
        out_specs=[any_spec] + [vmem] * 7,
        out_shape=[
            jax.ShapeDtypeStruct(unit.shape, BF16), out(terms[3]), out(terms[4]), out(terms[5]), out(terms[0]),
            out(terms[1]), out(terms[2]), jax.ShapeDtypeStruct((8, 128), F32),
        ],
        scratch_shapes=scratch,
        compiler_params=pltpu.CompilerParams(collective_id=1, has_side_effects=True, vmem_limit_bytes=VMEM_LIMIT),
        name="back",
    )(mixed, da, prob, unit, normt, gmid, wq, gu, gd, go, far, rstd, norms, gain2, shift2)


def widen_kernel(per, *refs):
    go_ref = refs[3]
    gus, gds = refs[4 : 4 + per], refs[4 + per : 4 + 2 * per]
    qkv_out, out_out, up_out, down_out = refs[4 + 2 * per :]
    for c in range(3):
        qkv_out[:, c * D : (c + 1) * D] = refs[c][...].astype(F32)
    out_out[...] = go_ref[...].astype(F32)
    for h in range(per):
        for f in range(gus[h].shape[1] // UNIT):
            at = (f * per + h) * UNIT
            up_out[:, at : at + UNIT] = gus[h][:, f * UNIT : (f + 1) * UNIT].astype(F32)
        down_out[h * UNIT : (h + 1) * UNIT, :] = gds[h][...].astype(F32)


def widen_call(gq, gk, gv, go, gus, gds):
    per = len(gus)
    flat = [v.reshape(-1, v.shape[-1]) for v in (gq, gk, gv, go, *gus, *gds)]
    rows = flat[0].shape[0]
    shapes = ((rows, 3 * D), (rows, D), (rows, FF), (per * UNIT, D))
    return pl.pallas_call(
        functools.partial(widen_kernel, per),
        out_shape=[jax.ShapeDtypeStruct(v, F32) for v in shapes],
        name="widen",
    )(*flat)


def local(shape, x, g, qkv_weight, out_weight, up_weight, down_weight, norm_gains, norm_shifts):
    width = norm_gains.shape[1]
    norms = jnp.concatenate([norm_gains, norm_shifts], axis=0).astype(F32)
    norms = jnp.pad(norms, ((0, 4), (0, 128 - width)))
    halved = lambda shard: shard.reshape(2, shard.shape[0] // 2, shard.shape[1])
    shards = [halved(qkv_weight), norms, halved(out_weight), halved(up_weight), halved(down_weight)]
    wq, wo, wu, wd, norms, mixed, prob, att, attt, normt, unit, far, rstd = front_call(shape, shards, x)
    wo, wu, wd = (w.reshape(-1, w.shape[-1]) for w in (wo, wu, wd))
    out, gmid, da, go, gu, gd, gu_sum, gd_sum, gain2, shift2 = middle_call(shape, x, g, att, attt, wo, wu, wd, norms)
    gin, gq, gk, gv, gu, gd, go, small = back_call(
        shape, mixed, da, prob, unit, normt, gmid, wq, gu, gd, go, far, rstd, norms, gain2, shift2
    )
    early = FF // shape["fsdp"] // UNIT > 1
    gq, go, gu, gd = widen_call(gq, gk, gv, go, [gu_sum, gu] if early else [gu], [gd_sum, gd] if early else [gd])
    small = small[0:4, 0:width]
    return out, gin, gq, go, gu, gd, small[0:2], small[2], small[3]


def solution(mesh):
    weight, norm, token = P("fsdp", None), P(None, "fsdp"), P("fsdp", "ctx", None)
    return jax.shard_map(
        functools.partial(local, dict(mesh.shape)),
        mesh=mesh,
        in_specs=(token, token, weight, weight, weight, weight, norm, norm),
        out_specs=(token, token, weight, weight, weight, weight, norm, P("fsdp"), P("fsdp")),
        check_vma=False,
    )
```

```python
import functools

import jax
import jax.numpy as jnp
from jax import lax
from jax.experimental import pallas as pl
from jax.experimental.pallas import tpu as pltpu
from jax.sharding import PartitionSpec as P

D = 512
HEADS = 8
FF = 2048
SPAN = 128
CONT = 1024
PAIRS = HEADS // 2
CHUNK = 512
UNIT = 128
EXTRA = 3

EPS = 1e-05
NEG = -1e30
F32 = jnp.float32
BF16 = jnp.bfloat16
VMEM_LIMIT = 60 * 1024 * 1024


def nn(a, b):
    return lax.dot_general(a, b, (((1,), (0,)), ((), ())), preferred_element_type=F32)


def nt(a, b):
    return lax.dot_general(a, b, (((1,), (1,)), ((), ())), preferred_element_type=F32)


def unit_of(values):
    center = values - jnp.mean(values, axis=-1, keepdims=True)
    rstd = lax.rsqrt(jnp.mean(center * center, axis=-1, keepdims=True) + EPS)
    return center * rstd, rstd


def norm_back(grad, unit, rstd, gain):
    scaled = grad * gain
    return rstd * (
        scaled
        - jnp.mean(scaled, axis=-1, keepdims=True)
        - unit * jnp.mean(scaled * unit, axis=-1, keepdims=True)
    )


def fold8(values):
    rows = values.shape[0]
    return jnp.sum(values.reshape(rows // 8, 8, values.shape[1]), axis=0)


def gelu_pair(x):
    cdf = lax.erf(x * 0.7071067811865476) + 1.0
    slope = jnp.exp2(x * x * (-0.5 * 1.4426950408889634)) * (x * 0.7978845608028654)
    return x * cdf, cdf + slope


MESH = pl.DeviceIdType.MESH


class Place:
    def __init__(self, mesh_shape):
        self.n, self.m = mesh_shape["ctx"], mesh_shape["fsdp"]
        self.inner = 2
        self.line = self.m // 2
        self.c, self.f = lax.axis_index("ctx"), lax.axis_index("fsdp")
        self.core = self.c % 2
        self.z, self.y = self.f // 2, self.f % 2

    def mate(self):
        return {"ctx": self.c + 1 - 2 * self.core, "fsdp": self.f}

    def across(self):
        return {"ctx": self.c, "fsdp": self.z * 2 + 1 - self.y}

    def along(self, step):
        return {"ctx": self.c, "fsdp": self.f + 2 * step}

    def greet(self, barrier, rows=False):
        signal = lambda where: pl.semaphore_signal(barrier, inc=1, device_id=where, device_id_type=MESH)
        for k in range(1, self.n):
            signal({"ctx": (self.c + k) % self.n, "fsdp": self.f})
        count = self.n - 1
        if rows:
            for k in range(1, self.m):
                signal({"ctx": self.c, "fsdp": (self.f + k) % self.m})
            count = count + self.m - 1
        else:
            signal(self.across())
            up = self.z < self.line - 1
            down = self.z > 0

            @pl.when(up)
            def _():
                signal(self.along(1))

            @pl.when(down)
            def _():
                signal(self.along(-1))

            count = count + 1 + up.astype(jnp.int32) + down.astype(jnp.int32)
        pl.semaphore_wait(barrier, count)


def remote(src, dst, send, recv, where):
    return pltpu.make_async_remote_copy(
        src_ref=src, dst_ref=dst, send_sem=send, recv_sem=recv, device_id=where, device_id_type=MESH
    )


class Gather:
    def __init__(self, place, shard, full, sems, channel, cols=slice(None), split=False):
        self.p, self.shard, self.full, self.cols = place, shard, full, cols
        self.send, self.recv, self.local = sems
        self.ch = channel
        self.split = split and place.n % 4 == 0
        self.part = (place.c // 2) % 2

    def rows(self, other=False):
        if not self.split:
            return slice(None)
        size = self.shard.shape[1] // 2
        part = 1 - self.part if other else self.part
        return pl.ds(pl.multiple_of(part * size, size), size)

    def copy(self, place, source, kind, index, where):
        sems = self.send.at[self.ch, kind, index], self.recv.at[self.ch, kind, index]
        return remote(place if source is None else source, place, *sems, where)

    def piece(self, j, y, core, other=False):
        return self.full.at[j * 2 + y, core, self.rows(other), self.cols]

    def source(self):
        return self.shard.at[self.p.core, self.rows(), self.cols]

    def behind(self, k):
        return (self.p.z + self.p.line - k) % self.p.line

    def line_out(self, k):
        p = self.p
        j = (p.z + k) % p.line
        return self.copy(self.piece(p.z, p.y, p.core), self.source(), 0, k, {"ctx": p.c, "fsdp": j * 2 + p.y})

    def across(self, k):
        p = self.p
        source = self.source() if k == 0 else None
        return self.copy(self.piece(self.behind(k), p.y, p.core), source, 1, k, p.across())

    def mate(self, k, same, core, other=False):
        p = self.p
        y = p.y if same else 1 - p.y
        kind = (2 if same else 3) + (4 if other else 0)
        return self.copy(self.piece(self.behind(k), y, core, other), None, kind, k, p.mate())

    def chip(self, k, same, other=False):
        p = self.p
        y = p.y if same else 1 - p.y
        where = {"ctx": p.c + 2 - 4 * self.part, "fsdp": p.f}
        return self.copy(self.piece(self.behind(k), y, p.core, other), None, 4 if same else 5, k, where)

    def own(self):
        return pltpu.make_async_copy(
            self.shard.at[:, :, self.cols], self.full.at[self.p.f, :, :, self.cols], self.local.at[self.ch]
        )

    def start(self):
        self.own().start()
        for k in range(1, self.p.line):
            self.line_out(k).start()

    def start_across(self):
        self.across(0).start()

    def line_in(self, *ks):
        p = self.p
        for k in ks or range(1, p.line):
            self.line_out(k).wait_recv()
            self.across(k).start()
            if self.split:
                self.chip(k, True).start()
            self.mate(k, True, p.core).start()

    def across_in(self, *ks):
        p = self.p
        for k in ks or range(p.line):
            self.across(k).wait_recv()
            if self.split:
                self.chip(k, False).start()
            self.mate(k, False, p.core).start()

    def chip_in(self, *ks):
        p = self.p
        for k in ks or range(p.line):
            for same in (True, False)[k == 0 :]:
                self.chip(k, same, True).wait_recv()
                self.mate(k, same, p.core, True).start()

    def finish(self):
        p = self.p
        self.own().wait()
        for k in range(p.line):
            if k:
                self.line_out(k).wait_send()
            self.across(k).wait_send()
            for same in (True, False)[k == 0 :]:
                for other in (False, True)[: 1 + self.split]:
                    self.mate(k, same, 1 - p.core, other).wait_recv()
                    self.mate(k, same, p.core, other).wait_send()
                if self.split:
                    self.chip(k, same).wait_send()


def gather_sems(place_line, channels):
    return [
        pltpu.SemaphoreType.DMA((channels, 8, place_line)),
        pltpu.SemaphoreType.DMA((channels, 8, place_line)),
        pltpu.SemaphoreType.DMA((channels,)),
    ]


class Reduce:
    def __init__(self, place, term, mine, out, bufs, sems, channel, line_first):
        self.p, self.term, self.mine, self.out = place, term, mine, out
        self.one, self.two, self.ins, self.parts = bufs
        self.send, self.recv = sems
        self.ch, self.line_first = channel, line_first

    def copy(self, src, dst, slot, where, back=None):
        back = slot if back is None else back
        return remote(src, dst, self.send.at[self.ch, slot], self.recv.at[self.ch, back], where)

    def mate_copy(self):
        p = self.p
        return self.copy(self.term.at[:, :, 1 - p.core], self.one, 0, p.mate())

    def mine_copy(self):
        return pltpu.make_async_copy(self.term.at[:, :, self.p.core], self.mine, self.send.at[self.ch, 2])

    def across_copy(self):
        p = self.p
        source = self.one.at[p.z, 1 - p.y] if self.line_first else self.one.at[:, 1 - p.y]
        return self.copy(source, self.two, 1, p.across())

    def line_out(self, k):
        p = self.p
        j = (p.z + k) % p.line
        source = self.one if self.line_first else self.two
        return self.copy(source.at[j], self.ins.at[k], 4 + k, {"ctx": p.c, "fsdp": j * 2 + p.y})

    def ctx_copy(self, k):
        p = self.p
        where = {"ctx": (p.c + 2 * k) % p.n, "fsdp": p.f}
        mine = self.parts.at[p.c // 2]
        return self.copy(mine, mine, 4 + p.line + k, where)

    def last_copy(self, core):
        return self.copy(self.out.at[core], self.out.at[core], 3, self.p.mate())

    def step0(self):
        self.mate_copy().start()
        if self.mine is not None:
            self.mine_copy().start()

    def from_mate(self):
        p = self.p
        if self.mine is not None:
            self.mine_copy().wait()
        self.mate_copy().wait_recv()

        def add(i, carry):
            for y in range(2):
                own = self.term[i, y, p.core] if self.mine is None else self.mine[i, y]
                self.one[i, y] = (self.one[i, y].astype(F32) + own.astype(F32)).astype(BF16)
            return carry

        lax.fori_loop(0, p.line, add, 0)

    def line_start(self):
        for k in range(1, self.p.line):
            self.line_out(k).start()

    def line_sum(self):
        p = self.p
        total = (self.one if self.line_first else self.two)[p.z].astype(F32)
        for k in range(1, p.line):
            self.line_out(k).wait_recv()
            total = total + self.ins[k].astype(F32)
        return total.astype(BF16)

    def ctx_start(self, value):
        p = self.p
        self.parts[p.c // 2] = value
        for k in range(1, p.n // 2):
            self.ctx_copy(k).start()

    def step1(self):
        self.from_mate()
        if self.line_first:
            self.line_start()
        else:
            self.across_copy().start()

    def step2(self):
        p = self.p
        if self.line_first:
            self.one[p.z] = self.line_sum()
            self.across_copy().start()
            return
        self.across_copy().wait_recv()

        def add(i, carry):
            self.two[i] = (self.two[i].astype(F32) + self.one[i, p.y].astype(F32)).astype(BF16)
            return carry

        lax.fori_loop(0, p.line, add, 0)
        self.line_start()

    def step3(self):
        p = self.p
        if self.line_first:
            self.across_copy().wait_recv()
            self.ctx_start((self.two[...].astype(F32) + self.one[p.z, p.y].astype(F32)).astype(BF16))
        else:
            self.ctx_start(self.line_sum())

    def step4(self):
        p = self.p
        for k in range(1, p.n // 2):
            self.ctx_copy(k).wait_recv()
        total = self.parts[0].astype(F32)
        for c in range(1, p.n // 2):
            total = total + self.parts[c].astype(F32)
        self.out[p.core] = total.astype(BF16)
        self.last_copy(p.core).start()

    def finish(self):
        p = self.p
        self.last_copy(1 - p.core).wait_recv()
        self.last_copy(p.core).wait_send()
        self.mate_copy().wait_send()
        self.across_copy().wait_send()
        for k in range(1, p.line):
            self.line_out(k).wait_send()
        for k in range(1, p.n // 2):
            self.ctx_copy(k).wait_send()


def reduce_scratch(shape, h, w, line_first, stored=True):
    line, n = shape["fsdp"] // 2, shape["ctx"]
    run = (line, 2, h, w) if line_first else (line, h, w)
    return [
        pltpu.VMEM((line, 2, h, w) if stored else (8, 128), BF16),
        pltpu.VMEM((line, 2, h, w), BF16),
        pltpu.VMEM((h, w) if line_first else (line, h, w), BF16),
        pltpu.VMEM(run, BF16),
        pltpu.VMEM((n // 2, h, w), BF16),
    ]


def reduce_sems(shape, channels):
    slots = 4 + shape["fsdp"] // 2 + shape["ctx"] // 2
    return [pltpu.SemaphoreType.DMA((channels, slots))] * 2


def halves(pair):
    low = lax.broadcasted_iota(jnp.int32, pair.shape, 1) < 64
    zero = jnp.zeros_like(pair)
    return jnp.concatenate([jnp.where(low, pair, zero), jnp.where(low, zero, pair)], axis=0)


def corner(both):
    return jnp.concatenate([both[0:64, 0:SPAN], both[64:128, SPAN : 2 * SPAN]], axis=0)


def turn(value):
    return value.astype(F32).T.astype(BF16)


class Agenda:
    def __init__(self, actions, places=None):
        self.plan = {}
        if places is None:
            for place, action in actions:
                self.plan.setdefault(place, []).append(action)
            return
        for i, action in enumerate(actions):
            self.plan.setdefault(i * places // len(actions), []).append(action)

    def at(self, place, index=None, count=1):
        if index is None:
            for action in self.plan.get(place, ()):
                action()
            return
        for k in range(count):
            if place + k in self.plan:

                @pl.when(index == k)
                def _(k=k):
                    for action in self.plan[place + k]:
                        action()


def front_kernel(shape, *refs):
    shards, x_hbm = refs[0:6], refs[6]
    wq_out, wo_out, wu_out, wd_out, norms_ref, mixed_out, prob_out, att_out, attt_out, normt_out, unit_out, far_ref, rstd_ref = refs[7:20]
    (x_ref, wq_ref, raw_ref, mixed_ref, prob_ref, att_ref, attt_ref, normt_ref, low_ref, own_ref, all_ref, fart_ref, bias_ref, norm_ref,
     gsend, grecv, glocal, ssend, srecv, nsend, nrecv, io_sem) = refs[20:]
    batches, tokens, _ = x_ref.shape
    spans = tokens // SPAN
    count = far_ref.shape[1]
    prompt = count // 2
    m = shape["fsdp"]
    width = D // m
    place = Place(shape)
    first = place.c * spans

    load = [pltpu.make_async_copy(x_hbm.at[b], x_ref.at[b], io_sem.at[0, b]) for b in range(batches)]
    for copy in load:
        copy.start()
    place.greet(pltpu.get_barrier_semaphore(), rows=True)
    norm_copies = []
    norm_ref[...] = jnp.zeros_like(norm_ref)
    for i in range(2):
        norm_ref[2 * i : 2 * i + 2, 0:width] = shards[4 + i][...].astype(F32)
    for k in range(1, m):
        where = {"ctx": place.c, "fsdp": (place.f + k) % m}
        norm_copies.append(remote(norm_ref, raw_ref.at[place.f], nsend.at[k], nrecv.at[k], where))
        norm_copies[-1].start()
    sems = (gsend, grecv, glocal)
    soon = [Gather(place, shards[0], wq_ref, sems, c, pl.ds(c * D, D)) for c in (1, 2, 0)]
    wo, wu, wd = (
        Gather(place, shards[i], full, sems, 2 + i, split=i == 3) for i, full in ((1, wo_out), (2, wu_out), (3, wd_out))
    )
    later = (wd, wo, wu)
    for part in soon:
        part.start()
        part.start_across()
    raw_ref[place.f] = norm_ref[...]
    for copy in norm_copies:
        copy.wait()
    for f in range(m):
        norms_ref[0:4, f * width : (f + 1) * width] = raw_ref[f, 0:4, 0:width]
    gain = norms_ref[0:1, :]
    shift = norms_ref[2:3, :]
    key_id = lax.broadcasted_iota(jnp.int32, (SPAN, 2 * SPAN), 0)
    query_id = lax.broadcasted_iota(jnp.int32, (SPAN, 2 * SPAN), 1) & (SPAN - 1)
    for s in range(2):
        bias_ref[s, 0:SPAN, :] = jnp.where(key_id <= query_id, 0.0, NEG)

    norm_outs = lambda b: [
        pltpu.make_async_copy(normt_ref.at[b], normt_out.at[b], io_sem.at[1, b]),
        pltpu.make_async_copy(x_ref.at[b], unit_out.at[b], io_sem.at[7, b]),
    ]
    tile = 512
    tiles = tokens // tile
    far_ones = range(2, place.line)
    plan = Agenda([
        (3, soon[0].line_in), (7, soon[1].across_in), (9, soon[2].across_in), (10, wd.line_in), (11, wo.line_in),
        (14, lambda: wu.line_in(1)), (14, lambda: wo.across_in()), (15, wd.across_in), (15, lambda: wu.across_in(0)),
        (17, lambda: wu.line_in(*far_ones)), (18, lambda: wu.across_in(1)), (19, wd.chip_in),
        (22, lambda: wu.across_in(*far_ones)),
    ])

    for b in range(batches):
        load[b].wait()

        def norm(i, carry, b=b):
            plan.at(b * tiles, i, tiles)
            rows = pl.ds(pl.multiple_of(i * tile, tile), tile)
            unit, rstd = unit_of(x_ref[b, rows, :].astype(F32))
            low = (unit * gain + shift).astype(BF16)
            low_ref[b, rows, :] = low
            normt_ref[b, :, rows] = low.T
            x_ref[b, rows, :] = unit.astype(BF16)
            rstd_ref[b, rows, :] = rstd
            return carry

        lax.fori_loop(0, tiles, norm, 0)
        for copy in norm_outs(b):
            copy.start()

    def share(k):
        to = (place.c + k) % place.n
        return remote(own_ref, all_ref.at[place.c], ssend.at[k], srecv.at[k], {"ctx": to, "fsdp": place.f})

    def project(c, at):
        def body(i, carry):
            plan.at(at, i, tiles)
            for b in range(batches):
                rows = pl.ds(pl.multiple_of(i * tile, tile), tile)
                part = nn(low_ref[b, rows, :], wq_ref[:, :, :, c * D : (c + 1) * D].reshape(D, D))
                if c == 0:
                    mixed_ref[b, rows, 0:D] = part.astype(BF16) * 0.125
                    continue
                mixed_ref[b, rows, c * D : (c + 1) * D] = part.astype(BF16)
                for s in range(tile // SPAN):
                    total = jnp.sum(part[s * SPAN : (s + 1) * SPAN, :], axis=0, keepdims=True) * SPAN ** (-0.5)
                    own_ref[b, pl.ds(i * (tile // SPAN) + s, 1), (c - 1) * D : c * D] = total.astype(BF16).astype(F32)
            return carry

        lax.fori_loop(0, tiles, body, 0)

    soon[1].line_in()
    soon[0].across_in()
    soon[2].line_in()
    for part in later:
        part.start()
        part.start_across()
    soon[0].finish()
    project(1, 6)
    soon[1].finish()
    project(2, 8)
    for k in range(1, place.n):
        share(k).start()
    all_ref[place.c] = own_ref[...]
    soon[2].finish()
    project(0, 10)
    pairs = spans // 2
    weight_out = pltpu.make_async_copy(wq_ref, wq_out, io_sem.at[6, 0])
    weight_out.start()
    for k in range(1, place.n):
        share(k).wait()

    out_copies = lambda b: [
        pltpu.make_async_copy(src.at[b], dst.at[b], io_sem.at[2 + i, b])
        for i, (src, dst) in enumerate(
            ((mixed_ref, mixed_out), (prob_ref, prob_out), (att_ref, att_out), (attt_ref, attt_out))
        )
    ]

    for b in range(batches):
        out_copies(b)[0].start()
        for c in range(place.n):
            far_ref[b, c * spans : (c + 1) * spans, :] = all_ref[c, b].astype(BF16)
        fart_ref[...] = far_ref[b, :, D:].T

        def attend(i, carry, b=b):
            plan.at(12 + b * pairs, i, pairs)
            for s in range(2):
                far_id = lax.broadcasted_iota(jnp.int32, (count, 2 * SPAN), 0)
                mine = first + i * 2 + s
                segment = (mine - prompt) >> 3
                seen = (far_id < mine) & ((far_id < prompt) | (((far_id - prompt) >> 3) == segment))
                bias_ref[s, SPAN:, :] = jnp.where(seen, 0.0, NEG)
            scores, probs = {}, {}
            items = [(s, p) for p in range(PAIRS) for s in range(2)]
            for t in range(len(items) + 2):
                if t < len(items):
                    s, p = items[t]
                    rows = pl.ds(pl.multiple_of(i * 2 * SPAN + s * SPAN, SPAN), SPAN)
                    lanes = slice(p * SPAN, (p + 1) * SPAN)
                    qs = halves(mixed_ref[b, rows, lanes])
                    keys = jnp.concatenate(
                        [mixed_ref[b, rows, D + p * SPAN : D + (p + 1) * SPAN], far_ref[b, :, lanes]], axis=0
                    )
                    scores[t] = nt(keys, qs)
                if 1 <= t <= len(items):
                    s, p = items[t - 1]
                    score = scores.pop(t - 1) + bias_ref[s]
                    score = jnp.exp(score - jnp.max(score, axis=0, keepdims=True))
                    prob = (score * (1.0 / jnp.sum(score, axis=0, keepdims=True))).astype(BF16)
                    prob_ref[b, i * 2 + s, p] = prob
                    probs[t - 1] = prob
                if t >= 2:
                    s, p = items[t - 2]
                    rows = pl.ds(pl.multiple_of(i * 2 * SPAN + s * SPAN, SPAN), SPAN)
                    lanes = slice(p * SPAN, (p + 1) * SPAN)
                    turned = mixed_ref[b, rows, 2 * D + p * SPAN : 2 * D + (p + 1) * SPAN].T
                    turned = jnp.concatenate([turned, fart_ref[lanes, :]], axis=1)
                    att = corner(nn(turned, probs.pop(t - 2))).astype(BF16)
                    attt_ref[b, lanes, rows] = att
                    att_ref[b, rows, lanes] = att.T
            return carry

        lax.fori_loop(0, pairs, attend, 0)
        for copy in out_copies(b)[1:]:
            copy.start()

    for part in later:
        part.finish()
    weight_out.wait()
    for b in range(batches):
        for copy in norm_outs(b) + out_copies(b):
            copy.wait()


def front_call(shape, shards, x):
    batches, tokens, _ = x.shape
    spans = tokens // SPAN
    n, m = shape["ctx"], shape["fsdp"]
    count = n * spans
    any_spec = pl.BlockSpec(memory_space=pl.ANY)
    vmem = pl.BlockSpec(memory_space=pltpu.VMEM)
    full = [jax.ShapeDtypeStruct((m,) + s.shape, s.dtype) for s in shards[0:4]]
    big = [
        jax.ShapeDtypeStruct((batches, tokens, 3 * D), BF16),
        jax.ShapeDtypeStruct((batches, spans, PAIRS, SPAN + count, 2 * SPAN), BF16),
        jax.ShapeDtypeStruct((batches, tokens, D), BF16),
        jax.ShapeDtypeStruct((batches, D, tokens), BF16),
        jax.ShapeDtypeStruct((batches, D, tokens), BF16),
    ]
    return pl.pallas_call(
        functools.partial(front_kernel, shape),
        in_specs=[any_spec] * 4 + [vmem] * 2 + [any_spec],
        out_specs=[any_spec] * 4 + [vmem] + [any_spec] * 6 + [vmem] * 2,
        out_shape=full + [jax.ShapeDtypeStruct((8, D), F32)]
        + big
        + [
            jax.ShapeDtypeStruct(x.shape, BF16),
            jax.ShapeDtypeStruct((batches, count, 2 * D), BF16),
            jax.ShapeDtypeStruct((batches, tokens, 1), F32),
        ],
        scratch_shapes=[
            pltpu.VMEM((batches, tokens, D), BF16),
            pltpu.VMEM(full[0].shape, BF16),
            pltpu.VMEM((m, 8, 128), F32),
        ]
        + [pltpu.VMEM(v.shape, v.dtype) for v in big]
        + [
            pltpu.VMEM((batches, tokens, D), BF16),
            pltpu.VMEM((batches, spans, 2 * D), F32),
            pltpu.VMEM((n, batches, spans, 2 * D), F32),
            pltpu.VMEM((D, count), BF16),
            pltpu.VMEM((2, SPAN + count, 2 * SPAN), F32),
            pltpu.VMEM((8, 128), F32),
        ]
        + gather_sems(m // 2, 6)
        + [
            pltpu.SemaphoreType.DMA((n,)),
            pltpu.SemaphoreType.DMA((n,)),
            pltpu.SemaphoreType.DMA((m,)),
            pltpu.SemaphoreType.DMA((m,)),
            pltpu.SemaphoreType.DMA((8, batches)),
        ],
        compiler_params=pltpu.CompilerParams(collective_id=0, has_side_effects=True, vmem_limit_bytes=VMEM_LIMIT),
        name="front",
    )(*shards, x)


def middle_kernel(shape, *refs):
    x_hbm, g_hbm, att_hbm, attt_hbm, wo_hbm, wu_hbm, wd_hbm, norms_ref = refs[0:8]
    out_hbm, gmid_hbm, da_hbm, go_ref, gu_ref, gd_ref, gu_sum, gd_sum, ggain_ref, gshift_ref = refs[8:18]
    (x_ref, att_ref, attt_ref, g_ref, n2_ref, n2t_ref, gt_ref, unit_ref, rstd_ref, acc_ref, gn2_ref, act_ref, gh_ref,
     wo_ref, wu_ref, wd_ref, goa_ref, gua_ref, gda_ref, gu_term, gd_term) = refs[18:39]
    bufs, sems, io_sem, w_sem = refs[39:47], refs[47:49], refs[49], refs[50]
    batches, tokens, _ = g_ref.shape
    m = shape["fsdp"]
    place = Place(shape)
    per = FF // m // UNIT
    group = UNIT * m
    tile = 512
    tiles = tokens // tile

    ins = lambda b: [
        pltpu.make_async_copy(src.at[b], dst, io_sem.at[i, b])
        for i, (src, dst) in enumerate(
            ((x_hbm, x_ref.at[b % 2]), (att_hbm, att_ref.at[b % 2]), (g_hbm, g_ref.at[b]))
        )
    ]
    turned = lambda b: pltpu.make_async_copy(attt_hbm.at[b], attt_ref.at[b % 2], io_sem.at[3, b])
    wo_copy = pltpu.make_async_copy(wo_hbm, wo_ref, io_sem.at[4, 0])
    weights = []
    for h in range(per):
        for f in range(m):
            src, dst = (f * per + h) * UNIT, h * group + f * UNIT
            weights.append(
                pltpu.make_async_copy(wu_hbm.at[:, pl.ds(src, UNIT)], wu_ref.at[:, pl.ds(dst, UNIT)], w_sem.at[0, h, f])
            )
            weights.append(
                pltpu.make_async_copy(wd_hbm.at[pl.ds(src, UNIT)], wd_ref.at[pl.ds(dst, UNIT)], w_sem.at[1, h, f])
            )
    wo_copy.start()
    for copy in ins(0):
        copy.start()
    for copy in weights:
        copy.start()
    early = per > 1
    if early:
        place.greet(pltpu.get_barrier_semaphore(), rows=True)
        gu = Reduce(place, gu_term, None, gu_sum, bufs[0:4], sems, 0, False)
        gd = Reduce(place, gd_term, None, gd_sum, bufs[4:8], sems, 1, False)
        chain = [(0, gu.step0), (0, gd.step0), (1, gu.step1), (1, gd.step1), (3, gu.step2), (4, gd.step2)]
        chain += [(6, gu.step3), (7, gd.step3), (9, gu.step4), (10, gd.step4)]
    gain = norms_ref[1:2, :]
    shift = norms_ref[3:4, :]

    wo_copy.wait()
    for b in range(batches):
        if b + 1 < batches:
            for copy in ins(b + 1):
                copy.start()
        for copy in ins(b):
            copy.wait()

        def before(i, carry, b=b):
            rows = pl.ds(pl.multiple_of(i * tile, tile), tile)
            middle = x_ref[b % 2, rows, :].astype(F32) + nn(att_ref[b % 2, rows, :], wo_ref[...])
            unit, rstd = unit_of(middle)
            low = (unit * gain + shift).astype(BF16)
            acc_ref[b, rows, :] = middle
            gn2_ref[b, rows, :] = jnp.zeros((tile, D), F32)
            unit_ref[b, rows, :] = unit.astype(BF16)
            rstd_ref[b, rows, :] = rstd
            n2_ref[b, rows, :] = low
            n2t_ref[b, :, rows] = low.T
            gt_ref[b, :, rows] = g_ref[b, rows, :].T
            return carry

        lax.fori_loop(0, tiles, before, 0)
    for copy in weights:
        copy.wait()
    wd_ref[...] = wd_ref[...] * 0.5
    act_ref[1] = jnp.zeros((tokens, CHUNK), BF16)
    gh_ref[1] = jnp.zeros((tokens, CHUNK), BF16)

    def wgrad(i):
        b = lax.rem(i, batches)
        slot = lax.rem(i, 2)
        keep = b > 0
        total = nn(n2t_ref[b], gh_ref[slot])
        gua_ref[...] = jnp.where(keep, gua_ref[...], 0.0) + total
        total = nn(gt_ref[b], act_ref[slot])
        gda_ref[...] = jnp.where(keep, gda_ref[...], 0.0) + total

    half = D // m // 2

    def close(c):
        h, base = c * CHUNK // group, c * CHUNK % group
        ups, downs = (gu_term, gd_term) if early and h == 0 else (gu_ref, gd_ref)

        def body(i, carry):
            for y in range(2):
                for s in range(2):
                    start = pl.multiple_of(((i * 2 + y) * 2 + s) * half, half)
                    ups[i, y, s, :, base : base + CHUNK] = gua_ref[pl.ds(start, half), :].astype(BF16)
            return carry

        lax.fori_loop(0, m // 2, body, 0)
        for k in range(CHUNK // UNIT):
            f = base // UNIT + k
            rows = (gda_ref[:, k * UNIT : (k + 1) * UNIT] * 0.5).astype(BF16).T
            downs[f // 2, f % 2, 0] = rows[0 : UNIT // 2]
            downs[f // 2, f % 2, 1] = rows[UNIT // 2 :]

    chunks = FF // CHUNK
    steps = chunks * batches
    opening = (chunks // per) * batches + 1 if early else steps
    agenda = Agenda(chain) if early else None

    def step(i, carry):
        for c in range(chunks - 1):

            @pl.when(i == (c + 1) * batches + 1)
            def _(c=c):
                close(c)

        if early:
            agenda.at(0, i - opening, steps - opening)
        c = lax.div(i, batches)
        b = lax.rem(i, batches)
        slot = lax.rem(i, 2)
        cols = pl.ds(pl.multiple_of(c * CHUNK, CHUNK), CHUNK)
        for r in range(1):
            rows = slice(0, tokens)
            act, slope = gelu_pair(nn(n2_ref[b, rows, :], wu_ref[:, cols]))
            act = act.astype(BF16)
            act_ref[slot, rows, :] = act
            grad = (nt(g_ref[b, rows, :], wd_ref[cols, :]) * slope).astype(BF16)
            gh_ref[slot, rows, :] = grad
            acc_ref[b, rows, :] += nn(act, wd_ref[cols, :])
            gn2_ref[b, rows, :] += nt(grad, wu_ref[:, cols])
            if r == 0:
                wgrad(i + steps * 2 - 1)
        return carry

    lax.fori_loop(0, steps, step, 0)
    wgrad(steps - 1)
    turned(0).start()
    close(chunks - 1)

    outs = lambda b: [
        pltpu.make_async_copy(src, dst.at[b], io_sem.at[5 + i, b])
        for i, (src, dst) in enumerate(((unit_ref.at[b], out_hbm), (g_ref.at[b], gmid_hbm), (n2_ref.at[b], da_hbm)))
    ]
    ggain_ref[...] = jnp.zeros_like(ggain_ref)
    gshift_ref[...] = jnp.zeros_like(gshift_ref)
    for b in range(batches):
        if b + 1 < batches:
            turned(b + 1).start()

        def after(i, carry, b=b):
            if early:
                agenda.at(steps - opening + b * tiles, i, tiles)
            rows = pl.ds(pl.multiple_of(i * tile, tile), tile)
            unit = unit_ref[b, rows, :].astype(F32)
            grad = gn2_ref[b, rows, :]
            ggain_ref[...] += fold8(grad * unit)
            gshift_ref[...] += fold8(grad)
            grad = g_ref[b, rows, :].astype(F32) + norm_back(grad, unit, rstd_ref[b, rows, :], gain)
            low = grad.astype(BF16)
            unit_ref[b, rows, :] = acc_ref[b, rows, :].astype(BF16)
            g_ref[b, rows, :] = low
            n2_ref[b, rows, :] = nt(low, wo_ref[...]).astype(BF16)
            return carry

        lax.fori_loop(0, tiles, after, 0)
        for copy in outs(b):
            copy.start()
        turned(b).wait()
        total = nn(attt_ref[b % 2], g_ref[b])
        goa_ref[...] = total if b == 0 else goa_ref[...] + total
    go_ref[...] = goa_ref[...].astype(BF16)
    if early:
        gu.finish()
        gd.finish()
    for b in range(batches):
        for copy in outs(b):
            copy.wait()


def middle_call(shape, x, g, att, attt, wo, wu, wd, norms):
    batches, tokens, _ = x.shape
    m = shape["fsdp"]
    line = m // 2
    group = UNIT * m
    any_spec = pl.BlockSpec(memory_space=pl.ANY)
    vmem = pl.BlockSpec(memory_space=pltpu.VMEM)
    up = (line, 2, 2, D // m // 2, group)
    down = (line, 2, 2, UNIT // 2, D)
    low = lambda *dims: jax.ShapeDtypeStruct(dims, BF16)
    seqs = lambda: pltpu.VMEM((batches, tokens, D), BF16)
    turned = lambda count: pltpu.VMEM((count, D, tokens), BF16)
    scratch = [
        pltpu.VMEM((2, tokens, D), BF16), pltpu.VMEM((2, tokens, D), BF16), turned(2), seqs(), seqs(), turned(batches),
        turned(batches), seqs(), pltpu.VMEM((batches, tokens, 1), F32), pltpu.VMEM((batches, tokens, D), F32),
        pltpu.VMEM((batches, tokens, D), F32), pltpu.VMEM((2, tokens, CHUNK), BF16), pltpu.VMEM((2, tokens, CHUNK), BF16),
        pltpu.VMEM((D, D), BF16), pltpu.VMEM((D, FF), BF16), pltpu.VMEM((FF, D), BF16),
        pltpu.VMEM((D, D), F32), pltpu.VMEM((D, CHUNK), F32), pltpu.VMEM((D, CHUNK), F32),
    ]
    early = FF // m // UNIT > 1
    small = (8, 128)
    scratch += [pltpu.VMEM(up if early else small, BF16), pltpu.VMEM(down if early else small, BF16)]
    for t in (up, down):
        if early:
            scratch += reduce_scratch(shape, *t[3:], False, False)[1:]
        else:
            scratch += [pltpu.VMEM(small, BF16)] * 4
    scratch += reduce_sems(shape, 2)
    scratch += [pltpu.SemaphoreType.DMA((8, batches)), pltpu.SemaphoreType.DMA((2, FF // m // UNIT, m))]
    return pl.pallas_call(
        functools.partial(middle_kernel, shape),
        in_specs=[any_spec] * 7 + [vmem],
        out_specs=[any_spec] * 3 + [vmem] * 7,
        out_shape=[
            low(*x.shape), low(*x.shape), low(*x.shape), low(D, D), low(*up), low(*down),
            low(*(up[2:] if early else small)), low(*(down[2:] if early else small)),
            jax.ShapeDtypeStruct((8, D), F32), jax.ShapeDtypeStruct((8, D), F32),
        ],
        scratch_shapes=scratch,
        compiler_params=pltpu.CompilerParams(
            collective_id=2 if early else None, has_side_effects=True, vmem_limit_bytes=VMEM_LIMIT
        ),
        name="middle",
    )(x, g, att, attt, wo, wu, wd, norms)


def back_kernel(shape, *refs):
    mixed_hbm, da_hbm, prob_hbm, unit_hbm, normt_hbm, gmid_hbm, wq_hbm, gu_hbm, gd_hbm, go_hbm = refs[0:10]
    far_ref, rstd_ref, norms_ref, gain2_ref, shift2_ref = refs[10:15]
    gin_out, gq_out, gk_out, gv_out, gu_out, gd_out, go_out, small_out = refs[15:23]
    (mixed_ref, da_ref, prob_ref, unit_ref, normt_ref, gmid_ref, wq_ref, dmixed_ref, gw_ref, gq_ref, gk_ref, gv_ref,
     far_t, dfar_ref, held_ref, gsum_ref, vec_ref, vecs_ref, vsum_ref, pieces_ref) = refs[23:43]
    bufs, sems = refs[43:73], refs[73:75]
    xsend, xrecv, vsend, vrecv, io_sem = refs[75:80]
    batches, tokens, _ = unit_ref.shape
    spans = tokens // SPAN
    count = far_ref.shape[1]
    m = shape["fsdp"]
    width = D // m
    place = Place(shape)

    ins = lambda b: [
        pltpu.make_async_copy(src.at[b], dst.at[b % 2], io_sem.at[i, b])
        for i, (src, dst) in enumerate(((mixed_hbm, mixed_ref), (da_hbm, da_ref), (prob_hbm, prob_ref)))
    ]
    rest = [
        pltpu.make_async_copy(src, dst, io_sem.at[4 + i, 0])
        for i, (src, dst) in enumerate(
            ((normt_hbm, normt_ref), (unit_hbm, unit_ref), (gmid_hbm, gmid_ref), (wq_hbm, wq_ref))
        )
    ]
    for copy in ins(0):
        copy.start()
    place.greet(pltpu.get_barrier_semaphore(), rows=True)
    channel = lambda i, term, out, line_first, stored: Reduce(
        place, term, bufs[5 * i] if stored else None, out, bufs[5 * i + 1 : 5 * i + 5], sems, i, line_first
    )
    gu = channel(0, gu_hbm, gu_out, False, True)
    gd = channel(1, gd_hbm, gd_out, False, True)
    go = channel(2, go_hbm, go_out, False, True)
    gq = channel(3, gq_ref, gq_out, False, False)
    gk = channel(4, gk_ref, gk_out, True, False)
    gv = channel(5, gv_ref, gv_out, False, False)
    for part in (gu, gd, go):
        part.step0()
    for copy in rest:
        copy.start()

    def swap(b, k):
        to = (place.c + k) % place.n
        source = dfar_ref.at[b, pl.ds(pl.multiple_of(to * spans, spans), spans)]
        return remote(source, held_ref.at[b, k], xsend.at[b, k], xrecv.at[b, k], {"ctx": to, "fsdp": place.f})

    pairs = spans // 2
    big = Agenda([(at, getattr(part, step)) for at, part, step in (
        (2, gu, "step1"), (3, gd, "step1"), (4, go, "step1"), (10, gu, "step2"), (16, gd, "step2"), (17, go, "step2"),
        (19, gu, "step3"), (20, gq, "step1"), (21, gu, "step4"), (23, gd, "step3"), (23, go, "step3"), (22, gk, "step1"),
        (22, gv, "step1"), (23, gq, "step2"), (25, gd, "step4"), (25, go, "step4"), (25, gv, "step2"), (26, gq, "step3"),
        (26, gk, "step2"), (27, gv, "step3"), (27, gk, "step3"), (27, gq, "step4"), (28, gv, "step4"), (28, gk, "step4"),
    )])

    def attend_back(b):
        slot = b % 2
        for copy in ins(b):
            copy.wait()
        if b + 1 < batches:
            for copy in ins(b + 1):
                copy.start()
        dfar_ref[b] = jnp.zeros((count, 2 * D), F32)
        far_t[...] = far_ref[b, :, 0:D].T
        base = b * (pairs + EXTRA)

        def body(i, carry):
            big.at(base, i, pairs)
            items = [(s, p) for p in range(PAIRS) for s in range(2)]
            held, grads = {}, {}
            where = lambda t: (
                pl.ds(pl.multiple_of(i * 2 * SPAN + items[t][0] * SPAN, SPAN), SPAN),
                *(slice(c * D + items[t][1] * SPAN, c * D + (items[t][1] + 1) * SPAN) for c in range(3)),
            )
            for t in range(len(items) + 2):
                if t < len(items):
                    rows, lanes, klanes, vlanes = where(t)
                    das = halves(da_ref[slot, rows, lanes])
                    values = jnp.concatenate([mixed_ref[slot, rows, vlanes], far_ref[b, :, klanes]], axis=0)
                    held[t] = (das, nt(values, das))
                if 1 <= t <= len(items):
                    rows, lanes, klanes, vlanes = where(t - 1)
                    das, slope = held.pop(t - 1)
                    low = prob_ref[slot, i * 2 + items[t - 1][0], items[t - 1][1]]
                    prob = low.astype(F32)
                    inner = jnp.sum(prob * slope, axis=0, keepdims=True)
                    grads[t - 1] = (prob * (slope - inner)).astype(BF16)
                    dv = nn(low, das)
                    dmixed_ref[b, rows, vlanes] = dv[0:SPAN].astype(BF16)
                    dfar_ref[b, :, klanes] += dv[SPAN:]
                if t >= 2:
                    rows, lanes, klanes, vlanes = where(t - 2)
                    grad = grads.pop(t - 2)
                    dk = nn(grad, halves(mixed_ref[slot, rows, lanes]))
                    dmixed_ref[b, rows, klanes] = dk[0:SPAN].astype(BF16)
                    dfar_ref[b, :, lanes] += dk[SPAN:]
                    turned = jnp.concatenate([mixed_ref[slot, rows, klanes].T, far_t[lanes, :]], axis=1)
                    dmixed_ref[b, rows, lanes] = (corner(nn(turned, grad)) * 0.125).astype(BF16).T
            return carry

        lax.fori_loop(0, pairs, body, 0)
        for k in range(1, place.n):
            swap(b, k).start()

    def wgrad(b, c):
        cols = slice(c * D, (c + 1) * D)
        part = nn(normt_ref[b], dmixed_ref[b, :, cols])
        gw_ref[:, cols] = part if b == 0 else gw_ref[:, cols] + part

    def spread(b):
        for k in range(1, place.n):
            swap(b, k).wait()
        total = dfar_ref[b, pl.ds(pl.multiple_of(place.c * spans, spans), spans), :]
        for k in range(1, place.n):
            total = total + held_ref[b, k]
        gsum_ref[...] = total * SPAN ** (-0.5)

        def body(s, carry):
            rows = pl.ds(pl.multiple_of(s * SPAN, SPAN), SPAN)
            extra = jnp.broadcast_to(gsum_ref[pl.ds(s, 1), :], (16, 2 * D)).astype(BF16)
            for r in range(SPAN // 16):
                at = pl.ds(pl.multiple_of(s * SPAN + r * 16, 16), 16)
                dmixed_ref[b, at, D:] = dmixed_ref[b, at, D:] + extra
            return carry

        lax.fori_loop(0, spans, body, 0)

    half = D // m // 2

    def low(dst, cols):
        def body(i, carry):
            for y in range(2):
                for s in range(2):
                    start = pl.multiple_of(((i * 2 + y) * 2 + s) * half, half)
                    dst[i, y, s] = gw_ref[pl.ds(start, half), cols].astype(BF16)
            return carry

        lax.fori_loop(0, m // 2, body, 0)

    for b in range(batches):
        attend_back(b)
        if b == 0:
            for copy in rest:
                copy.wait()
        base = b * (pairs + EXTRA) + pairs
        big.at(base)
        wgrad(b, 0)
        if b + 1 == batches:
            low(gq_ref, slice(0, D))
            gq.step0()
        big.at(base + 1)
        if b > 0:
            spread(b - 1)
            for c in (1, 2):
                wgrad(b - 1, c)
        big.at(base + 2)
    last = batches - 1
    spread(last)
    for c in (1, 2):
        wgrad(last, c)
    low(gk_ref, slice(D, 2 * D))
    low(gv_ref, slice(2 * D, 3 * D))
    gk.step0()
    gv.step0()

    gain = norms_ref[0:1, :]
    tile = 512
    tiles = tokens // tile
    late = batches * (pairs + EXTRA)
    gin_copy = lambda b: pltpu.make_async_copy(gmid_ref.at[b], gin_out.at[b], io_sem.at[3, b])
    gains_at = jnp.zeros((8, D), F32)
    shifts_at = jnp.zeros((8, D), F32)
    for b in range(batches):

        def data(i, carry, b=b):
            big.at(late + b * tiles, i, tiles)
            spots = [pl.ds(pl.multiple_of(i * tile + r * (tile // 2), tile // 2), tile // 2) for r in range(2)]
            grads = [nt(dmixed_ref[b, rows, :], wq_ref[...].reshape(D, 3 * D)) for rows in spots]
            gains_at, shifts_at = carry
            for rows, grad in zip(spots, grads):
                unit = unit_ref[b, rows, :].astype(F32)
                change = norm_back(grad, unit, rstd_ref[b, rows, :], gain)
                gmid_ref[b, rows, :] = (gmid_ref[b, rows, :].astype(F32) + change).astype(BF16)
                gains_at = gains_at + fold8(grad * unit)
                shifts_at = shifts_at + fold8(grad)
            return gains_at, shifts_at

        gains_at, shifts_at = lax.fori_loop(0, tiles, data, (gains_at, shifts_at))
        gin_copy(b).start()

    sums = [jnp.sum(v, axis=0, keepdims=True) for v in (gains_at, gain2_ref[...], shifts_at, shift2_ref[...])]
    vec_ref[...] = jnp.concatenate(sums + [jnp.zeros((4, D), F32)], axis=0)
    over_ctx = [
        remote(vec_ref, vecs_ref.at[k], vsend.at[0, k], vrecv.at[0, k], {"ctx": (place.c + k) % place.n, "fsdp": place.f})
        for k in range(1, place.n)
    ]
    for copy in over_ctx:
        copy.start()
    vecs_ref[0] = vec_ref[...]
    big.at(late + batches * tiles)
    for copy in over_ctx:
        copy.wait()
    total = jnp.zeros((8, D), F32)
    for c in range(place.n):
        total = total + vecs_ref[(place.c - c + place.n) % place.n]
    vsum_ref[...] = jnp.zeros_like(vsum_ref)
    for f in range(m):
        vsum_ref[f, :, 0:width] = total[:, f * width : (f + 1) * width]
    over_rows = []
    for k in range(1, m):
        to = (place.f + k) % m
        over_rows.append(
            remote(vsum_ref.at[to], pieces_ref.at[place.f], vsend.at[1, k], vrecv.at[1, k], {"ctx": place.c, "fsdp": to})
        )
        over_rows[-1].start()
    pieces_ref[place.f] = vsum_ref[place.f]
    big.at(late + batches * tiles + 1)
    for copy in over_rows:
        copy.wait()
    total = pieces_ref[0]
    for f in range(1, m):
        total = total + pieces_ref[f]
    small_out[...] = total
    for part in (gu, gd, go, gq, gk, gv):
        part.finish()
    for b in range(batches):
        gin_copy(b).wait()


def back_call(shape, mixed, da, prob, unit, normt, gmid, wq, gu, gd, go, far, rstd, norms, gain2, shift2):
    batches, tokens, _ = unit.shape
    spans = tokens // SPAN
    n, m = shape["ctx"], shape["fsdp"]
    line = m // 2
    count = n * spans
    any_spec = pl.BlockSpec(memory_space=pl.ANY)
    vmem = pl.BlockSpec(memory_space=pltpu.VMEM)
    halved = lambda rows, w: (line, 2, 2, rows // (2 * m), w)
    terms = [gu.shape, gd.shape, halved(D, D), halved(D, D), halved(D, D), halved(D, D)]
    go = go.reshape(terms[2])
    out = lambda t: jax.ShapeDtypeStruct(t[2:], BF16)
    two = lambda *dims: pltpu.VMEM((2,) + dims, BF16)
    scratch = [
        two(tokens, 3 * D), two(tokens, D), two(spans, PAIRS, SPAN + count, 2 * SPAN),
        pltpu.VMEM(unit.shape, BF16), pltpu.VMEM(normt.shape, BF16), pltpu.VMEM(unit.shape, BF16),
        pltpu.VMEM(wq.shape, BF16), pltpu.VMEM((batches, tokens, 3 * D), BF16), pltpu.VMEM((D, 3 * D), F32),
        pltpu.VMEM(terms[3], BF16), pltpu.VMEM(terms[4], BF16), pltpu.VMEM(terms[5], BF16),
        pltpu.VMEM((D, count), BF16), pltpu.VMEM((batches, count, 2 * D), F32),
        pltpu.VMEM((batches, n, spans, 2 * D), F32), pltpu.VMEM((spans, 2 * D), F32),
        pltpu.VMEM((8, D), F32), pltpu.VMEM((n, 8, D), F32), pltpu.VMEM((m, 8, 128), F32), pltpu.VMEM((m, 8, 128), F32),
    ]
    for t, line_first, stored in zip(terms, (False,) * 4 + (True, False), (True,) * 3 + (False,) * 3):
        scratch += reduce_scratch(shape, *t[3:], line_first, stored)
    scratch += reduce_sems(shape, 6)
    most = max(n, m)
    scratch += [
        pltpu.SemaphoreType.DMA((batches, n)), pltpu.SemaphoreType.DMA((batches, n)),
        pltpu.SemaphoreType.DMA((2, most)), pltpu.SemaphoreType.DMA((2, most)), pltpu.SemaphoreType.DMA((8, batches)),
    ]
    return pl.pallas_call(
        functools.partial(back_kernel, shape),
        in_specs=[any_spec] * 10 + [vmem] * 5,
        out_specs=[any_spec] + [vmem] * 7,
        out_shape=[
            jax.ShapeDtypeStruct(unit.shape, BF16), out(terms[3]), out(terms[4]), out(terms[5]), out(terms[0]),
            out(terms[1]), out(terms[2]), jax.ShapeDtypeStruct((8, 128), F32),
        ],
        scratch_shapes=scratch,
        compiler_params=pltpu.CompilerParams(collective_id=1, has_side_effects=True, vmem_limit_bytes=VMEM_LIMIT),
        name="back",
    )(mixed, da, prob, unit, normt, gmid, wq, gu, gd, go, far, rstd, norms, gain2, shift2)


def widen_kernel(per, *refs):
    small_ref, go_ref = refs[0], refs[4]
    gus, gds = refs[5 : 5 + per], refs[5 + per : 5 + 2 * per]
    qkv_out, out_out, up_out, down_out, gain_out, first_out, second_out = refs[5 + 2 * per :]
    for c in range(3):
        qkv_out[:, c * D : (c + 1) * D] = refs[1 + c][...].astype(F32)
    out_out[...] = go_ref[...].astype(F32)
    for h in range(per):
        for f in range(gus[h].shape[1] // UNIT):
            at = (f * per + h) * UNIT
            up_out[:, at : at + UNIT] = gus[h][:, f * UNIT : (f + 1) * UNIT].astype(F32)
        down_out[h * UNIT : (h + 1) * UNIT, :] = gds[h][...].astype(F32)
    width = gain_out.shape[1]
    gain_out[...] = small_ref[0:2, 0:width]
    first_out[...] = small_ref[2, 0:width]
    second_out[...] = small_ref[3, 0:width]


def widen_call(width, small, gq, gk, gv, go, gus, gds):
    per = len(gus)
    flat = [small] + [v.reshape(-1, v.shape[-1]) for v in (gq, gk, gv, go, *gus, *gds)]
    rows = flat[1].shape[0]
    wide = lambda *dims: jax.ShapeDtypeStruct(dims, F32)
    return pl.pallas_call(
        functools.partial(widen_kernel, per),
        out_shape=[
            wide(rows, 3 * D), wide(rows, D), wide(rows, FF), wide(per * UNIT, D), wide(2, width), wide(width), wide(width)
        ],
        name="widen",
    )(*flat)


def local(shape, x, g, qkv_weight, out_weight, up_weight, down_weight, norm_gains, norm_shifts):
    width = norm_gains.shape[1]
    halved = lambda shard: shard.reshape(2, shard.shape[0] // 2, shard.shape[1])
    shards = [halved(v) for v in (qkv_weight, out_weight, up_weight, down_weight)] + [norm_gains, norm_shifts]
    wq, wo, wu, wd, norms, mixed, prob, att, attt, normt, unit, far, rstd = front_call(shape, shards, x)
    wo, wu, wd = (w.reshape(-1, w.shape[-1]) for w in (wo, wu, wd))
    out, gmid, da, go, gu, gd, gu_sum, gd_sum, gain2, shift2 = middle_call(shape, x, g, att, attt, wo, wu, wd, norms)
    gin, gq, gk, gv, gu, gd, go, small = back_call(
        shape, mixed, da, prob, unit, normt, gmid, wq, gu, gd, go, far, rstd, norms, gain2, shift2
    )
    early = FF // shape["fsdp"] // UNIT > 1
    gus, gds = ([gu_sum, gu], [gd_sum, gd]) if early else ([gu], [gd])
    return out, gin, *widen_call(width, small, gq, gk, gv, go, gus, gds)


def solution(mesh):
    weight, norm, token = P("fsdp", None), P(None, "fsdp"), P("fsdp", "ctx", None)
    return jax.shard_map(
        functools.partial(local, dict(mesh.shape)),
        mesh=mesh,
        in_specs=(token, token, weight, weight, weight, weight, norm, norm),
        out_specs=(token, token, weight, weight, weight, weight, norm, P("fsdp"), P("fsdp")),
        check_vma=False,
    )
```

```python
import functools

import jax
import jax.numpy as jnp
from jax import lax
from jax.experimental import pallas as pl
from jax.experimental.pallas import tpu as pltpu
from jax.sharding import PartitionSpec as P

D = 512
HEADS = 8
FF = 2048
SPAN = 128
CONT = 1024
PAIRS = HEADS // 2
CHUNK = 512
UNIT = 128
EXTRA = 3
GU = (3, 12, 20, 22)
GD = (5, 18, 25, 27)
GO = (6, 19, 25, 27)
GQ = (21, 24, 26, 28)
GK = (22, 27, 27, 28)
GV = (22, 26, 27, 28)

EPS = 1e-05
NEG = -1e30
F32 = jnp.float32
BF16 = jnp.bfloat16
VMEM_LIMIT = 60 * 1024 * 1024


def nn(a, b):
    return lax.dot_general(a, b, (((1,), (0,)), ((), ())), preferred_element_type=F32)


def nt(a, b):
    return lax.dot_general(a, b, (((1,), (1,)), ((), ())), preferred_element_type=F32)


def unit_of(values):
    center = values - jnp.mean(values, axis=-1, keepdims=True)
    rstd = lax.rsqrt(jnp.mean(center * center, axis=-1, keepdims=True) + EPS)
    return center * rstd, rstd


def norm_back(grad, unit, rstd, gain):
    scaled = grad * gain
    return rstd * (
        scaled
        - jnp.mean(scaled, axis=-1, keepdims=True)
        - unit * jnp.mean(scaled * unit, axis=-1, keepdims=True)
    )


def fold8(values):
    rows = values.shape[0]
    return jnp.sum(values.reshape(rows // 8, 8, values.shape[1]), axis=0)


def gelu_pair(x):
    cdf = lax.erf(x * 0.7071067811865476) + 1.0
    slope = jnp.exp2(x * x * (-0.5 * 1.4426950408889634)) * (x * 0.7978845608028654)
    return x * cdf, cdf + slope


MESH = pl.DeviceIdType.MESH


class Place:
    def __init__(self, mesh_shape):
        self.n, self.m = mesh_shape["ctx"], mesh_shape["fsdp"]
        self.inner = 2
        self.line = self.m // 2
        self.c, self.f = lax.axis_index("ctx"), lax.axis_index("fsdp")
        self.core = self.c % 2
        self.z, self.y = self.f // 2, self.f % 2

    def mate(self):
        return {"ctx": self.c + 1 - 2 * self.core, "fsdp": self.f}

    def across(self):
        return {"ctx": self.c, "fsdp": self.z * 2 + 1 - self.y}

    def along(self, step):
        return {"ctx": self.c, "fsdp": self.f + 2 * step}

    def greet(self, barrier, rows=False):
        signal = lambda where: pl.semaphore_signal(barrier, inc=1, device_id=where, device_id_type=MESH)
        for k in range(1, self.n):
            signal({"ctx": (self.c + k) % self.n, "fsdp": self.f})
        count = self.n - 1
        if rows:
            for k in range(1, self.m):
                signal({"ctx": self.c, "fsdp": (self.f + k) % self.m})
            count = count + self.m - 1
        else:
            signal(self.across())
            up = self.z < self.line - 1
            down = self.z > 0

            @pl.when(up)
            def _():
                signal(self.along(1))

            @pl.when(down)
            def _():
                signal(self.along(-1))

            count = count + 1 + up.astype(jnp.int32) + down.astype(jnp.int32)
        pl.semaphore_wait(barrier, count)


def remote(src, dst, send, recv, where):
    return pltpu.make_async_remote_copy(
        src_ref=src, dst_ref=dst, send_sem=send, recv_sem=recv, device_id=where, device_id_type=MESH
    )


class Gather:
    def __init__(self, place, shard, full, sems, channel, cols=slice(None), split=False):
        self.p, self.shard, self.full, self.cols = place, shard, full, cols
        self.send, self.recv, self.local = sems
        self.ch = channel
        self.split = split and place.n % 4 == 0
        self.part = (place.c // 2) % 2

    def rows(self, other=False):
        if not self.split:
            return slice(None)
        size = self.shard.shape[1] // 2
        part = 1 - self.part if other else self.part
        return pl.ds(pl.multiple_of(part * size, size), size)

    def copy(self, place, source, kind, index, where):
        sems = self.send.at[self.ch, kind, index], self.recv.at[self.ch, kind, index]
        return remote(place if source is None else source, place, *sems, where)

    def piece(self, j, y, core, other=False):
        return self.full.at[j * 2 + y, core, self.rows(other), self.cols]

    def source(self):
        return self.shard.at[self.p.core, self.rows(), self.cols]

    def behind(self, k):
        return (self.p.z + self.p.line - k) % self.p.line

    def line_out(self, k):
        p = self.p
        j = (p.z + k) % p.line
        return self.copy(self.piece(p.z, p.y, p.core), self.source(), 0, k, {"ctx": p.c, "fsdp": j * 2 + p.y})

    def across(self, k):
        p = self.p
        source = self.source() if k == 0 else None
        return self.copy(self.piece(self.behind(k), p.y, p.core), source, 1, k, p.across())

    def mate(self, k, same, core, other=False):
        p = self.p
        y = p.y if same else 1 - p.y
        kind = (2 if same else 3) + (4 if other else 0)
        return self.copy(self.piece(self.behind(k), y, core, other), None, kind, k, p.mate())

    def chip(self, k, same, other=False):
        p = self.p
        y = p.y if same else 1 - p.y
        where = {"ctx": p.c + 2 - 4 * self.part, "fsdp": p.f}
        return self.copy(self.piece(self.behind(k), y, p.core, other), None, 4 if same else 5, k, where)

    def own(self):
        return pltpu.make_async_copy(
            self.shard.at[:, :, self.cols], self.full.at[self.p.f, :, :, self.cols], self.local.at[self.ch]
        )

    def start(self):
        self.own().start()
        for k in range(1, self.p.line):
            self.line_out(k).start()

    def start_across(self):
        self.across(0).start()

    def line_in(self, *ks):
        p = self.p
        for k in ks or range(1, p.line):
            self.line_out(k).wait_recv()
            self.across(k).start()
            if self.split:
                self.chip(k, True).start()
            self.mate(k, True, p.core).start()

    def across_in(self, *ks):
        p = self.p
        for k in ks or range(p.line):
            self.across(k).wait_recv()
            if self.split:
                self.chip(k, False).start()
            self.mate(k, False, p.core).start()

    def chip_in(self, *ks):
        p = self.p
        for k in ks or range(p.line):
            for same in (True, False)[k == 0 :]:
                self.chip(k, same, True).wait_recv()
                self.mate(k, same, p.core, True).start()

    def finish(self):
        p = self.p
        self.own().wait()
        for k in range(p.line):
            if k:
                self.line_out(k).wait_send()
            self.across(k).wait_send()
            for same in (True, False)[k == 0 :]:
                for other in (False, True)[: 1 + self.split]:
                    self.mate(k, same, 1 - p.core, other).wait_recv()
                    self.mate(k, same, p.core, other).wait_send()
                if self.split:
                    self.chip(k, same).wait_send()


def gather_sems(place_line, channels):
    return [
        pltpu.SemaphoreType.DMA((channels, 8, place_line)),
        pltpu.SemaphoreType.DMA((channels, 8, place_line)),
        pltpu.SemaphoreType.DMA((channels,)),
    ]


class Reduce:
    def __init__(self, place, term, mine, out, bufs, sems, channel, line_first):
        self.p, self.term, self.mine, self.out = place, term, mine, out
        self.one, self.two, self.ins, self.parts = bufs
        self.send, self.recv = sems
        self.ch, self.line_first = channel, line_first

    def copy(self, src, dst, slot, where, back=None):
        back = slot if back is None else back
        return remote(src, dst, self.send.at[self.ch, slot], self.recv.at[self.ch, back], where)

    def mate_copy(self):
        p = self.p
        return self.copy(self.term.at[:, :, 1 - p.core], self.one, 0, p.mate())

    def mine_copy(self):
        return pltpu.make_async_copy(self.term.at[:, :, self.p.core], self.mine, self.send.at[self.ch, 2])

    def across_copy(self):
        p = self.p
        source = self.one.at[p.z, 1 - p.y] if self.line_first else self.one.at[:, 1 - p.y]
        return self.copy(source, self.two, 1, p.across())

    def line_out(self, k):
        p = self.p
        j = (p.z + k) % p.line
        source = self.one if self.line_first else self.two
        return self.copy(source.at[j], self.ins.at[k], 4 + k, {"ctx": p.c, "fsdp": j * 2 + p.y})

    def ctx_copy(self, k):
        p = self.p
        where = {"ctx": (p.c + 2 * k) % p.n, "fsdp": p.f}
        mine = self.parts.at[p.c // 2]
        return self.copy(mine, mine, 4 + p.line + k, where)

    def last_copy(self, core):
        return self.copy(self.out.at[core], self.out.at[core], 3, self.p.mate())

    def step0(self):
        self.mate_copy().start()
        if self.mine is not None:
            self.mine_copy().start()

    def from_mate(self):
        p = self.p
        if self.mine is not None:
            self.mine_copy().wait()
        self.mate_copy().wait_recv()

        def add(i, carry):
            for y in range(2):
                own = self.term[i, y, p.core] if self.mine is None else self.mine[i, y]
                self.one[i, y] = (self.one[i, y].astype(F32) + own.astype(F32)).astype(BF16)
            return carry

        lax.fori_loop(0, p.line, add, 0)

    def line_start(self):
        for k in range(1, self.p.line):
            self.line_out(k).start()

    def line_sum(self):
        p = self.p
        total = (self.one if self.line_first else self.two)[p.z].astype(F32)
        for k in range(1, p.line):
            self.line_out(k).wait_recv()
            total = total + self.ins[k].astype(F32)
        return total.astype(BF16)

    def ctx_start(self, value):
        p = self.p
        self.parts[p.c // 2] = value
        for k in range(1, p.n // 2):
            self.ctx_copy(k).start()

    def step1(self):
        self.from_mate()
        if self.line_first:
            self.line_start()
        else:
            self.across_copy().start()

    def step2(self):
        p = self.p
        if self.line_first:
            self.one[p.z] = self.line_sum()
            self.across_copy().start()
            return
        self.across_copy().wait_recv()

        def add(i, carry):
            self.two[i] = (self.two[i].astype(F32) + self.one[i, p.y].astype(F32)).astype(BF16)
            return carry

        lax.fori_loop(0, p.line, add, 0)
        self.line_start()

    def step3(self):
        p = self.p
        if self.line_first:
            self.across_copy().wait_recv()
            self.ctx_start((self.two[...].astype(F32) + self.one[p.z, p.y].astype(F32)).astype(BF16))
        else:
            self.ctx_start(self.line_sum())

    def step4(self):
        p = self.p
        for k in range(1, p.n // 2):
            self.ctx_copy(k).wait_recv()
        total = self.parts[0].astype(F32)
        for c in range(1, p.n // 2):
            total = total + self.parts[c].astype(F32)
        self.out[p.core] = total.astype(BF16)
        self.last_copy(p.core).start()

    def finish(self):
        p = self.p
        self.last_copy(1 - p.core).wait_recv()
        self.last_copy(p.core).wait_send()
        self.mate_copy().wait_send()
        self.across_copy().wait_send()
        for k in range(1, p.line):
            self.line_out(k).wait_send()
        for k in range(1, p.n // 2):
            self.ctx_copy(k).wait_send()


def reduce_scratch(shape, h, w, line_first, stored=True):
    line, n = shape["fsdp"] // 2, shape["ctx"]
    run = (line, 2, h, w) if line_first else (line, h, w)
    return [
        pltpu.VMEM((line, 2, h, w) if stored else (8, 128), BF16),
        pltpu.VMEM((line, 2, h, w), BF16),
        pltpu.VMEM((h, w) if line_first else (line, h, w), BF16),
        pltpu.VMEM(run, BF16),
        pltpu.VMEM((n // 2, h, w), BF16),
    ]


def reduce_sems(shape, channels):
    slots = 4 + shape["fsdp"] // 2 + shape["ctx"] // 2
    return [pltpu.SemaphoreType.DMA((channels, slots))] * 2


def halves(pair):
    low = lax.broadcasted_iota(jnp.int32, pair.shape, 1) < 64
    zero = jnp.zeros_like(pair)
    return jnp.concatenate([jnp.where(low, pair, zero), jnp.where(low, zero, pair)], axis=0)


def corner(both):
    return jnp.concatenate([both[0:64, 0:SPAN], both[64:128, SPAN : 2 * SPAN]], axis=0)


def turn(value):
    return value.astype(F32).T.astype(BF16)


class Agenda:
    def __init__(self, actions, places=None):
        self.plan = {}
        if places is None:
            for place, action in actions:
                self.plan.setdefault(place, []).append(action)
            return
        for i, action in enumerate(actions):
            self.plan.setdefault(i * places // len(actions), []).append(action)

    def at(self, place, index=None, count=1):
        if index is None:
            for action in self.plan.get(place, ()):
                action()
            return
        for k in range(count):
            if place + k in self.plan:

                @pl.when(index == k)
                def _(k=k):
                    for action in self.plan[place + k]:
                        action()


def front_kernel(shape, *refs):
    shards, x_hbm = refs[0:6], refs[6]
    wq_out, wo_out, wu_out, wd_out, norms_ref, mixed_out, prob_out, att_out, attt_out, normt_out, unit_out, far_ref, rstd_ref = refs[7:20]
    (x_ref, wq_ref, raw_ref, mixed_ref, prob_ref, att_ref, attt_ref, normt_ref, low_ref, own_ref, all_ref, fart_ref, bias_ref, norm_ref,
     gsend, grecv, glocal, ssend, srecv, nsend, nrecv, io_sem) = refs[20:]
    batches, tokens, _ = x_ref.shape
    spans = tokens // SPAN
    count = far_ref.shape[1]
    prompt = count // 2
    m = shape["fsdp"]
    width = D // m
    place = Place(shape)
    first = place.c * spans

    load = [pltpu.make_async_copy(x_hbm.at[b], x_ref.at[b], io_sem.at[0, b]) for b in range(batches)]
    for copy in load:
        copy.start()
    place.greet(pltpu.get_barrier_semaphore(), rows=True)
    norm_copies = []
    norm_ref[...] = jnp.zeros_like(norm_ref)
    for i in range(2):
        norm_ref[2 * i : 2 * i + 2, 0:width] = shards[4 + i][...].astype(F32)
    for k in range(1, m):
        where = {"ctx": place.c, "fsdp": (place.f + k) % m}
        norm_copies.append(remote(norm_ref, raw_ref.at[place.f], nsend.at[k], nrecv.at[k], where))
        norm_copies[-1].start()
    sems = (gsend, grecv, glocal)
    soon = [Gather(place, shards[0], wq_ref, sems, c, pl.ds(c * D, D)) for c in (1, 2, 0)]
    wo, wu, wd = (
        Gather(place, shards[i], full, sems, 2 + i, split=i == 3) for i, full in ((1, wo_out), (2, wu_out), (3, wd_out))
    )
    later = (wd, wo, wu)
    for part in soon:
        part.start()
        part.start_across()
    raw_ref[place.f] = norm_ref[...]
    for copy in norm_copies:
        copy.wait()
    for f in range(m):
        norms_ref[0:4, f * width : (f + 1) * width] = raw_ref[f, 0:4, 0:width]
    gain = norms_ref[0:1, :]
    shift = norms_ref[2:3, :]
    key_id = lax.broadcasted_iota(jnp.int32, (SPAN, 2 * SPAN), 0)
    query_id = lax.broadcasted_iota(jnp.int32, (SPAN, 2 * SPAN), 1) & (SPAN - 1)
    for s in range(2):
        bias_ref[s, 0:SPAN, :] = jnp.where(key_id <= query_id, 0.0, NEG)

    norm_outs = lambda b: [
        pltpu.make_async_copy(normt_ref.at[b], normt_out.at[b], io_sem.at[1, b]),
        pltpu.make_async_copy(x_ref.at[b], unit_out.at[b], io_sem.at[7, b]),
    ]
    tile = 512
    tiles = tokens // tile
    far_ones = range(2, place.line)
    plan = Agenda([
        (3, soon[0].line_in), (7, soon[1].across_in), (9, soon[2].across_in), (11, wd.line_in), (12, wo.line_in),
        (15, lambda: wo.across_in()), (15, wd.across_in), (16, lambda: wu.line_in(1)), (17, lambda: wu.across_in(0)),
        (18, lambda: wu.line_in(*far_ones)), (19, lambda: wu.across_in(1)), (20, wd.chip_in),
        (23, lambda: wu.across_in(*far_ones)),
    ])

    for b in range(batches):
        load[b].wait()

        def norm(i, carry, b=b):
            plan.at(b * tiles, i, tiles)
            rows = pl.ds(pl.multiple_of(i * tile, tile), tile)
            unit, rstd = unit_of(x_ref[b, rows, :].astype(F32))
            low = (unit * gain + shift).astype(BF16)
            low_ref[b, rows, :] = low
            normt_ref[b, :, rows] = low.T
            x_ref[b, rows, :] = unit.astype(BF16)
            rstd_ref[b, rows, :] = rstd
            return carry

        lax.fori_loop(0, tiles, norm, 0)
        for copy in norm_outs(b):
            copy.start()

    def share(k):
        to = (place.c + k) % place.n
        return remote(own_ref, all_ref.at[place.c], ssend.at[k], srecv.at[k], {"ctx": to, "fsdp": place.f})

    def project(c, at):
        def body(i, carry):
            plan.at(at, i, tiles)
            for b in range(batches):
                rows = pl.ds(pl.multiple_of(i * tile, tile), tile)
                part = nn(low_ref[b, rows, :], wq_ref[:, :, :, c * D : (c + 1) * D].reshape(D, D))
                if c == 0:
                    mixed_ref[b, rows, 0:D] = part.astype(BF16) * 0.125
                    continue
                mixed_ref[b, rows, c * D : (c + 1) * D] = part.astype(BF16)
                for s in range(tile // SPAN):
                    total = jnp.sum(part[s * SPAN : (s + 1) * SPAN, :], axis=0, keepdims=True) * SPAN ** (-0.5)
                    own_ref[b, pl.ds(i * (tile // SPAN) + s, 1), (c - 1) * D : c * D] = total.astype(BF16).astype(F32)
            return carry

        lax.fori_loop(0, tiles, body, 0)

    soon[1].line_in()
    soon[0].across_in()
    soon[2].line_in()
    for part in later:
        part.start()
        part.start_across()
    soon[0].finish()
    project(1, 6)
    soon[1].finish()
    project(2, 8)
    for k in range(1, place.n):
        share(k).start()
    all_ref[place.c] = own_ref[...]
    soon[2].finish()
    project(0, 10)
    pairs = spans // 2
    weight_out = pltpu.make_async_copy(wq_ref, wq_out, io_sem.at[6, 0])
    weight_out.start()
    for k in range(1, place.n):
        share(k).wait()

    out_copies = lambda b: [
        pltpu.make_async_copy(src.at[b], dst.at[b], io_sem.at[2 + i, b])
        for i, (src, dst) in enumerate(
            ((mixed_ref, mixed_out), (prob_ref, prob_out), (att_ref, att_out), (attt_ref, attt_out))
        )
    ]

    for b in range(batches):
        out_copies(b)[0].start()
        for c in range(place.n):
            far_ref[b, c * spans : (c + 1) * spans, :] = all_ref[c, b].astype(BF16)
        fart_ref[...] = far_ref[b, :, D:].T

        def attend(i, carry, b=b):
            plan.at(12 + b * pairs, i, pairs)
            for s in range(2):
                far_id = lax.broadcasted_iota(jnp.int32, (count, 2 * SPAN), 0)
                mine = first + i * 2 + s
                segment = (mine - prompt) >> 3
                seen = (far_id < mine) & ((far_id < prompt) | (((far_id - prompt) >> 3) == segment))
                bias_ref[s, SPAN:, :] = jnp.where(seen, 0.0, NEG)
            scores, probs = {}, {}
            items = [(s, p) for p in range(PAIRS) for s in range(2)]
            for t in range(len(items) + 2):
                if t < len(items):
                    s, p = items[t]
                    rows = pl.ds(pl.multiple_of(i * 2 * SPAN + s * SPAN, SPAN), SPAN)
                    lanes = slice(p * SPAN, (p + 1) * SPAN)
                    qs = halves(mixed_ref[b, rows, lanes])
                    keys = jnp.concatenate(
                        [mixed_ref[b, rows, D + p * SPAN : D + (p + 1) * SPAN], far_ref[b, :, lanes]], axis=0
                    )
                    scores[t] = nt(keys, qs)
                if 1 <= t <= len(items):
                    s, p = items[t - 1]
                    score = scores.pop(t - 1) + bias_ref[s]
                    score = jnp.exp(score - jnp.max(score, axis=0, keepdims=True))
                    prob = (score * (1.0 / jnp.sum(score, axis=0, keepdims=True))).astype(BF16)
                    prob_ref[b, i * 2 + s, p] = prob
                    probs[t - 1] = prob
                if t >= 2:
                    s, p = items[t - 2]
                    rows = pl.ds(pl.multiple_of(i * 2 * SPAN + s * SPAN, SPAN), SPAN)
                    lanes = slice(p * SPAN, (p + 1) * SPAN)
                    turned = mixed_ref[b, rows, 2 * D + p * SPAN : 2 * D + (p + 1) * SPAN].T
                    turned = jnp.concatenate([turned, fart_ref[lanes, :]], axis=1)
                    att = corner(nn(turned, probs.pop(t - 2))).astype(BF16)
                    attt_ref[b, lanes, rows] = att
                    att_ref[b, rows, lanes] = att.T
            return carry

        lax.fori_loop(0, pairs, attend, 0)
        for copy in out_copies(b)[1:]:
            copy.start()

    for part in later:
        part.finish()
    weight_out.wait()
    for b in range(batches):
        for copy in norm_outs(b) + out_copies(b):
            copy.wait()


def front_call(shape, shards, x):
    batches, tokens, _ = x.shape
    spans = tokens // SPAN
    n, m = shape["ctx"], shape["fsdp"]
    count = n * spans
    any_spec = pl.BlockSpec(memory_space=pl.ANY)
    vmem = pl.BlockSpec(memory_space=pltpu.VMEM)
    full = [jax.ShapeDtypeStruct((m,) + s.shape, s.dtype) for s in shards[0:4]]
    big = [
        jax.ShapeDtypeStruct((batches, tokens, 3 * D), BF16),
        jax.ShapeDtypeStruct((batches, spans, PAIRS, SPAN + count, 2 * SPAN), BF16),
        jax.ShapeDtypeStruct((batches, tokens, D), BF16),
        jax.ShapeDtypeStruct((batches, D, tokens), BF16),
        jax.ShapeDtypeStruct((batches, D, tokens), BF16),
    ]
    return pl.pallas_call(
        functools.partial(front_kernel, shape),
        in_specs=[any_spec] * 4 + [vmem] * 2 + [any_spec],
        out_specs=[any_spec] * 4 + [vmem] + [any_spec] * 6 + [vmem] * 2,
        out_shape=full + [jax.ShapeDtypeStruct((8, D), F32)]
        + big
        + [
            jax.ShapeDtypeStruct(x.shape, BF16),
            jax.ShapeDtypeStruct((batches, count, 2 * D), BF16),
            jax.ShapeDtypeStruct((batches, tokens, 1), F32),
        ],
        scratch_shapes=[
            pltpu.VMEM((batches, tokens, D), BF16),
            pltpu.VMEM(full[0].shape, BF16),
            pltpu.VMEM((m, 8, 128), F32),
        ]
        + [pltpu.VMEM(v.shape, v.dtype) for v in big]
        + [
            pltpu.VMEM((batches, tokens, D), BF16),
            pltpu.VMEM((batches, spans, 2 * D), F32),
            pltpu.VMEM((n, batches, spans, 2 * D), F32),
            pltpu.VMEM((D, count), BF16),
            pltpu.VMEM((2, SPAN + count, 2 * SPAN), F32),
            pltpu.VMEM((8, 128), F32),
        ]
        + gather_sems(m // 2, 6)
        + [
            pltpu.SemaphoreType.DMA((n,)),
            pltpu.SemaphoreType.DMA((n,)),
            pltpu.SemaphoreType.DMA((m,)),
            pltpu.SemaphoreType.DMA((m,)),
            pltpu.SemaphoreType.DMA((8, batches)),
        ],
        compiler_params=pltpu.CompilerParams(collective_id=0, has_side_effects=True, vmem_limit_bytes=VMEM_LIMIT),
        name="front",
    )(*shards, x)


def middle_kernel(shape, *refs):
    x_hbm, g_hbm, att_hbm, attt_hbm, wo_hbm, wu_hbm, wd_hbm, norms_ref = refs[0:8]
    out_hbm, gmid_hbm, da_hbm, go_ref, gu_ref, gd_ref, gu_sum, gd_sum, ggain_ref, gshift_ref = refs[8:18]
    (x_ref, att_ref, attt_ref, g_ref, n2_ref, n2t_ref, gt_ref, unit_ref, rstd_ref, acc_ref, gn2_ref, act_ref, gh_ref,
     wo_ref, wu_ref, wd_ref, goa_ref, gua_ref, gda_ref, gu_term, gd_term) = refs[18:39]
    bufs, sems, io_sem, w_sem = refs[39:47], refs[47:49], refs[49], refs[50]
    batches, tokens, _ = g_ref.shape
    m = shape["fsdp"]
    place = Place(shape)
    per = FF // m // UNIT
    group = UNIT * m
    tile = 512
    tiles = tokens // tile

    ins = lambda b: [
        pltpu.make_async_copy(src.at[b], dst, io_sem.at[i, b])
        for i, (src, dst) in enumerate(
            ((x_hbm, x_ref.at[b % 2]), (att_hbm, att_ref.at[b % 2]), (g_hbm, g_ref.at[b]))
        )
    ]
    turned = lambda b: pltpu.make_async_copy(attt_hbm.at[b], attt_ref.at[b % 2], io_sem.at[3, b])
    wo_copy = pltpu.make_async_copy(wo_hbm, wo_ref, io_sem.at[4, 0])
    weights = []
    for h in range(per):
        for f in range(m):
            src, dst = (f * per + h) * UNIT, h * group + f * UNIT
            weights.append(
                pltpu.make_async_copy(wu_hbm.at[:, pl.ds(src, UNIT)], wu_ref.at[:, pl.ds(dst, UNIT)], w_sem.at[0, h, f])
            )
            weights.append(
                pltpu.make_async_copy(wd_hbm.at[pl.ds(src, UNIT)], wd_ref.at[pl.ds(dst, UNIT)], w_sem.at[1, h, f])
            )
    wo_copy.start()
    for copy in ins(0):
        copy.start()
    for copy in weights:
        copy.start()
    early = per > 1
    if early:
        place.greet(pltpu.get_barrier_semaphore(), rows=True)
        gu = Reduce(place, gu_term, None, gu_sum, bufs[0:4], sems, 0, False)
        gd = Reduce(place, gd_term, None, gd_sum, bufs[4:8], sems, 1, False)
        chain = [(0, gu.step0), (0, gd.step0), (1, gu.step1), (1, gd.step1), (3, gu.step2), (4, gd.step2)]
        chain += [(6, gu.step3), (7, gd.step3), (9, gu.step4), (10, gd.step4)]
    gain = norms_ref[1:2, :]
    shift = norms_ref[3:4, :]

    wo_copy.wait()
    for b in range(batches):
        if b + 1 < batches:
            for copy in ins(b + 1):
                copy.start()
        for copy in ins(b):
            copy.wait()

        def before(i, carry, b=b):
            rows = pl.ds(pl.multiple_of(i * tile, tile), tile)
            middle = x_ref[b % 2, rows, :].astype(F32) + nn(att_ref[b % 2, rows, :], wo_ref[...])
            unit, rstd = unit_of(middle)
            low = (unit * gain + shift).astype(BF16)
            acc_ref[b, rows, :] = middle
            gn2_ref[b, rows, :] = jnp.zeros((tile, D), F32)
            unit_ref[b, rows, :] = unit.astype(BF16)
            rstd_ref[b, rows, :] = rstd
            n2_ref[b, rows, :] = low
            n2t_ref[b, :, rows] = low.T
            gt_ref[b, :, rows] = g_ref[b, rows, :].T
            return carry

        lax.fori_loop(0, tiles, before, 0)
    for copy in weights:
        copy.wait()
    wd_ref[...] = wd_ref[...] * 0.5
    act_ref[1] = jnp.zeros((tokens, CHUNK), BF16)
    gh_ref[1] = jnp.zeros((tokens, CHUNK), BF16)

    def wgrad(i):
        b = lax.rem(i, batches)
        slot = lax.rem(i, 2)
        keep = b > 0
        total = nn(n2t_ref[b], gh_ref[slot])
        gua_ref[...] = jnp.where(keep, gua_ref[...], 0.0) + total
        total = nn(gt_ref[b], act_ref[slot])
        gda_ref[...] = jnp.where(keep, gda_ref[...], 0.0) + total

    half = D // m // 2

    def close(c):
        h, base = c * CHUNK // group, c * CHUNK % group
        ups, downs = (gu_term, gd_term) if early and h == 0 else (gu_ref, gd_ref)

        def body(i, carry):
            for y in range(2):
                for s in range(2):
                    start = pl.multiple_of(((i * 2 + y) * 2 + s) * half, half)
                    ups[i, y, s, :, base : base + CHUNK] = gua_ref[pl.ds(start, half), :].astype(BF16)
            return carry

        lax.fori_loop(0, m // 2, body, 0)
        for k in range(CHUNK // UNIT):
            f = base // UNIT + k
            rows = (gda_ref[:, k * UNIT : (k + 1) * UNIT] * 0.5).astype(BF16).T
            downs[f // 2, f % 2, 0] = rows[0 : UNIT // 2]
            downs[f // 2, f % 2, 1] = rows[UNIT // 2 :]

    chunks = FF // CHUNK
    steps = chunks * batches
    opening = (chunks // per) * batches + 1 if early else steps
    agenda = Agenda(chain) if early else None

    def step(i, carry):
        for c in range(chunks - 1):

            @pl.when(i == (c + 1) * batches + 1)
            def _(c=c):
                close(c)

        if early:
            agenda.at(0, i - opening, steps - opening)
        c = lax.div(i, batches)
        b = lax.rem(i, batches)
        slot = lax.rem(i, 2)
        cols = pl.ds(pl.multiple_of(c * CHUNK, CHUNK), CHUNK)
        for r in range(1):
            rows = slice(0, tokens)
            act, slope = gelu_pair(nn(n2_ref[b, rows, :], wu_ref[:, cols]))
            act = act.astype(BF16)
            act_ref[slot, rows, :] = act
            grad = (nt(g_ref[b, rows, :], wd_ref[cols, :]) * slope).astype(BF16)
            gh_ref[slot, rows, :] = grad
            acc_ref[b, rows, :] += nn(act, wd_ref[cols, :])
            gn2_ref[b, rows, :] += nt(grad, wu_ref[:, cols])
            if r == 0:
                wgrad(i + steps * 2 - 1)
        return carry

    lax.fori_loop(0, steps, step, 0)
    wgrad(steps - 1)
    turned(0).start()
    close(chunks - 1)

    outs = lambda b: [
        pltpu.make_async_copy(src, dst.at[b], io_sem.at[5 + i, b])
        for i, (src, dst) in enumerate(((unit_ref.at[b], out_hbm), (g_ref.at[b], gmid_hbm), (n2_ref.at[b], da_hbm)))
    ]
    ggain_ref[...] = jnp.zeros_like(ggain_ref)
    gshift_ref[...] = jnp.zeros_like(gshift_ref)
    for b in range(batches):
        if b + 1 < batches:
            turned(b + 1).start()

        def after(i, carry, b=b):
            if early:
                agenda.at(steps - opening + b * tiles, i, tiles)
            rows = pl.ds(pl.multiple_of(i * tile, tile), tile)
            unit = unit_ref[b, rows, :].astype(F32)
            grad = gn2_ref[b, rows, :]
            ggain_ref[...] += fold8(grad * unit)
            gshift_ref[...] += fold8(grad)
            grad = g_ref[b, rows, :].astype(F32) + norm_back(grad, unit, rstd_ref[b, rows, :], gain)
            low = grad.astype(BF16)
            unit_ref[b, rows, :] = acc_ref[b, rows, :].astype(BF16)
            g_ref[b, rows, :] = low
            n2_ref[b, rows, :] = nt(low, wo_ref[...]).astype(BF16)
            return carry

        lax.fori_loop(0, tiles, after, 0)
        for copy in outs(b):
            copy.start()
        turned(b).wait()
        total = nn(attt_ref[b % 2], g_ref[b])
        goa_ref[...] = total if b == 0 else goa_ref[...] + total
    go_ref[...] = goa_ref[...].astype(BF16)
    if early:
        gu.finish()
        gd.finish()
    for b in range(batches):
        for copy in outs(b):
            copy.wait()


def middle_call(shape, x, g, att, attt, wo, wu, wd, norms):
    batches, tokens, _ = x.shape
    m = shape["fsdp"]
    line = m // 2
    group = UNIT * m
    any_spec = pl.BlockSpec(memory_space=pl.ANY)
    vmem = pl.BlockSpec(memory_space=pltpu.VMEM)
    up = (line, 2, 2, D // m // 2, group)
    down = (line, 2, 2, UNIT // 2, D)
    low = lambda *dims: jax.ShapeDtypeStruct(dims, BF16)
    seqs = lambda: pltpu.VMEM((batches, tokens, D), BF16)
    turned = lambda count: pltpu.VMEM((count, D, tokens), BF16)
    scratch = [
        pltpu.VMEM((2, tokens, D), BF16), pltpu.VMEM((2, tokens, D), BF16), turned(2), seqs(), seqs(), turned(batches),
        turned(batches), seqs(), pltpu.VMEM((batches, tokens, 1), F32), pltpu.VMEM((batches, tokens, D), F32),
        pltpu.VMEM((batches, tokens, D), F32), pltpu.VMEM((2, tokens, CHUNK), BF16), pltpu.VMEM((2, tokens, CHUNK), BF16),
        pltpu.VMEM((D, D), BF16), pltpu.VMEM((D, FF), BF16), pltpu.VMEM((FF, D), BF16),
        pltpu.VMEM((D, D), F32), pltpu.VMEM((D, CHUNK), F32), pltpu.VMEM((D, CHUNK), F32),
    ]
    early = FF // m // UNIT > 1
    small = (8, 128)
    scratch += [pltpu.VMEM(up if early else small, BF16), pltpu.VMEM(down if early else small, BF16)]
    for t in (up, down):
        if early:
            scratch += reduce_scratch(shape, *t[3:], False, False)[1:]
        else:
            scratch += [pltpu.VMEM(small, BF16)] * 4
    scratch += reduce_sems(shape, 2)
    scratch += [pltpu.SemaphoreType.DMA((8, batches)), pltpu.SemaphoreType.DMA((2, FF // m // UNIT, m))]
    return pl.pallas_call(
        functools.partial(middle_kernel, shape),
        in_specs=[any_spec] * 7 + [vmem],
        out_specs=[any_spec] * 3 + [vmem] * 7,
        out_shape=[
            low(*x.shape), low(*x.shape), low(*x.shape), low(D, D), low(*up), low(*down),
            low(*(up[2:] if early else small)), low(*(down[2:] if early else small)),
            jax.ShapeDtypeStruct((8, D), F32), jax.ShapeDtypeStruct((8, D), F32),
        ],
        scratch_shapes=scratch,
        compiler_params=pltpu.CompilerParams(
            collective_id=2 if early else None, has_side_effects=True, vmem_limit_bytes=VMEM_LIMIT
        ),
        name="middle",
    )(x, g, att, attt, wo, wu, wd, norms)


def back_kernel(shape, *refs):
    mixed_hbm, da_hbm, prob_hbm, unit_hbm, normt_hbm, gmid_hbm, wq_hbm, gu_hbm, gd_hbm, go_hbm = refs[0:10]
    far_ref, rstd_ref, norms_ref, gain2_ref, shift2_ref = refs[10:15]
    gin_out, gq_out, gk_out, gv_out, gu_out, gd_out, go_out, small_out = refs[15:23]
    (mixed_ref, da_ref, prob_ref, unit_ref, normt_ref, gmid_ref, wq_ref, dmixed_ref, gw_ref, gq_ref, gk_ref, gv_ref,
     far_t, dfar_ref, held_ref, gsum_ref, vec_ref, vecs_ref, vsum_ref, pieces_ref) = refs[23:43]
    bufs, sems = refs[43:73], refs[73:75]
    xsend, xrecv, vsend, vrecv, io_sem = refs[75:80]
    batches, tokens, _ = unit_ref.shape
    spans = tokens // SPAN
    count = far_ref.shape[1]
    m = shape["fsdp"]
    width = D // m
    place = Place(shape)

    ins = lambda b: [
        pltpu.make_async_copy(src.at[b], dst.at[b % 2], io_sem.at[i, b])
        for i, (src, dst) in enumerate(((mixed_hbm, mixed_ref), (da_hbm, da_ref), (prob_hbm, prob_ref)))
    ]
    rest = [
        pltpu.make_async_copy(src, dst, io_sem.at[4 + i, 0])
        for i, (src, dst) in enumerate(
            ((normt_hbm, normt_ref), (unit_hbm, unit_ref), (gmid_hbm, gmid_ref), (wq_hbm, wq_ref))
        )
    ]
    for copy in ins(0):
        copy.start()
    place.greet(pltpu.get_barrier_semaphore(), rows=True)
    channel = lambda i, term, out, line_first, stored: Reduce(
        place, term, bufs[5 * i] if stored else None, out, bufs[5 * i + 1 : 5 * i + 5], sems, i, line_first
    )
    gu = channel(0, gu_hbm, gu_out, False, True)
    gd = channel(1, gd_hbm, gd_out, False, True)
    go = channel(2, go_hbm, go_out, False, True)
    gq = channel(3, gq_ref, gq_out, False, False)
    gk = channel(4, gk_ref, gk_out, True, False)
    gv = channel(5, gv_ref, gv_out, False, False)
    for part in (gu, gd, go):
        part.step0()
    for copy in rest:
        copy.start()

    def swap(b, k):
        to = (place.c + k) % place.n
        source = dfar_ref.at[b, pl.ds(pl.multiple_of(to * spans, spans), spans)]
        return remote(source, held_ref.at[b, k], xsend.at[b, k], xrecv.at[b, k], {"ctx": to, "fsdp": place.f})

    pairs = spans // 2
    big = Agenda([(at, getattr(part, "step" + step)) for part, places in (
        (gu, GU), (gd, GD), (go, GO), (gq, GQ), (gk, GK), (gv, GV)
    ) for at, step in zip(places, "1234")])

    def attend_back(b):
        slot = b % 2
        for copy in ins(b):
            copy.wait()
        if b + 1 < batches:
            for copy in ins(b + 1):
                copy.start()
        dfar_ref[b] = jnp.zeros((count, 2 * D), F32)
        far_t[...] = far_ref[b, :, 0:D].T
        base = b * (pairs + EXTRA)

        def body(i, carry):
            big.at(base, i, pairs)
            items = [(s, p) for p in range(PAIRS) for s in range(2)]
            held, grads = {}, {}
            where = lambda t: (
                pl.ds(pl.multiple_of(i * 2 * SPAN + items[t][0] * SPAN, SPAN), SPAN),
                *(slice(c * D + items[t][1] * SPAN, c * D + (items[t][1] + 1) * SPAN) for c in range(3)),
            )
            for t in range(len(items) + 2):
                if t < len(items):
                    rows, lanes, klanes, vlanes = where(t)
                    das = halves(da_ref[slot, rows, lanes])
                    values = jnp.concatenate([mixed_ref[slot, rows, vlanes], far_ref[b, :, klanes]], axis=0)
                    held[t] = (das, nt(values, das))
                if 1 <= t <= len(items):
                    rows, lanes, klanes, vlanes = where(t - 1)
                    das, slope = held.pop(t - 1)
                    low = prob_ref[slot, i * 2 + items[t - 1][0], items[t - 1][1]]
                    prob = low.astype(F32)
                    inner = jnp.sum(prob * slope, axis=0, keepdims=True)
                    grads[t - 1] = (prob * (slope - inner)).astype(BF16)
                    dv = nn(low, das)
                    dmixed_ref[b, rows, vlanes] = dv[0:SPAN].astype(BF16)
                    dfar_ref[b, :, klanes] += dv[SPAN:]
                if t >= 2:
                    rows, lanes, klanes, vlanes = where(t - 2)
                    grad = grads.pop(t - 2)
                    dk = nn(grad, halves(mixed_ref[slot, rows, lanes]))
                    dmixed_ref[b, rows, klanes] = dk[0:SPAN].astype(BF16)
                    dfar_ref[b, :, lanes] += dk[SPAN:]
                    turned = jnp.concatenate([mixed_ref[slot, rows, klanes].T, far_t[lanes, :]], axis=1)
                    dmixed_ref[b, rows, lanes] = (corner(nn(turned, grad)) * 0.125).astype(BF16).T
            return carry

        lax.fori_loop(0, pairs, body, 0)
        for k in range(1, place.n):
            swap(b, k).start()

    def wgrad(b, c):
        cols = slice(c * D, (c + 1) * D)
        part = nn(normt_ref[b], dmixed_ref[b, :, cols])
        gw_ref[:, cols] = part if b == 0 else gw_ref[:, cols] + part

    def spread(b):
        for k in range(1, place.n):
            swap(b, k).wait()
        total = dfar_ref[b, pl.ds(pl.multiple_of(place.c * spans, spans), spans), :]
        for k in range(1, place.n):
            total = total + held_ref[b, k]
        gsum_ref[...] = total * SPAN ** (-0.5)

        def body(s, carry):
            rows = pl.ds(pl.multiple_of(s * SPAN, SPAN), SPAN)
            extra = jnp.broadcast_to(gsum_ref[pl.ds(s, 1), :], (16, 2 * D)).astype(BF16)
            for r in range(SPAN // 16):
                at = pl.ds(pl.multiple_of(s * SPAN + r * 16, 16), 16)
                dmixed_ref[b, at, D:] = dmixed_ref[b, at, D:] + extra
            return carry

        lax.fori_loop(0, spans, body, 0)

    half = D // m // 2

    def low(dst, cols):
        def body(i, carry):
            for y in range(2):
                for s in range(2):
                    start = pl.multiple_of(((i * 2 + y) * 2 + s) * half, half)
                    dst[i, y, s] = gw_ref[pl.ds(start, half), cols].astype(BF16)
            return carry

        lax.fori_loop(0, m // 2, body, 0)

    for b in range(batches):
        attend_back(b)
        if b == 0:
            for copy in rest:
                copy.wait()
        base = b * (pairs + EXTRA) + pairs
        big.at(base)
        wgrad(b, 0)
        if b + 1 == batches:
            low(gq_ref, slice(0, D))
            gq.step0()
        big.at(base + 1)
        if b > 0:
            spread(b - 1)
            for c in (1, 2):
                wgrad(b - 1, c)
        big.at(base + 2)
    last = batches - 1
    spread(last)
    for c, part, term in ((1, gk, gk_ref), (2, gv, gv_ref)):
        wgrad(last, c)
        low(term, slice(c * D, (c + 1) * D))
        part.step0()

    gain = norms_ref[0:1, :]
    tile = 512
    tiles = tokens // tile
    late = batches * (pairs + EXTRA)
    gin_copy = lambda b: pltpu.make_async_copy(gmid_ref.at[b], gin_out.at[b], io_sem.at[3, b])
    gains_at = jnp.zeros((8, D), F32)
    shifts_at = jnp.zeros((8, D), F32)
    for b in range(batches):

        def data(i, carry, b=b):
            big.at(late + b * tiles, i, tiles)
            spots = [pl.ds(pl.multiple_of(i * tile + r * (tile // 2), tile // 2), tile // 2) for r in range(2)]
            grads = [nt(dmixed_ref[b, rows, :], wq_ref[...].reshape(D, 3 * D)) for rows in spots]
            gains_at, shifts_at = carry
            for rows, grad in zip(spots, grads):
                unit = unit_ref[b, rows, :].astype(F32)
                change = norm_back(grad, unit, rstd_ref[b, rows, :], gain)
                gmid_ref[b, rows, :] = (gmid_ref[b, rows, :].astype(F32) + change).astype(BF16)
                gains_at = gains_at + fold8(grad * unit)
                shifts_at = shifts_at + fold8(grad)
            return gains_at, shifts_at

        gains_at, shifts_at = lax.fori_loop(0, tiles, data, (gains_at, shifts_at))
        gin_copy(b).start()

    sums = [jnp.sum(v, axis=0, keepdims=True) for v in (gains_at, gain2_ref[...], shifts_at, shift2_ref[...])]
    vec_ref[...] = jnp.concatenate(sums + [jnp.zeros((4, D), F32)], axis=0)
    over_ctx = [
        remote(vec_ref, vecs_ref.at[k], vsend.at[0, k], vrecv.at[0, k], {"ctx": (place.c + k) % place.n, "fsdp": place.f})
        for k in range(1, place.n)
    ]
    for copy in over_ctx:
        copy.start()
    vecs_ref[0] = vec_ref[...]
    big.at(late + batches * tiles)
    for copy in over_ctx:
        copy.wait()
    total = jnp.zeros((8, D), F32)
    for c in range(place.n):
        total = total + vecs_ref[(place.c - c + place.n) % place.n]
    vsum_ref[...] = jnp.zeros_like(vsum_ref)
    for f in range(m):
        vsum_ref[f, :, 0:width] = total[:, f * width : (f + 1) * width]
    over_rows = []
    for k in range(1, m):
        to = (place.f + k) % m
        over_rows.append(
            remote(vsum_ref.at[to], pieces_ref.at[place.f], vsend.at[1, k], vrecv.at[1, k], {"ctx": place.c, "fsdp": to})
        )
        over_rows[-1].start()
    pieces_ref[place.f] = vsum_ref[place.f]
    big.at(late + batches * tiles + 1)
    for copy in over_rows:
        copy.wait()
    total = pieces_ref[0]
    for f in range(1, m):
        total = total + pieces_ref[f]
    small_out[...] = total
    for part in (gu, gd, go, gq, gk, gv):
        part.finish()
    for b in range(batches):
        gin_copy(b).wait()


def back_call(shape, mixed, da, prob, unit, normt, gmid, wq, gu, gd, go, far, rstd, norms, gain2, shift2):
    batches, tokens, _ = unit.shape
    spans = tokens // SPAN
    n, m = shape["ctx"], shape["fsdp"]
    line = m // 2
    count = n * spans
    any_spec = pl.BlockSpec(memory_space=pl.ANY)
    vmem = pl.BlockSpec(memory_space=pltpu.VMEM)
    halved = lambda rows, w: (line, 2, 2, rows // (2 * m), w)
    terms = [gu.shape, gd.shape, halved(D, D), halved(D, D), halved(D, D), halved(D, D)]
    go = go.reshape(terms[2])
    out = lambda t: jax.ShapeDtypeStruct(t[2:], BF16)
    two = lambda *dims: pltpu.VMEM((2,) + dims, BF16)
    scratch = [
        two(tokens, 3 * D), two(tokens, D), two(spans, PAIRS, SPAN + count, 2 * SPAN),
        pltpu.VMEM(unit.shape, BF16), pltpu.VMEM(normt.shape, BF16), pltpu.VMEM(unit.shape, BF16),
        pltpu.VMEM(wq.shape, BF16), pltpu.VMEM((batches, tokens, 3 * D), BF16), pltpu.VMEM((D, 3 * D), F32),
        pltpu.VMEM(terms[3], BF16), pltpu.VMEM(terms[4], BF16), pltpu.VMEM(terms[5], BF16),
        pltpu.VMEM((D, count), BF16), pltpu.VMEM((batches, count, 2 * D), F32),
        pltpu.VMEM((batches, n, spans, 2 * D), F32), pltpu.VMEM((spans, 2 * D), F32),
        pltpu.VMEM((8, D), F32), pltpu.VMEM((n, 8, D), F32), pltpu.VMEM((m, 8, 128), F32), pltpu.VMEM((m, 8, 128), F32),
    ]
    for t, line_first, stored in zip(terms, (False,) * 4 + (True, False), (True,) * 3 + (False,) * 3):
        scratch += reduce_scratch(shape, *t[3:], line_first, stored)
    scratch += reduce_sems(shape, 6)
    most = max(n, m)
    scratch += [
        pltpu.SemaphoreType.DMA((batches, n)), pltpu.SemaphoreType.DMA((batches, n)),
        pltpu.SemaphoreType.DMA((2, most)), pltpu.SemaphoreType.DMA((2, most)), pltpu.SemaphoreType.DMA((8, batches)),
    ]
    return pl.pallas_call(
        functools.partial(back_kernel, shape),
        in_specs=[any_spec] * 10 + [vmem] * 5,
        out_specs=[any_spec] + [vmem] * 7,
        out_shape=[
            jax.ShapeDtypeStruct(unit.shape, BF16), out(terms[3]), out(terms[4]), out(terms[5]), out(terms[0]),
            out(terms[1]), out(terms[2]), jax.ShapeDtypeStruct((8, 128), F32),
        ],
        scratch_shapes=scratch,
        compiler_params=pltpu.CompilerParams(collective_id=1, has_side_effects=True, vmem_limit_bytes=VMEM_LIMIT),
        name="back",
    )(mixed, da, prob, unit, normt, gmid, wq, gu, gd, go, far, rstd, norms, gain2, shift2)


def widen_kernel(per, *refs):
    small_ref, go_ref = refs[0], refs[4]
    gus, gds = refs[5 : 5 + per], refs[5 + per : 5 + 2 * per]
    qkv_out, out_out, up_out, down_out, gain_out, first_out, second_out = refs[5 + 2 * per :]
    for c in range(3):
        qkv_out[:, c * D : (c + 1) * D] = refs[1 + c][...].astype(F32)
    out_out[...] = go_ref[...].astype(F32)
    for h in range(per):
        for f in range(gus[h].shape[1] // UNIT):
            at = (f * per + h) * UNIT
            up_out[:, at : at + UNIT] = gus[h][:, f * UNIT : (f + 1) * UNIT].astype(F32)
        down_out[h * UNIT : (h + 1) * UNIT, :] = gds[h][...].astype(F32)
    width = gain_out.shape[1]
    gain_out[...] = small_ref[0:2, 0:width]
    first_out[...] = small_ref[2, 0:width]
    second_out[...] = small_ref[3, 0:width]


def widen_call(width, small, gq, gk, gv, go, gus, gds):
    per = len(gus)
    flat = [small] + [v.reshape(-1, v.shape[-1]) for v in (gq, gk, gv, go, *gus, *gds)]
    rows = flat[1].shape[0]
    wide = lambda *dims: jax.ShapeDtypeStruct(dims, F32)
    return pl.pallas_call(
        functools.partial(widen_kernel, per),
        out_shape=[
            wide(rows, 3 * D), wide(rows, D), wide(rows, FF), wide(per * UNIT, D), wide(2, width), wide(width), wide(width)
        ],
        name="widen",
    )(*flat)


def local(shape, x, g, qkv_weight, out_weight, up_weight, down_weight, norm_gains, norm_shifts):
    width = norm_gains.shape[1]
    halved = lambda shard: shard.reshape(2, shard.shape[0] // 2, shard.shape[1])
    shards = [halved(v) for v in (qkv_weight, out_weight, up_weight, down_weight)] + [norm_gains, norm_shifts]
    wq, wo, wu, wd, norms, mixed, prob, att, attt, normt, unit, far, rstd = front_call(shape, shards, x)
    wo, wu, wd = (w.reshape(-1, w.shape[-1]) for w in (wo, wu, wd))
    out, gmid, da, go, gu, gd, gu_sum, gd_sum, gain2, shift2 = middle_call(shape, x, g, att, attt, wo, wu, wd, norms)
    gin, gq, gk, gv, gu, gd, go, small = back_call(
        shape, mixed, da, prob, unit, normt, gmid, wq, gu, gd, go, far, rstd, norms, gain2, shift2
    )
    early = FF // shape["fsdp"] // UNIT > 1
    gus, gds = ([gu_sum, gu], [gd_sum, gd]) if early else ([gu], [gd])
    return out, gin, *widen_call(width, small, gq, gk, gv, go, gus, gds)


def solution(mesh):
    weight, norm, token = P("fsdp", None), P(None, "fsdp"), P("fsdp", "ctx", None)
    return jax.shard_map(
        functools.partial(local, dict(mesh.shape)),
        mesh=mesh,
        in_specs=(token, token, weight, weight, weight, weight, norm, norm),
        out_specs=(token, token, weight, weight, weight, weight, norm, P("fsdp"), P("fsdp")),
        check_vma=False,
    )
```

```python
import functools

import jax
import jax.numpy as jnp
from jax import lax
from jax.experimental import pallas as pl
from jax.experimental.pallas import tpu as pltpu
from jax.sharding import PartitionSpec as P

D = 512
HEADS = 8
FF = 2048
SPAN = 128
CONT = 1024
PAIRS = HEADS // 2
CHUNK = 512
UNIT = 128
EXTRA = 3
GU = (3, 12, 20, 22)
GD = (5, 18, 25, 27)
GO = (6, 19, 25, 27)
GQ = (21, 24, 26, 28)
GK = (22, 27, 27, 28)
GV = (22, 26, 27, 28)

EPS = 1e-05
NEG = -1e30
F32 = jnp.float32
BF16 = jnp.bfloat16
VMEM_LIMIT = 60 * 1024 * 1024


def nn(a, b):
    return lax.dot_general(a, b, (((1,), (0,)), ((), ())), preferred_element_type=F32)


def nt(a, b):
    return lax.dot_general(a, b, (((1,), (1,)), ((), ())), preferred_element_type=F32)


def unit_of(values):
    center = values - jnp.mean(values, axis=-1, keepdims=True)
    rstd = lax.rsqrt(jnp.mean(center * center, axis=-1, keepdims=True) + EPS)
    return center * rstd, rstd


def norm_back(grad, unit, rstd, gain):
    scaled = grad * gain
    return rstd * (
        scaled
        - jnp.mean(scaled, axis=-1, keepdims=True)
        - unit * jnp.mean(scaled * unit, axis=-1, keepdims=True)
    )


def fold8(values):
    rows = values.shape[0]
    return jnp.sum(values.reshape(rows // 8, 8, values.shape[1]), axis=0)


def gelu_pair(x):
    cdf = lax.erf(x * 0.7071067811865476) + 1.0
    slope = jnp.exp2(x * x * (-0.5 * 1.4426950408889634)) * (x * 0.7978845608028654)
    return x * cdf, cdf + slope


MESH = pl.DeviceIdType.MESH


class Place:
    def __init__(self, mesh_shape):
        self.n, self.m = mesh_shape["ctx"], mesh_shape["fsdp"]
        self.inner = 2
        self.line = self.m // 2
        self.c, self.f = lax.axis_index("ctx"), lax.axis_index("fsdp")
        self.core = self.c % 2
        self.z, self.y = self.f // 2, self.f % 2

    def mate(self):
        return {"ctx": self.c + 1 - 2 * self.core, "fsdp": self.f}

    def across(self):
        return {"ctx": self.c, "fsdp": self.z * 2 + 1 - self.y}

    def along(self, step):
        return {"ctx": self.c, "fsdp": self.f + 2 * step}

    def greet(self, barrier, rows=False):
        signal = lambda where: pl.semaphore_signal(barrier, inc=1, device_id=where, device_id_type=MESH)
        for k in range(1, self.n):
            signal({"ctx": (self.c + k) % self.n, "fsdp": self.f})
        count = self.n - 1
        if rows:
            for k in range(1, self.m):
                signal({"ctx": self.c, "fsdp": (self.f + k) % self.m})
            count = count + self.m - 1
        else:
            signal(self.across())
            up = self.z < self.line - 1
            down = self.z > 0

            @pl.when(up)
            def _():
                signal(self.along(1))

            @pl.when(down)
            def _():
                signal(self.along(-1))

            count = count + 1 + up.astype(jnp.int32) + down.astype(jnp.int32)
        pl.semaphore_wait(barrier, count)


def remote(src, dst, send, recv, where):
    return pltpu.make_async_remote_copy(
        src_ref=src, dst_ref=dst, send_sem=send, recv_sem=recv, device_id=where, device_id_type=MESH
    )


class Gather:
    def __init__(self, place, shard, full, sems, channel, cols=slice(None), split=False):
        self.p, self.shard, self.full, self.cols = place, shard, full, cols
        self.send, self.recv, self.local = sems
        self.ch = channel
        self.split = split and place.n % 4 == 0
        self.part = (place.c // 2) % 2

    def rows(self, other=False):
        if not self.split:
            return slice(None)
        size = self.shard.shape[1] // 2
        part = 1 - self.part if other else self.part
        return pl.ds(pl.multiple_of(part * size, size), size)

    def copy(self, place, source, kind, index, where):
        sems = self.send.at[self.ch, kind, index], self.recv.at[self.ch, kind, index]
        return remote(place if source is None else source, place, *sems, where)

    def piece(self, j, y, core, other=False):
        return self.full.at[j * 2 + y, core, self.rows(other), self.cols]

    def source(self):
        return self.shard.at[self.p.core, self.rows(), self.cols]

    def behind(self, k):
        return (self.p.z + self.p.line - k) % self.p.line

    def line_out(self, k):
        p = self.p
        j = (p.z + k) % p.line
        return self.copy(self.piece(p.z, p.y, p.core), self.source(), 0, k, {"ctx": p.c, "fsdp": j * 2 + p.y})

    def across(self, k):
        p = self.p
        source = self.source() if k == 0 else None
        return self.copy(self.piece(self.behind(k), p.y, p.core), source, 1, k, p.across())

    def mate(self, k, same, core, other=False):
        p = self.p
        y = p.y if same else 1 - p.y
        kind = (2 if same else 3) + (4 if other else 0)
        return self.copy(self.piece(self.behind(k), y, core, other), None, kind, k, p.mate())

    def chip(self, k, same, other=False):
        p = self.p
        y = p.y if same else 1 - p.y
        where = {"ctx": p.c + 2 - 4 * self.part, "fsdp": p.f}
        return self.copy(self.piece(self.behind(k), y, p.core, other), None, 4 if same else 5, k, where)

    def own(self):
        return pltpu.make_async_copy(
            self.shard.at[:, :, self.cols], self.full.at[self.p.f, :, :, self.cols], self.local.at[self.ch]
        )

    def start(self):
        self.own().start()
        for k in range(1, self.p.line):
            self.line_out(k).start()

    def start_across(self):
        self.across(0).start()

    def line_in(self, *ks):
        p = self.p
        for k in ks or range(1, p.line):
            self.line_out(k).wait_recv()
            self.across(k).start()
            if self.split:
                self.chip(k, True).start()
            self.mate(k, True, p.core).start()

    def across_in(self, *ks):
        p = self.p
        for k in ks or range(p.line):
            self.across(k).wait_recv()
            if self.split:
                self.chip(k, False).start()
            self.mate(k, False, p.core).start()

    def chip_in(self, *ks):
        p = self.p
        for k in ks or range(p.line):
            for same in (True, False)[k == 0 :]:
                self.chip(k, same, True).wait_recv()
                self.mate(k, same, p.core, True).start()

    def finish(self):
        p = self.p
        self.own().wait()
        for k in range(p.line):
            if k:
                self.line_out(k).wait_send()
            self.across(k).wait_send()
            for same in (True, False)[k == 0 :]:
                for other in (False, True)[: 1 + self.split]:
                    self.mate(k, same, 1 - p.core, other).wait_recv()
                    self.mate(k, same, p.core, other).wait_send()
                if self.split:
                    self.chip(k, same).wait_send()


def gather_sems(place_line, channels):
    return [
        pltpu.SemaphoreType.DMA((channels, 8, place_line)),
        pltpu.SemaphoreType.DMA((channels, 8, place_line)),
        pltpu.SemaphoreType.DMA((channels,)),
    ]


class Reduce:
    def __init__(self, place, term, mine, out, bufs, sems, channel, line_first):
        self.p, self.term, self.mine, self.out = place, term, mine, out
        self.one, self.two, self.ins, self.parts = bufs
        self.send, self.recv = sems
        self.ch, self.line_first = channel, line_first

    def copy(self, src, dst, slot, where, back=None):
        back = slot if back is None else back
        return remote(src, dst, self.send.at[self.ch, slot], self.recv.at[self.ch, back], where)

    def mate_copy(self):
        p = self.p
        return self.copy(self.term.at[:, :, 1 - p.core], self.one, 0, p.mate())

    def mine_copy(self):
        return pltpu.make_async_copy(self.term.at[:, :, self.p.core], self.mine, self.send.at[self.ch, 2])

    def across_copy(self):
        p = self.p
        source = self.one.at[p.z, 1 - p.y] if self.line_first else self.one.at[:, 1 - p.y]
        return self.copy(source, self.two, 1, p.across())

    def line_out(self, k):
        p = self.p
        j = (p.z + k) % p.line
        source = self.one if self.line_first else self.two
        return self.copy(source.at[j], self.ins.at[k], 4 + k, {"ctx": p.c, "fsdp": j * 2 + p.y})

    def ctx_copy(self, k):
        p = self.p
        where = {"ctx": (p.c + 2 * k) % p.n, "fsdp": p.f}
        mine = self.parts.at[p.c // 2]
        return self.copy(mine, mine, 4 + p.line + k, where)

    def last_copy(self, core):
        return self.copy(self.out.at[core], self.out.at[core], 3, self.p.mate())

    def step0(self):
        self.mate_copy().start()
        if self.mine is not None:
            self.mine_copy().start()

    def from_mate(self):
        p = self.p
        if self.mine is not None:
            self.mine_copy().wait()
        self.mate_copy().wait_recv()

        def add(i, carry):
            for y in range(2):
                own = self.term[i, y, p.core] if self.mine is None else self.mine[i, y]
                self.one[i, y] = (self.one[i, y].astype(F32) + own.astype(F32)).astype(BF16)
            return carry

        lax.fori_loop(0, p.line, add, 0)

    def line_start(self):
        for k in range(1, self.p.line):
            self.line_out(k).start()

    def line_sum(self):
        p = self.p
        total = (self.one if self.line_first else self.two)[p.z].astype(F32)
        for k in range(1, p.line):
            self.line_out(k).wait_recv()
            total = total + self.ins[k].astype(F32)
        return total.astype(BF16)

    def ctx_start(self, value):
        p = self.p
        self.parts[p.c // 2] = value
        for k in range(1, p.n // 2):
            self.ctx_copy(k).start()

    def step1(self):
        self.from_mate()
        if self.line_first:
            self.line_start()
        else:
            self.across_copy().start()

    def step2(self):
        p = self.p
        if self.line_first:
            self.one[p.z] = self.line_sum()
            self.across_copy().start()
            return
        self.across_copy().wait_recv()

        def add(i, carry):
            self.two[i] = (self.two[i].astype(F32) + self.one[i, p.y].astype(F32)).astype(BF16)
            return carry

        lax.fori_loop(0, p.line, add, 0)
        self.line_start()

    def step3(self):
        p = self.p
        if self.line_first:
            self.across_copy().wait_recv()
            self.ctx_start((self.two[...].astype(F32) + self.one[p.z, p.y].astype(F32)).astype(BF16))
        else:
            self.ctx_start(self.line_sum())

    def step4(self):
        p = self.p
        for k in range(1, p.n // 2):
            self.ctx_copy(k).wait_recv()
        total = self.parts[0].astype(F32)
        for c in range(1, p.n // 2):
            total = total + self.parts[c].astype(F32)
        self.out[p.core] = total.astype(BF16)
        self.last_copy(p.core).start()

    def finish(self):
        p = self.p
        self.last_copy(1 - p.core).wait_recv()
        self.last_copy(p.core).wait_send()
        self.mate_copy().wait_send()
        self.across_copy().wait_send()
        for k in range(1, p.line):
            self.line_out(k).wait_send()
        for k in range(1, p.n // 2):
            self.ctx_copy(k).wait_send()


def reduce_scratch(shape, h, w, line_first, stored=True):
    line, n = shape["fsdp"] // 2, shape["ctx"]
    run = (line, 2, h, w) if line_first else (line, h, w)
    return [
        pltpu.VMEM((line, 2, h, w) if stored else (8, 128), BF16),
        pltpu.VMEM((line, 2, h, w), BF16),
        pltpu.VMEM((h, w) if line_first else (line, h, w), BF16),
        pltpu.VMEM(run, BF16),
        pltpu.VMEM((n // 2, h, w), BF16),
    ]


def reduce_sems(shape, channels):
    slots = 4 + shape["fsdp"] // 2 + shape["ctx"] // 2
    return [pltpu.SemaphoreType.DMA((channels, slots))] * 2


def halves(pair):
    low = lax.broadcasted_iota(jnp.int32, pair.shape, 1) < 64
    zero = jnp.zeros_like(pair)
    return jnp.concatenate([jnp.where(low, pair, zero), jnp.where(low, zero, pair)], axis=0)


def corner(both):
    return jnp.concatenate([both[0:64, 0:SPAN], both[64:128, SPAN : 2 * SPAN]], axis=0)


def turn(value):
    return value.astype(F32).T.astype(BF16)


class Agenda:
    def __init__(self, actions, places=None):
        self.plan = {}
        if places is None:
            for place, action in actions:
                self.plan.setdefault(place, []).append(action)
            return
        for i, action in enumerate(actions):
            self.plan.setdefault(i * places // len(actions), []).append(action)

    def at(self, place, index=None, count=1):
        if index is None:
            for action in self.plan.get(place, ()):
                action()
            return
        for k in range(count):
            if place + k in self.plan:

                @pl.when(index == k)
                def _(k=k):
                    for action in self.plan[place + k]:
                        action()


def front_kernel(shape, *refs):
    shards, x_hbm = refs[0:6], refs[6]
    wq_out, wo_out, wu_out, wd_out, norms_ref, mixed_out, prob_out, att_out, attt_out, normt_out, unit_out, far_ref, rstd_ref = refs[7:20]
    (x_ref, wq_ref, raw_ref, mixed_ref, prob_ref, att_ref, attt_ref, normt_ref, low_ref, own_ref, all_ref, fart_ref, bias_ref, norm_ref, down_ref,
     gsend, grecv, glocal, ssend, srecv, nsend, nrecv, io_sem) = refs[20:]
    batches, tokens, _ = x_ref.shape
    spans = tokens // SPAN
    count = far_ref.shape[1]
    prompt = count // 2
    m = shape["fsdp"]
    width = D // m
    place = Place(shape)
    first = place.c * spans

    load = [pltpu.make_async_copy(x_hbm.at[b], x_ref.at[b], io_sem.at[0, b]) for b in range(batches)]
    for copy in load:
        copy.start()
    down_copy = pltpu.make_async_copy(shards[3], down_ref, io_sem.at[6, 1])
    down_copy.start()
    place.greet(pltpu.get_barrier_semaphore(), rows=True)
    norm_copies = []
    norm_ref[...] = jnp.zeros_like(norm_ref)
    for i in range(2):
        norm_ref[2 * i : 2 * i + 2, 0:width] = shards[4 + i][...].astype(F32)
    for k in range(1, m):
        where = {"ctx": place.c, "fsdp": (place.f + k) % m}
        norm_copies.append(remote(norm_ref, raw_ref.at[place.f], nsend.at[k], nrecv.at[k], where))
        norm_copies[-1].start()
    sems = (gsend, grecv, glocal)
    soon = [Gather(place, shards[0], wq_ref, sems, c, pl.ds(c * D, D)) for c in (1, 2, 0)]
    wo, wu, wd = (
        Gather(place, shard, full, sems, 3 + i, split=i == 2)
        for i, (shard, full) in enumerate(((shards[1], wo_out), (shards[2], wu_out), (down_ref, wd_out)))
    )
    later = (wd, wo, wu)
    for part in soon:
        part.start()
        part.start_across()
    raw_ref[place.f] = norm_ref[...]
    down_copy.wait()
    down_ref[...] = down_ref[...] * 0.5
    for copy in norm_copies:
        copy.wait()
    for f in range(m):
        norms_ref[0:4, f * width : (f + 1) * width] = raw_ref[f, 0:4, 0:width]
    gain = norms_ref[0:1, :]
    shift = norms_ref[2:3, :]
    key_id = lax.broadcasted_iota(jnp.int32, (SPAN, 2 * SPAN), 0)
    query_id = lax.broadcasted_iota(jnp.int32, (SPAN, 2 * SPAN), 1) & (SPAN - 1)
    for s in range(2):
        bias_ref[s, 0:SPAN, :] = jnp.where(key_id <= query_id, 0.0, NEG)

    norm_outs = lambda b: [
        pltpu.make_async_copy(normt_ref.at[b], normt_out.at[b], io_sem.at[1, b]),
        pltpu.make_async_copy(x_ref.at[b], unit_out.at[b], io_sem.at[7, b]),
    ]
    tile = 512
    tiles = tokens // tile
    far_ones = range(2, place.line)
    plan = Agenda([
        (3, soon[0].line_in), (7, soon[1].across_in), (9, soon[2].across_in), (11, wd.line_in), (12, wo.line_in),
        (15, lambda: wo.across_in()), (15, wd.across_in), (16, lambda: wu.line_in(1)), (17, lambda: wu.across_in(0)),
        (18, lambda: wu.line_in(*far_ones)), (19, lambda: wu.across_in(1)), (20, wd.chip_in),
        (23, lambda: wu.across_in(*far_ones)),
    ])

    for b in range(batches):
        load[b].wait()

        def norm(i, carry, b=b):
            plan.at(b * tiles, i, tiles)
            rows = pl.ds(pl.multiple_of(i * tile, tile), tile)
            unit, rstd = unit_of(x_ref[b, rows, :].astype(F32))
            low = (unit * gain + shift).astype(BF16)
            low_ref[b, rows, :] = low
            normt_ref[b, :, rows] = low.T
            x_ref[b, rows, :] = unit.astype(BF16)
            rstd_ref[b, rows, :] = rstd
            return carry

        lax.fori_loop(0, tiles, norm, 0)
        for copy in norm_outs(b):
            copy.start()

    def share(k):
        to = (place.c + k) % place.n
        return remote(own_ref, all_ref.at[place.c], ssend.at[k], srecv.at[k], {"ctx": to, "fsdp": place.f})

    def project(c, at):
        def body(i, carry):
            plan.at(at, i, tiles)
            for b in range(batches):
                rows = pl.ds(pl.multiple_of(i * tile, tile), tile)
                part = nn(low_ref[b, rows, :], wq_ref[:, :, :, c * D : (c + 1) * D].reshape(D, D))
                if c == 0:
                    mixed_ref[b, rows, 0:D] = part.astype(BF16) * 0.125
                    continue
                mixed_ref[b, rows, c * D : (c + 1) * D] = part.astype(BF16)
                for s in range(tile // SPAN):
                    total = jnp.sum(part[s * SPAN : (s + 1) * SPAN, :], axis=0, keepdims=True) * SPAN ** (-0.5)
                    own_ref[b, pl.ds(i * (tile // SPAN) + s, 1), (c - 1) * D : c * D] = total.astype(BF16).astype(F32)
            return carry

        lax.fori_loop(0, tiles, body, 0)

    soon[1].line_in()
    soon[0].across_in()
    soon[2].line_in()
    for part in later:
        part.start()
        part.start_across()
    soon[0].finish()
    project(1, 6)
    soon[1].finish()
    project(2, 8)
    for k in range(1, place.n):
        share(k).start()
    all_ref[place.c] = own_ref[...]
    soon[2].finish()
    project(0, 10)
    pairs = spans // 2
    weight_out = pltpu.make_async_copy(wq_ref, wq_out, io_sem.at[6, 0])
    weight_out.start()
    for k in range(1, place.n):
        share(k).wait()

    out_copies = lambda b: [
        pltpu.make_async_copy(src.at[b], dst.at[b], io_sem.at[2 + i, b])
        for i, (src, dst) in enumerate(
            ((mixed_ref, mixed_out), (prob_ref, prob_out), (att_ref, att_out), (attt_ref, attt_out))
        )
    ]

    for b in range(batches):
        out_copies(b)[0].start()
        for c in range(place.n):
            far_ref[b, c * spans : (c + 1) * spans, :] = all_ref[c, b].astype(BF16)
        fart_ref[...] = far_ref[b, :, D:].T

        def attend(i, carry, b=b):
            plan.at(12 + b * pairs, i, pairs)
            for s in range(2):
                far_id = lax.broadcasted_iota(jnp.int32, (count, 2 * SPAN), 0)
                mine = first + i * 2 + s
                segment = (mine - prompt) >> 3
                seen = (far_id < mine) & ((far_id < prompt) | (((far_id - prompt) >> 3) == segment))
                bias_ref[s, SPAN:, :] = jnp.where(seen, 0.0, NEG)
            scores, probs = {}, {}
            items = [(s, p) for p in range(PAIRS) for s in range(2)]
            for t in range(len(items) + 2):
                if t < len(items):
                    s, p = items[t]
                    rows = pl.ds(pl.multiple_of(i * 2 * SPAN + s * SPAN, SPAN), SPAN)
                    lanes = slice(p * SPAN, (p + 1) * SPAN)
                    qs = halves(mixed_ref[b, rows, lanes])
                    keys = jnp.concatenate(
                        [mixed_ref[b, rows, D + p * SPAN : D + (p + 1) * SPAN], far_ref[b, :, lanes]], axis=0
                    )
                    scores[t] = nt(keys, qs)
                if 1 <= t <= len(items):
                    s, p = items[t - 1]
                    score = scores.pop(t - 1) + bias_ref[s]
                    score = jnp.exp(score - jnp.max(score, axis=0, keepdims=True))
                    prob = (score * (1.0 / jnp.sum(score, axis=0, keepdims=True))).astype(BF16)
                    prob_ref[b, i * 2 + s, p] = prob
                    probs[t - 1] = prob
                if t >= 2:
                    s, p = items[t - 2]
                    rows = pl.ds(pl.multiple_of(i * 2 * SPAN + s * SPAN, SPAN), SPAN)
                    lanes = slice(p * SPAN, (p + 1) * SPAN)
                    turned = mixed_ref[b, rows, 2 * D + p * SPAN : 2 * D + (p + 1) * SPAN].T
                    turned = jnp.concatenate([turned, fart_ref[lanes, :]], axis=1)
                    att = corner(nn(turned, probs.pop(t - 2))).astype(BF16)
                    attt_ref[b, lanes, rows] = att
                    att_ref[b, rows, lanes] = att.T
            return carry

        lax.fori_loop(0, pairs, attend, 0)
        for copy in out_copies(b)[1:]:
            copy.start()

    for part in later:
        part.finish()
    weight_out.wait()
    for b in range(batches):
        for copy in norm_outs(b) + out_copies(b):
            copy.wait()


def front_call(shape, shards, x):
    batches, tokens, _ = x.shape
    spans = tokens // SPAN
    n, m = shape["ctx"], shape["fsdp"]
    count = n * spans
    any_spec = pl.BlockSpec(memory_space=pl.ANY)
    vmem = pl.BlockSpec(memory_space=pltpu.VMEM)
    full = [jax.ShapeDtypeStruct((m,) + s.shape, s.dtype) for s in shards[0:4]]
    big = [
        jax.ShapeDtypeStruct((batches, tokens, 3 * D), BF16),
        jax.ShapeDtypeStruct((batches, spans, PAIRS, SPAN + count, 2 * SPAN), BF16),
        jax.ShapeDtypeStruct((batches, tokens, D), BF16),
        jax.ShapeDtypeStruct((batches, D, tokens), BF16),
        jax.ShapeDtypeStruct((batches, D, tokens), BF16),
    ]
    return pl.pallas_call(
        functools.partial(front_kernel, shape),
        in_specs=[any_spec] * 4 + [vmem] * 2 + [any_spec],
        out_specs=[any_spec] * 4 + [vmem] + [any_spec] * 6 + [vmem] * 2,
        out_shape=full + [jax.ShapeDtypeStruct((8, D), F32)]
        + big
        + [
            jax.ShapeDtypeStruct(x.shape, BF16),
            jax.ShapeDtypeStruct((batches, count, 2 * D), BF16),
            jax.ShapeDtypeStruct((batches, tokens, 1), F32),
        ],
        scratch_shapes=[
            pltpu.VMEM((batches, tokens, D), BF16),
            pltpu.VMEM(full[0].shape, BF16),
            pltpu.VMEM((m, 8, 128), F32),
        ]
        + [pltpu.VMEM(v.shape, v.dtype) for v in big]
        + [
            pltpu.VMEM((batches, tokens, D), BF16),
            pltpu.VMEM((batches, spans, 2 * D), F32),
            pltpu.VMEM((n, batches, spans, 2 * D), F32),
            pltpu.VMEM((D, count), BF16),
            pltpu.VMEM((2, SPAN + count, 2 * SPAN), F32),
            pltpu.VMEM((8, 128), F32),
            pltpu.VMEM(shards[3].shape, BF16),
        ]
        + gather_sems(m // 2, 6)
        + [
            pltpu.SemaphoreType.DMA((n,)),
            pltpu.SemaphoreType.DMA((n,)),
            pltpu.SemaphoreType.DMA((m,)),
            pltpu.SemaphoreType.DMA((m,)),
            pltpu.SemaphoreType.DMA((8, batches)),
        ],
        compiler_params=pltpu.CompilerParams(collective_id=0, has_side_effects=True, vmem_limit_bytes=VMEM_LIMIT),
        name="front",
    )(*shards, x)


def middle_kernel(shape, *refs):
    x_hbm, g_hbm, att_hbm, attt_hbm, wo_hbm, wu_hbm, wd_hbm, norms_ref = refs[0:8]
    out_hbm, gmid_hbm, da_hbm, go_ref, gu_ref, gd_ref, gu_sum, gd_sum, ggain_ref, gshift_ref = refs[8:18]
    (x_ref, att_ref, attt_ref, g_ref, n2_ref, n2t_ref, gt_ref, unit_ref, rstd_ref, acc_ref, gn2_ref, act_ref, gh_ref,
     wo_ref, wu_ref, wd_ref, goa_ref, gua_ref, gda_ref, gu_term, gd_term) = refs[18:39]
    bufs, sems, io_sem, w_sem = refs[39:47], refs[47:49], refs[49], refs[50]
    batches, tokens, _ = g_ref.shape
    m = shape["fsdp"]
    place = Place(shape)
    per = FF // m // UNIT
    group = UNIT * m
    tile = 512
    tiles = tokens // tile

    ins = lambda b: [
        pltpu.make_async_copy(src.at[b], dst, io_sem.at[i, b])
        for i, (src, dst) in enumerate(
            ((x_hbm, x_ref.at[b % 2]), (att_hbm, att_ref.at[b % 2]), (g_hbm, g_ref.at[b]))
        )
    ]
    turned = lambda b: pltpu.make_async_copy(attt_hbm.at[b], attt_ref.at[b % 2], io_sem.at[3, b])
    wo_copy = pltpu.make_async_copy(wo_hbm, wo_ref, io_sem.at[4, 0])
    weights = []
    for h in range(per):
        for f in range(m):
            src, dst = (f * per + h) * UNIT, h * group + f * UNIT
            weights.append(
                pltpu.make_async_copy(wu_hbm.at[:, pl.ds(src, UNIT)], wu_ref.at[:, pl.ds(dst, UNIT)], w_sem.at[0, h, f])
            )
            weights.append(
                pltpu.make_async_copy(wd_hbm.at[pl.ds(src, UNIT)], wd_ref.at[pl.ds(dst, UNIT)], w_sem.at[1, h, f])
            )
    wo_copy.start()
    for copy in ins(0):
        copy.start()
    for copy in weights:
        copy.start()
    early = per > 1
    if early:
        place.greet(pltpu.get_barrier_semaphore(), rows=True)
        gu = Reduce(place, gu_term, None, gu_sum, bufs[0:4], sems, 0, False)
        gd = Reduce(place, gd_term, None, gd_sum, bufs[4:8], sems, 1, False)
        chain = [(0, gu.step0), (0, gd.step0), (1, gu.step1), (1, gd.step1), (3, gu.step2), (4, gd.step2)]
        chain += [(6, gu.step3), (7, gd.step3), (9, gu.step4), (10, gd.step4)]
    gain = norms_ref[1:2, :]
    shift = norms_ref[3:4, :]

    wo_copy.wait()
    for b in range(batches):
        if b + 1 < batches:
            for copy in ins(b + 1):
                copy.start()
        for copy in ins(b):
            copy.wait()

        def before(i, carry, b=b):
            rows = pl.ds(pl.multiple_of(i * tile, tile), tile)
            middle = x_ref[b % 2, rows, :].astype(F32) + nn(att_ref[b % 2, rows, :], wo_ref[...])
            unit, rstd = unit_of(middle)
            low = (unit * gain + shift).astype(BF16)
            acc_ref[b, rows, :] = middle
            gn2_ref[b, rows, :] = jnp.zeros((tile, D), F32)
            unit_ref[b, rows, :] = unit.astype(BF16)
            rstd_ref[b, rows, :] = rstd
            n2_ref[b, rows, :] = low
            n2t_ref[b, :, rows] = low.T
            gt_ref[b, :, rows] = g_ref[b, rows, :].T
            return carry

        lax.fori_loop(0, tiles, before, 0)
    for copy in weights:
        copy.wait()
    act_ref[1] = jnp.zeros((tokens, CHUNK), BF16)
    gh_ref[1] = jnp.zeros((tokens, CHUNK), BF16)

    def wgrad(i):
        b = lax.rem(i, batches)
        slot = lax.rem(i, 2)
        keep = b > 0
        total = nn(n2t_ref[b], gh_ref[slot])
        gua_ref[...] = jnp.where(keep, gua_ref[...], 0.0) + total
        total = nn(gt_ref[b], act_ref[slot])
        gda_ref[...] = jnp.where(keep, gda_ref[...], 0.0) + total

    half = D // m // 2

    def close(c):
        h, base = c * CHUNK // group, c * CHUNK % group
        ups, downs = (gu_term, gd_term) if early and h == 0 else (gu_ref, gd_ref)

        def body(i, carry):
            for y in range(2):
                for s in range(2):
                    start = pl.multiple_of(((i * 2 + y) * 2 + s) * half, half)
                    ups[i, y, s, :, base : base + CHUNK] = gua_ref[pl.ds(start, half), :].astype(BF16)
            return carry

        lax.fori_loop(0, m // 2, body, 0)
        for k in range(CHUNK // UNIT):
            f = base // UNIT + k
            rows = (gda_ref[:, k * UNIT : (k + 1) * UNIT] * 0.5).astype(BF16).T
            downs[f // 2, f % 2, 0] = rows[0 : UNIT // 2]
            downs[f // 2, f % 2, 1] = rows[UNIT // 2 :]

    chunks = FF // CHUNK
    steps = chunks * batches
    opening = (chunks // per) * batches + 1 if early else steps
    agenda = Agenda(chain) if early else None

    def step(i, carry):
        for c in range(chunks - 1):

            @pl.when(i == (c + 1) * batches + 1)
            def _(c=c):
                close(c)

        if early:
            agenda.at(0, i - opening, steps - opening)
        c = lax.div(i, batches)
        b = lax.rem(i, batches)
        slot = lax.rem(i, 2)
        cols = pl.ds(pl.multiple_of(c * CHUNK, CHUNK), CHUNK)
        for r in range(1):
            rows = slice(0, tokens)
            act, slope = gelu_pair(nn(n2_ref[b, rows, :], wu_ref[:, cols]))
            act = act.astype(BF16)
            act_ref[slot, rows, :] = act
            grad = (nt(g_ref[b, rows, :], wd_ref[cols, :]) * slope).astype(BF16)
            gh_ref[slot, rows, :] = grad
            acc_ref[b, rows, :] += nn(act, wd_ref[cols, :])
            gn2_ref[b, rows, :] += nt(grad, wu_ref[:, cols])
            if r == 0:
                wgrad(i + steps * 2 - 1)
        return carry

    lax.fori_loop(0, steps, step, 0)
    wgrad(steps - 1)
    turned(0).start()
    close(chunks - 1)

    outs = lambda b: [
        pltpu.make_async_copy(src, dst.at[b], io_sem.at[5 + i, b])
        for i, (src, dst) in enumerate(((unit_ref.at[b], out_hbm), (g_ref.at[b], gmid_hbm), (n2_ref.at[b], da_hbm)))
    ]
    ggain_ref[...] = jnp.zeros_like(ggain_ref)
    gshift_ref[...] = jnp.zeros_like(gshift_ref)
    for b in range(batches):
        if b + 1 < batches:
            turned(b + 1).start()

        def after(i, carry, b=b):
            if early:
                agenda.at(steps - opening + b * tiles, i, tiles)
            rows = pl.ds(pl.multiple_of(i * tile, tile), tile)
            unit = unit_ref[b, rows, :].astype(F32)
            grad = gn2_ref[b, rows, :]
            ggain_ref[...] += fold8(grad * unit)
            gshift_ref[...] += fold8(grad)
            grad = g_ref[b, rows, :].astype(F32) + norm_back(grad, unit, rstd_ref[b, rows, :], gain)
            low = grad.astype(BF16)
            unit_ref[b, rows, :] = acc_ref[b, rows, :].astype(BF16)
            g_ref[b, rows, :] = low
            n2_ref[b, rows, :] = nt(low, wo_ref[...]).astype(BF16)
            return carry

        lax.fori_loop(0, tiles, after, 0)
        for copy in outs(b):
            copy.start()
        turned(b).wait()
        total = nn(attt_ref[b % 2], g_ref[b])
        goa_ref[...] = total if b == 0 else goa_ref[...] + total
    go_ref[...] = goa_ref[...].astype(BF16)
    if early:
        gu.finish()
        gd.finish()
    for b in range(batches):
        for copy in outs(b):
            copy.wait()


def middle_call(shape, x, g, att, attt, wo, wu, wd, norms):
    batches, tokens, _ = x.shape
    m = shape["fsdp"]
    line = m // 2
    group = UNIT * m
    any_spec = pl.BlockSpec(memory_space=pl.ANY)
    vmem = pl.BlockSpec(memory_space=pltpu.VMEM)
    up = (line, 2, 2, D // m // 2, group)
    down = (line, 2, 2, UNIT // 2, D)
    low = lambda *dims: jax.ShapeDtypeStruct(dims, BF16)
    seqs = lambda: pltpu.VMEM((batches, tokens, D), BF16)
    turned = lambda count: pltpu.VMEM((count, D, tokens), BF16)
    scratch = [
        pltpu.VMEM((2, tokens, D), BF16), pltpu.VMEM((2, tokens, D), BF16), turned(2), seqs(), seqs(), turned(batches),
        turned(batches), seqs(), pltpu.VMEM((batches, tokens, 1), F32), pltpu.VMEM((batches, tokens, D), F32),
        pltpu.VMEM((batches, tokens, D), F32), pltpu.VMEM((2, tokens, CHUNK), BF16), pltpu.VMEM((2, tokens, CHUNK), BF16),
        pltpu.VMEM((D, D), BF16), pltpu.VMEM((D, FF), BF16), pltpu.VMEM((FF, D), BF16),
        pltpu.VMEM((D, D), F32), pltpu.VMEM((D, CHUNK), F32), pltpu.VMEM((D, CHUNK), F32),
    ]
    early = FF // m // UNIT > 1
    small = (8, 128)
    scratch += [pltpu.VMEM(up if early else small, BF16), pltpu.VMEM(down if early else small, BF16)]
    for t in (up, down):
        if early:
            scratch += reduce_scratch(shape, *t[3:], False, False)[1:]
        else:
            scratch += [pltpu.VMEM(small, BF16)] * 4
    scratch += reduce_sems(shape, 2)
    scratch += [pltpu.SemaphoreType.DMA((8, batches)), pltpu.SemaphoreType.DMA((2, FF // m // UNIT, m))]
    return pl.pallas_call(
        functools.partial(middle_kernel, shape),
        in_specs=[any_spec] * 7 + [vmem],
        out_specs=[any_spec] * 3 + [vmem] * 7,
        out_shape=[
            low(*x.shape), low(*x.shape), low(*x.shape), low(D, D), low(*up), low(*down),
            low(*(up[2:] if early else small)), low(*(down[2:] if early else small)),
            jax.ShapeDtypeStruct((8, D), F32), jax.ShapeDtypeStruct((8, D), F32),
        ],
        scratch_shapes=scratch,
        compiler_params=pltpu.CompilerParams(
            collective_id=2 if early else None, has_side_effects=True, vmem_limit_bytes=VMEM_LIMIT
        ),
        name="middle",
    )(x, g, att, attt, wo, wu, wd, norms)


def back_kernel(shape, *refs):
    mixed_hbm, da_hbm, prob_hbm, unit_hbm, normt_hbm, gmid_hbm, wq_hbm, gu_hbm, gd_hbm, go_hbm = refs[0:10]
    far_ref, rstd_ref, norms_ref, gain2_ref, shift2_ref = refs[10:15]
    gin_out, gq_out, gk_out, gv_out, gu_out, gd_out, go_out, small_out = refs[15:23]
    (mixed_ref, da_ref, prob_ref, unit_ref, normt_ref, gmid_ref, wq_ref, dmixed_ref, gw_ref, gq_ref, gk_ref, gv_ref,
     far_t, dfar_ref, held_ref, gsum_ref, vec_ref, vecs_ref, vsum_ref, pieces_ref) = refs[23:43]
    bufs, sems = refs[43:73], refs[73:75]
    xsend, xrecv, vsend, vrecv, io_sem = refs[75:80]
    batches, tokens, _ = unit_ref.shape
    spans = tokens // SPAN
    count = far_ref.shape[1]
    m = shape["fsdp"]
    width = D // m
    place = Place(shape)

    ins = lambda b: [
        pltpu.make_async_copy(src.at[b], dst.at[b % 2], io_sem.at[i, b])
        for i, (src, dst) in enumerate(((mixed_hbm, mixed_ref), (da_hbm, da_ref), (prob_hbm, prob_ref)))
    ]
    rest = [
        pltpu.make_async_copy(src, dst, io_sem.at[4 + i, 0])
        for i, (src, dst) in enumerate(
            ((normt_hbm, normt_ref), (unit_hbm, unit_ref), (gmid_hbm, gmid_ref), (wq_hbm, wq_ref))
        )
    ]
    for copy in ins(0):
        copy.start()
    place.greet(pltpu.get_barrier_semaphore(), rows=True)
    channel = lambda i, term, out, line_first, stored: Reduce(
        place, term, bufs[5 * i] if stored else None, out, bufs[5 * i + 1 : 5 * i + 5], sems, i, line_first
    )
    gu = channel(0, gu_hbm, gu_out, False, True)
    gd = channel(1, gd_hbm, gd_out, False, True)
    go = channel(2, go_hbm, go_out, False, True)
    gq = channel(3, gq_ref, gq_out, False, False)
    gk = channel(4, gk_ref, gk_out, True, False)
    gv = channel(5, gv_ref, gv_out, False, False)
    for part in (gu, gd, go):
        part.step0()
    for copy in rest:
        copy.start()

    def swap(b, k):
        to = (place.c + k) % place.n
        source = dfar_ref.at[b, pl.ds(pl.multiple_of(to * spans, spans), spans)]
        return remote(source, held_ref.at[b, k], xsend.at[b, k], xrecv.at[b, k], {"ctx": to, "fsdp": place.f})

    pairs = spans // 2
    big = Agenda([(at, getattr(part, "step" + step)) for part, places in (
        (gu, GU), (gd, GD), (go, GO), (gq, GQ), (gk, GK), (gv, GV)
    ) for at, step in zip(places, "1234")])

    def attend_back(b):
        slot = b % 2
        for copy in ins(b):
            copy.wait()
        if b + 1 < batches:
            for copy in ins(b + 1):
                copy.start()
        dfar_ref[b] = jnp.zeros((count, 2 * D), F32)
        far_t[...] = far_ref[b, :, 0:D].T
        base = b * (pairs + EXTRA)

        def body(i, carry):
            big.at(base, i, pairs)
            items = [(s, p) for p in range(PAIRS) for s in range(2)]
            held, grads = {}, {}
            where = lambda t: (
                pl.ds(pl.multiple_of(i * 2 * SPAN + items[t][0] * SPAN, SPAN), SPAN),
                *(slice(c * D + items[t][1] * SPAN, c * D + (items[t][1] + 1) * SPAN) for c in range(3)),
            )
            for t in range(len(items) + 2):
                if t < len(items):
                    rows, lanes, klanes, vlanes = where(t)
                    das = halves(da_ref[slot, rows, lanes])
                    values = jnp.concatenate([mixed_ref[slot, rows, vlanes], far_ref[b, :, klanes]], axis=0)
                    held[t] = (das, nt(values, das))
                if 1 <= t <= len(items):
                    rows, lanes, klanes, vlanes = where(t - 1)
                    das, slope = held.pop(t - 1)
                    low = prob_ref[slot, i * 2 + items[t - 1][0], items[t - 1][1]]
                    prob = low.astype(F32)
                    inner = jnp.sum(prob * slope, axis=0, keepdims=True)
                    grads[t - 1] = (prob * (slope - inner)).astype(BF16)
                    dv = nn(low, das)
                    dmixed_ref[b, rows, vlanes] = dv[0:SPAN].astype(BF16)
                    dfar_ref[b, :, klanes] += dv[SPAN:]
                if t >= 2:
                    rows, lanes, klanes, vlanes = where(t - 2)
                    grad = grads.pop(t - 2)
                    dk = nn(grad, halves(mixed_ref[slot, rows, lanes]))
                    dmixed_ref[b, rows, klanes] = dk[0:SPAN].astype(BF16)
                    dfar_ref[b, :, lanes] += dk[SPAN:]
                    turned = jnp.concatenate([mixed_ref[slot, rows, klanes].T, far_t[lanes, :]], axis=1)
                    dmixed_ref[b, rows, lanes] = (corner(nn(turned, grad)) * 0.125).astype(BF16).T
            return carry

        lax.fori_loop(0, pairs, body, 0)
        for k in range(1, place.n):
            swap(b, k).start()

    def wgrad(b, c):
        cols = slice(c * D, (c + 1) * D)
        part = nn(normt_ref[b], dmixed_ref[b, :, cols])
        gw_ref[:, cols] = part if b == 0 else gw_ref[:, cols] + part

    def spread(b):
        for k in range(1, place.n):
            swap(b, k).wait()
        total = dfar_ref[b, pl.ds(pl.multiple_of(place.c * spans, spans), spans), :]
        for k in range(1, place.n):
            total = total + held_ref[b, k]
        gsum_ref[...] = total * SPAN ** (-0.5)

        def body(s, carry):
            rows = pl.ds(pl.multiple_of(s * SPAN, SPAN), SPAN)
            extra = jnp.broadcast_to(gsum_ref[pl.ds(s, 1), :], (16, 2 * D)).astype(BF16)
            for r in range(SPAN // 16):
                at = pl.ds(pl.multiple_of(s * SPAN + r * 16, 16), 16)
                dmixed_ref[b, at, D:] = dmixed_ref[b, at, D:] + extra
            return carry

        lax.fori_loop(0, spans, body, 0)

    half = D // m // 2

    def low(dst, cols):
        def body(i, carry):
            for y in range(2):
                for s in range(2):
                    start = pl.multiple_of(((i * 2 + y) * 2 + s) * half, half)
                    dst[i, y, s] = gw_ref[pl.ds(start, half), cols].astype(BF16)
            return carry

        lax.fori_loop(0, m // 2, body, 0)

    for b in range(batches):
        attend_back(b)
        if b == 0:
            for copy in rest:
                copy.wait()
        base = b * (pairs + EXTRA) + pairs
        big.at(base)
        wgrad(b, 0)
        if b + 1 == batches:
            low(gq_ref, slice(0, D))
            gq.step0()
        big.at(base + 1)
        if b > 0:
            spread(b - 1)
            for c in (1, 2):
                wgrad(b - 1, c)
        big.at(base + 2)
    last = batches - 1
    spread(last)
    for c, part, term in ((1, gk, gk_ref), (2, gv, gv_ref)):
        wgrad(last, c)
        low(term, slice(c * D, (c + 1) * D))
        part.step0()

    gain = norms_ref[0:1, :]
    tile = 512
    tiles = tokens // tile
    late = batches * (pairs + EXTRA)
    gin_copy = lambda b: pltpu.make_async_copy(gmid_ref.at[b], gin_out.at[b], io_sem.at[3, b])
    gains_at = jnp.zeros((8, D), F32)
    shifts_at = jnp.zeros((8, D), F32)
    for b in range(batches):

        def data(i, carry, b=b):
            big.at(late + b * tiles, i, tiles)
            spots = [pl.ds(pl.multiple_of(i * tile + r * (tile // 2), tile // 2), tile // 2) for r in range(2)]
            grads = [nt(dmixed_ref[b, rows, :], wq_ref[...].reshape(D, 3 * D)) for rows in spots]
            gains_at, shifts_at = carry
            for rows, grad in zip(spots, grads):
                unit = unit_ref[b, rows, :].astype(F32)
                change = norm_back(grad, unit, rstd_ref[b, rows, :], gain)
                gmid_ref[b, rows, :] = (gmid_ref[b, rows, :].astype(F32) + change).astype(BF16)
                gains_at = gains_at + fold8(grad * unit)
                shifts_at = shifts_at + fold8(grad)
            return gains_at, shifts_at

        gains_at, shifts_at = lax.fori_loop(0, tiles, data, (gains_at, shifts_at))
        gin_copy(b).start()

    sums = [jnp.sum(v, axis=0, keepdims=True) for v in (gains_at, gain2_ref[...], shifts_at, shift2_ref[...])]
    vec_ref[...] = jnp.concatenate(sums + [jnp.zeros((4, D), F32)], axis=0)
    over_ctx = [
        remote(vec_ref, vecs_ref.at[k], vsend.at[0, k], vrecv.at[0, k], {"ctx": (place.c + k) % place.n, "fsdp": place.f})
        for k in range(1, place.n)
    ]
    for copy in over_ctx:
        copy.start()
    vecs_ref[0] = vec_ref[...]
    big.at(late + batches * tiles)
    for copy in over_ctx:
        copy.wait()
    total = jnp.zeros((8, D), F32)
    for c in range(place.n):
        total = total + vecs_ref[(place.c - c + place.n) % place.n]
    vsum_ref[...] = jnp.zeros_like(vsum_ref)
    for f in range(m):
        vsum_ref[f, :, 0:width] = total[:, f * width : (f + 1) * width]
    over_rows = []
    for k in range(1, m):
        to = (place.f + k) % m
        over_rows.append(
            remote(vsum_ref.at[to], pieces_ref.at[place.f], vsend.at[1, k], vrecv.at[1, k], {"ctx": place.c, "fsdp": to})
        )
        over_rows[-1].start()
    pieces_ref[place.f] = vsum_ref[place.f]
    big.at(late + batches * tiles + 1)
    for copy in over_rows:
        copy.wait()
    total = pieces_ref[0]
    for f in range(1, m):
        total = total + pieces_ref[f]
    small_out[...] = total
    for part in (gu, gd, go, gq, gk, gv):
        part.finish()
    for b in range(batches):
        gin_copy(b).wait()


def back_call(shape, mixed, da, prob, unit, normt, gmid, wq, gu, gd, go, far, rstd, norms, gain2, shift2):
    batches, tokens, _ = unit.shape
    spans = tokens // SPAN
    n, m = shape["ctx"], shape["fsdp"]
    line = m // 2
    count = n * spans
    any_spec = pl.BlockSpec(memory_space=pl.ANY)
    vmem = pl.BlockSpec(memory_space=pltpu.VMEM)
    halved = lambda rows, w: (line, 2, 2, rows // (2 * m), w)
    terms = [gu.shape, gd.shape, halved(D, D), halved(D, D), halved(D, D), halved(D, D)]
    go = go.reshape(terms[2])
    out = lambda t: jax.ShapeDtypeStruct(t[2:], BF16)
    two = lambda *dims: pltpu.VMEM((2,) + dims, BF16)
    scratch = [
        two(tokens, 3 * D), two(tokens, D), two(spans, PAIRS, SPAN + count, 2 * SPAN),
        pltpu.VMEM(unit.shape, BF16), pltpu.VMEM(normt.shape, BF16), pltpu.VMEM(unit.shape, BF16),
        pltpu.VMEM(wq.shape, BF16), pltpu.VMEM((batches, tokens, 3 * D), BF16), pltpu.VMEM((D, 3 * D), F32),
        pltpu.VMEM(terms[3], BF16), pltpu.VMEM(terms[4], BF16), pltpu.VMEM(terms[5], BF16),
        pltpu.VMEM((D, count), BF16), pltpu.VMEM((batches, count, 2 * D), F32),
        pltpu.VMEM((batches, n, spans, 2 * D), F32), pltpu.VMEM((spans, 2 * D), F32),
        pltpu.VMEM((8, D), F32), pltpu.VMEM((n, 8, D), F32), pltpu.VMEM((m, 8, 128), F32), pltpu.VMEM((m, 8, 128), F32),
    ]
    for t, line_first, stored in zip(terms, (False,) * 4 + (True, False), (True,) * 3 + (False,) * 3):
        scratch += reduce_scratch(shape, *t[3:], line_first, stored)
    scratch += reduce_sems(shape, 6)
    most = max(n, m)
    scratch += [
        pltpu.SemaphoreType.DMA((batches, n)), pltpu.SemaphoreType.DMA((batches, n)),
        pltpu.SemaphoreType.DMA((2, most)), pltpu.SemaphoreType.DMA((2, most)), pltpu.SemaphoreType.DMA((8, batches)),
    ]
    return pl.pallas_call(
        functools.partial(back_kernel, shape),
        in_specs=[any_spec] * 10 + [vmem] * 5,
        out_specs=[any_spec] + [vmem] * 7,
        out_shape=[
            jax.ShapeDtypeStruct(unit.shape, BF16), out(terms[3]), out(terms[4]), out(terms[5]), out(terms[0]),
            out(terms[1]), out(terms[2]), jax.ShapeDtypeStruct((8, 128), F32),
        ],
        scratch_shapes=scratch,
        compiler_params=pltpu.CompilerParams(collective_id=1, has_side_effects=True, vmem_limit_bytes=VMEM_LIMIT),
        name="back",
    )(mixed, da, prob, unit, normt, gmid, wq, gu, gd, go, far, rstd, norms, gain2, shift2)


def widen_kernel(per, *refs):
    small_ref, go_ref = refs[0], refs[4]
    gus, gds = refs[5 : 5 + per], refs[5 + per : 5 + 2 * per]
    qkv_out, out_out, up_out, down_out, gain_out, first_out, second_out = refs[5 + 2 * per :]
    for c in range(3):
        qkv_out[:, c * D : (c + 1) * D] = refs[1 + c][...].astype(F32)
    out_out[...] = go_ref[...].astype(F32)
    for h in range(per):
        for f in range(gus[h].shape[1] // UNIT):
            at = (f * per + h) * UNIT
            up_out[:, at : at + UNIT] = gus[h][:, f * UNIT : (f + 1) * UNIT].astype(F32)
        down_out[h * UNIT : (h + 1) * UNIT, :] = gds[h][...].astype(F32)
    width = gain_out.shape[1]
    gain_out[...] = small_ref[0:2, 0:width]
    first_out[...] = small_ref[2, 0:width]
    second_out[...] = small_ref[3, 0:width]


def widen_call(width, small, gq, gk, gv, go, gus, gds):
    per = len(gus)
    flat = [small] + [v.reshape(-1, v.shape[-1]) for v in (gq, gk, gv, go, *gus, *gds)]
    rows = flat[1].shape[0]
    wide = lambda *dims: jax.ShapeDtypeStruct(dims, F32)
    return pl.pallas_call(
        functools.partial(widen_kernel, per),
        out_shape=[
            wide(rows, 3 * D), wide(rows, D), wide(rows, FF), wide(per * UNIT, D), wide(2, width), wide(width), wide(width)
        ],
        name="widen",
    )(*flat)


def local(shape, x, g, qkv_weight, out_weight, up_weight, down_weight, norm_gains, norm_shifts):
    width = norm_gains.shape[1]
    halved = lambda shard: shard.reshape(2, shard.shape[0] // 2, shard.shape[1])
    shards = [halved(v) for v in (qkv_weight, out_weight, up_weight, down_weight)] + [norm_gains, norm_shifts]
    wq, wo, wu, wd, norms, mixed, prob, att, attt, normt, unit, far, rstd = front_call(shape, shards, x)
    wo, wu, wd = (w.reshape(-1, w.shape[-1]) for w in (wo, wu, wd))
    out, gmid, da, go, gu, gd, gu_sum, gd_sum, gain2, shift2 = middle_call(shape, x, g, att, attt, wo, wu, wd, norms)
    gin, gq, gk, gv, gu, gd, go, small = back_call(
        shape, mixed, da, prob, unit, normt, gmid, wq, gu, gd, go, far, rstd, norms, gain2, shift2
    )
    early = FF // shape["fsdp"] // UNIT > 1
    gus, gds = ([gu_sum, gu], [gd_sum, gd]) if early else ([gu], [gd])
    return out, gin, *widen_call(width, small, gq, gk, gv, go, gus, gds)


def solution(mesh):
    weight, norm, token = P("fsdp", None), P(None, "fsdp"), P("fsdp", "ctx", None)
    return jax.shard_map(
        functools.partial(local, dict(mesh.shape)),
        mesh=mesh,
        in_specs=(token, token, weight, weight, weight, weight, norm, norm),
        out_specs=(token, token, weight, weight, weight, weight, norm, P("fsdp"), P("fsdp")),
        check_vma=False,
    )
```
